32 devices in a mesh: expert: 4 (over y, core), shard: 8 (over z, x).
Axes of the slice: x: 2, y: 2, z: 4, core: 2. Of those that a mesh axis runs over, the one named last changes fastest.
Arguments:
- tokens: bfloat16 [8192, 1536], P(('expert', 'shard')), may hold values from -6 to 6
- lengths: int32 [32], P(('expert', 'shard')), may hold values from 64 to 256, as said below
- routes: int32 [8192, 8], P(('expert', 'shard')), may hold values from 0 to 19, all different within a row; in each aligned block of 256 rows (0 to 255, 256 to 511, ...) at most 104 rows name the same one
- cotangent: bfloat16 [8192, 1536], P(('expert', 'shard')), may hold values from -6 to 6
- first_gain: bfloat16 [1536], P('shard'), may hold values from 0.5 to 1.5
- query_weight: bfloat16 [1536, 1536], P('shard'), may hold values from -0.15625 to 0.15625
- key_matrix: bfloat16 [1536, 512], P('shard'), may hold values from -0.15625 to 0.15625
- value_matrix: bfloat16 [1536, 512], P('shard'), may hold values from -0.15625 to 0.15625
- output_weight: bfloat16 [1536, 1536], P('shard'), may hold values from -1.25 to 1.25
- second_gain: bfloat16 [1536], P('shard'), may hold values from 0.5 to 1.5
- router_weight: bfloat16 [1536, 20], P('shard'), may hold values from -0.078125 to 0.078125
- gate_up_weight: bfloat16 [1536, 20, 1024], P('shard', 'expert'), may hold values from -0.15625 to 0.15625
- down_weight: bfloat16 [1536, 20, 512], P('shard', 'expert'), may hold values from -1 to 1
Outputs:
- layer_out: bfloat16 [8192, 1536], P(('expert', 'shard'))
- tokens_grad: float32 [8192, 1536], P(('expert', 'shard'))
- first_gain_grad: float32 [1536], P('shard')
- query_grad: float32 [1536, 1536], P('shard')
- key_grad: float32 [1536, 512], P('shard')
- value_grad: float32 [1536, 512], P('shard')
- output_grad: float32 [1536, 1536], P('shard')
- second_gain_grad: float32 [1536], P('shard')
- router_grad: float32 [1536, 20], P('shard')
- gate_up_grad: float32 [1536, 20, 1024], P('shard', 'expert')
- down_grad: float32 [1536, 20, 512], P('shard', 'expert')
The draws below stay inside these ranges and needn't reach their ends.
Inputs may be any that keep to these rules, and one draw needn't show every extreme that they name: `lengths`: some sequence has 256 valid tokens and some 256 // 4. `routes`: each row names 8 different experts; among the 256 rows of one sequence no expert is named more than 104 times, a bound that some block reaches.
All inputs are finite; a program needn't handle non-finite values.
Results may differ from the reference program's by a relative error of at most 0.02.
Values may be sent and summed in bfloat16 or wider, within the bound.
A program may use at most 320 MiB of HBM per device.

```python
import math
from functools import partial
import jax
import jax.numpy as jnp
import numpy as np
from jax import lax

MODEL_DIM = 1536
QUERY_HEADS = 24
KEY_VALUE_HEADS = 8
HEAD_DIM = 64
FFE = 512
TOPK = 8
SEQUENCE_SLOTS = 256
EXPERTS = 20
MOST = 104
NSEQ = 32
TOKENS = 8192


def draw_lengths(key, part):
    shortest = SEQUENCE_SLOTS // 4
    drawn = jax.random.randint(jax.random.fold_in(key, 11), (NSEQ,), shortest, SEQUENCE_SLOTS + 1)
    shuffled = jax.random.permutation(jax.random.fold_in(key, 12), NSEQ)
    drawn = drawn.at[shuffled[0]].set(SEQUENCE_SLOTS)
    drawn = drawn.at[shuffled[1]].set(shortest)
    return drawn.astype(jnp.int32)


def level_of(own_key, extent, cuts, low, high):
    factor_of = 1.0
    for dim, shards_of in cuts:
        heights = jax.random.uniform(jax.random.fold_in(jax.random.fold_in(own_key, 6), dim), (shards_of,), jnp.float32, low / len(cuts), high / len(cuts))
        factor_of = factor_of * jnp.repeat(jnp.exp(heights), extent[dim] // shards_of).reshape((-1,) + (1,) * (len(extent) - 1 - dim))
    return factor_of


def shared_out(own_key, own, number, rows, amount, top, bound, lean):
    ranking = jax.random.permutation(own_key, amount)
    heavy_load, ordinary = portions_of(amount, rows * top, bound, lean, True), portions_of(amount, rows * top, bound, lean, False)
    places = jnp.arange(amount)

    def named(sizes, rotation):
        used = int((sizes > 0).sum())
        fixed = max(1, used // 4)
        moved = fixed + (places - fixed + rotation * (used - fixed)) % max(1, amount - fixed)
        return jnp.zeros((amount,), jnp.int32).at[ranking[jnp.where(places < fixed, places, moved)]].set(jnp.asarray(sizes, jnp.int32))

    sizes = jnp.where(number % 4 == 0, named(heavy_load, number // 4), named(ordinary, number - number // 4 - 1))
    mixed = jax.random.permutation(jax.random.fold_in(own, 3), amount)
    giver, taker = mixed[0:amount // 2 * 2:2], mixed[1:amount // 2 * 2:2]
    room = jnp.minimum(sizes[giver] - 1, bound - sizes[taker]) // 2
    room = jnp.where((giver == ranking[0]) | (taker == ranking[0]) | (sizes[taker] == 0), 0, jnp.maximum(room, 0))
    moved = jax.random.randint(jax.random.fold_in(own, 4), (amount // 2,), 0, 1 << 20) % (room + 1)
    sizes = sizes.at[giver].add(-moved).at[taker].add(moved)
    members = jnp.searchsorted(jnp.cumsum(sizes), jnp.arange(rows * top), side="right").astype(jnp.int32)
    table = members.reshape(top, rows).T
    table = table[jax.random.permutation(jax.random.fold_in(own, 1), rows)]
    rotation = jax.random.randint(jax.random.fold_in(own, 2), (rows, 1), 0, top)
    return jnp.take_along_axis(table, (jnp.arange(top)[None, :] + rotation) % top, axis=1)


def portions_of(amount, total, reach, lean, full):
    portions = [(1 << 20) // math.isqrt(grade ** lean) + 1 for grade in range(1, amount + 1)]
    largest = reach if full else min(reach, max(-(-total // amount), total * portions[0] // sum(portions)))
    least = 1 if total - largest >= amount - 1 else 0
    holding, surplus = [largest] + [least] * (amount - 1), total - largest - least * (amount - 1)
    while surplus > 0:
        candidates = [i for i in range(1, amount) if holding[i] < largest] or [i for i in range(1, amount) if holding[i] < reach]
        whole, budget = sum([portions[i] for i in candidates]), surplus
        for i in candidates:
            more = min(reach - holding[i], max(1, budget * portions[i] // whole), surplus)
            holding[i] = holding[i] + more
            surplus = surplus - more
    return np.array(holding)


def gaussian(rng, dims, scale, reach, cuts=(), kind=jnp.bfloat16):
    loudness = level_of(rng, dims, cuts, -0.22, 0.18) if cuts else 1.0
    values = jax.random.normal(rng, dims, jnp.float32) * scale * loudness
    return jnp.minimum(jnp.maximum(values, -reach), reach).astype(kind)


def setup_inputs(seed: int = 0) -> dict:
    keys = jax.random.split(jax.random.key(seed), 14)
    tokens = gaussian(keys[0], (TOKENS, MODEL_DIM), 1.0, 6.0, ((0, 32),))
    lengths = draw_lengths(jax.random.fold_in(keys[13], 71), 0)
    routes_keys = jax.random.split(jax.random.fold_in(keys[2], 1), TOKENS // SEQUENCE_SLOTS)
    routes_turns = jax.random.permutation(jax.random.fold_in(keys[2], 3), TOKENS // SEQUENCE_SLOTS)
    routes = jax.vmap(lambda own, number: shared_out(jax.random.fold_in(keys[2], 2), own, number, SEQUENCE_SLOTS, EXPERTS, TOPK, MOST, 1))(routes_keys, routes_turns).reshape((TOKENS, TOPK))
    cotangent = gaussian(keys[3], (TOKENS, MODEL_DIM), 1.0, 6.0, ((0, 32),))
    first_gain = jnp.clip(1.0 + 0.1 * jax.random.normal(keys[4], (MODEL_DIM,), jnp.float32), 0.5, 1.5).astype(jnp.bfloat16)
    query_weight = gaussian(keys[5], (MODEL_DIM, QUERY_HEADS * HEAD_DIM), MODEL_DIM ** -0.5, 0.15625, ((0, 8),))
    key_matrix = gaussian(keys[6], (MODEL_DIM, KEY_VALUE_HEADS * HEAD_DIM), MODEL_DIM ** -0.5, 0.15625, ((0, 8),))
    value_matrix = gaussian(keys[7], (MODEL_DIM, KEY_VALUE_HEADS * HEAD_DIM), MODEL_DIM ** -0.5, 0.15625, ((0, 8),))
    output_weight = gaussian(keys[8], (MODEL_DIM, QUERY_HEADS * HEAD_DIM), (QUERY_HEADS * HEAD_DIM // 64) ** -0.5, 1.25, ((0, 8),))
    second_gain = jnp.clip(1.0 + 0.1 * jax.random.normal(keys[9], (MODEL_DIM,), jnp.float32), 0.5, 1.5).astype(jnp.bfloat16)
    router_weight = gaussian(keys[10], (MODEL_DIM, EXPERTS), (4 * MODEL_DIM) ** -0.5, 0.078125, ((0, 8),))
    gate_up_weight = gaussian(keys[11], (MODEL_DIM, EXPERTS, 2 * FFE), MODEL_DIM ** -0.5, 0.15625, ((0, 8), (1, 4)))
    down_weight = gaussian(keys[12], (MODEL_DIM, EXPERTS, FFE), (FFE // 16) ** -0.5, 1.0, ((0, 8), (1, 4)))
    return {"tokens": tokens, "lengths": lengths, "routes": routes, "cotangent": cotangent, "first_gain": first_gain, "query_weight": query_weight, "key_matrix": key_matrix, "value_matrix": value_matrix, "output_weight": output_weight, "second_gain": second_gain, "router_weight": router_weight, "gate_up_weight": gate_up_weight, "down_weight": down_weight}


norm_eps = 1e-06

@jax.custom_vjp
def low_precision(v):
    return lax.optimization_barrier(v.astype(jnp.bfloat16)).astype(jnp.float32)

@jax.custom_vjp
def low_precision_backward(v):
    return v

def low_keep(v):
    return (low_precision(v), None)

def low_pass(kept, grad):
    return (grad,)

def back_keep(v):
    return (v, None)

def back_low(kept, grad):
    return (low_precision(grad),)
low_precision.defvjp(low_keep, low_pass)
low_precision_backward.defvjp(back_keep, back_low)

def highest_precision(form, left, right):
    return jnp.einsum(form, left, right, precision=lax.Precision.HIGHEST)

def rope_tables():
    half_width = HEAD_DIM // 2
    frequency = 10000.0 ** (-(jnp.arange(half_width, dtype=jnp.float32) * (2.0 / HEAD_DIM)))
    angles = jnp.arange(SEQUENCE_SLOTS, dtype=jnp.float32)[:, None] * frequency[None, :]
    return (jnp.cos(angles)[:, None, :], jnp.sin(angles)[:, None, :])

def rotate(values_in, cosine, sine_table):
    half_width = HEAD_DIM // 2
    first_half = values_in[..., :half_width]
    second_half = values_in[..., half_width:]
    return jnp.concatenate([first_half * cosine - second_half * sine_table, second_half * cosine + first_half * sine_table], axis=-1)

def attend(seq_rows, length, params):
    first_gain, query_full, key_complete, value_complete, output_full, second_gain, router_full = params
    cosine, sine_table = rope_tables()
    first_scale = lax.rsqrt(lax.optimization_barrier(jnp.mean(seq_rows * seq_rows, axis=-1, keepdims=True)) + norm_eps)
    first_norm_output = low_precision(seq_rows * first_scale * first_gain)
    queries = low_precision_backward(highest_precision('za,ao->zo', first_norm_output, query_full)).reshape(SEQUENCE_SLOTS, QUERY_HEADS, HEAD_DIM)
    queries = low_precision(rotate(queries, cosine, sine_table))
    key_row_block = low_precision_backward(highest_precision('za,ao->zo', first_norm_output, key_complete)).reshape(SEQUENCE_SLOTS, KEY_VALUE_HEADS, HEAD_DIM)
    key_row_block = low_precision(rotate(key_row_block, cosine, sine_table))
    value_row_block = low_precision(low_precision_backward(highest_precision('za,ao->zo', first_norm_output, value_complete))).reshape(SEQUENCE_SLOTS, KEY_VALUE_HEADS, HEAD_DIM)
    key_row_block = jnp.repeat(key_row_block, QUERY_HEADS // KEY_VALUE_HEADS, axis=1)
    value_row_block = jnp.repeat(value_row_block, QUERY_HEADS // KEY_VALUE_HEADS, axis=1)
    scores = low_precision_backward(highest_precision('qhd,khd->hqk', queries, key_row_block) * HEAD_DIM ** (-0.5))
    position = jnp.arange(SEQUENCE_SLOTS, dtype=jnp.int32)
    allowed = (position[None, :] <= position[:, None]) & (position[None, :] < length)
    scores = jnp.where(allowed[None], scores, -1e+30)
    probabilities = low_precision(jax.nn.softmax(scores, axis=-1))
    mixed_heads = low_precision(low_precision_backward(highest_precision('hqk,khd->qhd', probabilities, value_row_block).reshape(SEQUENCE_SLOTS, QUERY_HEADS * HEAD_DIM)))
    attention = low_precision_backward(highest_precision('sf,df->sd', mixed_heads, output_full))
    hidden = seq_rows + attention
    second_scale = lax.rsqrt(lax.optimization_barrier(jnp.mean(hidden * hidden, axis=-1, keepdims=True)) + norm_eps)
    second_normed = low_precision(hidden * second_scale * second_gain)
    logits = low_precision_backward(highest_precision('sd,de->se', second_normed, router_full))
    return (hidden, second_normed, logits)

def group_layer(seq_block, length_block, route_block, params, experts):
    gate_up_full, down_full = experts
    hidden, second_normed, logits = jax.vmap(partial(attend, params=params))(seq_block, length_block)
    group_count = seq_block.shape[0]
    position = jnp.arange(SEQUENCE_SLOTS, dtype=jnp.int32)
    valid_rows = position[None, :] < length_block[:, None]
    chosen = route_block[..., None] == jnp.arange(EXPERTS, dtype=jnp.int32)
    picked = lax.optimization_barrier(jnp.sum(jnp.where(chosen, logits[:, :, None, :], 0.0), axis=-1))
    gate_soft = low_precision(jax.nn.softmax(picked, axis=-1))
    routed = jnp.any(chosen, axis=2) & valid_rows[:, :, None]
    used_int = routed.astype(jnp.int32)
    rank_rows = jnp.cumsum(used_int, axis=1) - used_int
    span_rows = group_count * MOST
    slot_index = jnp.arange(EXPERTS, dtype=jnp.int32)[None, None, :] * span_rows + jnp.arange(group_count, dtype=jnp.int32)[:, None, None] * MOST + rank_rows
    token_id = jnp.arange(group_count * SEQUENCE_SLOTS, dtype=jnp.int32).reshape(group_count, SEQUENCE_SLOTS)
    target = jnp.where(routed, slot_index, EXPERTS * span_rows)
    row_table = jnp.full((EXPERTS * span_rows,), group_count * SEQUENCE_SLOTS, jnp.int32)
    row_table = row_table.at[target.reshape(-1)].set(jnp.broadcast_to(token_id[:, :, None], target.shape).reshape(-1), mode='drop')
    padded_rows = jnp.concatenate([second_normed.reshape(-1, MODEL_DIM), jnp.zeros((1, MODEL_DIM), second_normed.dtype)], axis=0)
    inputs = low_precision_backward(padded_rows[row_table].reshape(EXPERTS, span_rows, MODEL_DIM))
    both_pre = low_precision_backward(highest_precision('emd,def->emf', inputs, gate_up_full))
    active = low_precision(jax.nn.silu(both_pre[..., :FFE]) * both_pre[..., FFE:])
    flat_answer = low_precision(low_precision_backward(highest_precision('emf,def->emd', active, down_full))).reshape(EXPERTS * span_rows, MODEL_DIM)
    expert_sum = jnp.zeros((group_count, SEQUENCE_SLOTS, MODEL_DIM), jnp.float32)
    for pick_number in range(TOPK):
        expert_id = route_block[:, :, pick_number]
        pick_index = jnp.take_along_axis(slot_index, expert_id[..., None], axis=-1)[..., 0]
        pick_index = jnp.where(valid_rows, pick_index, 0)
        weight = jnp.where(valid_rows, gate_soft[:, :, pick_number], 0.0)
        expert_sum = expert_sum + weight[..., None] * flat_answer[pick_index]
    return hidden + expert_sum

def reference(tokens, lengths, routes, cotangent, first_gain, query_weight, key_matrix, value_matrix, output_weight, second_gain, router_weight, gate_up_weight, down_weight):
    group_size = max(1, min(NSEQ, 4096 // SEQUENCE_SLOTS))
    while NSEQ % group_size:
        group_size -= 1
    group_count = NSEQ // group_size

    def forward(seq_all, gain_one, query_full, key_complete, value_complete, output_full, gain_two, router_full, gate_up_full, down_full):
        params = (gain_one, query_full, key_complete, value_complete, output_full, gain_two, router_full)

        def group_step(pieces):
            return group_layer(pieces[0], pieces[1], pieces[2], params, (gate_up_full, down_full))
        result = lax.map(jax.checkpoint(group_step), (seq_all.reshape(group_count, group_size, SEQUENCE_SLOTS, MODEL_DIM), lengths.reshape(group_count, group_size), routes.reshape(group_count, group_size, SEQUENCE_SLOTS, TOPK)))
        return result.reshape(NSEQ * SEQUENCE_SLOTS, MODEL_DIM)
    floats = [item_arg.astype(jnp.float32) for item_arg in (tokens, first_gain, query_weight, key_matrix, value_matrix, output_weight, second_gain, router_weight, gate_up_weight, down_weight)]
    layer_value, pullback = jax.vjp(forward, *floats)
    position = jnp.arange(SEQUENCE_SLOTS, dtype=jnp.int32)
    valid_rows = (position[None, :] < lengths[:, None]).reshape(NSEQ * SEQUENCE_SLOTS, 1)
    gradients = pullback(jnp.where(valid_rows, cotangent.astype(jnp.float32), 0.0))
    return (layer_value.astype(jnp.bfloat16), gradients[0], gradients[1], gradients[2], gradients[3], gradients[4], gradients[5], gradients[6], gradients[7], gradients[8], gradients[9])
```

```python
import functools
import itertools

import jax
import jax.numpy as jnp
from jax import lax
from jax.experimental import pallas as pl
from jax.experimental.pallas import tpu as pltpu
from jax.sharding import PartitionSpec as P

HEAD_DIM = 64
EXPERT, SHARD = "expert", "shard"


norm_eps = 1e-06


def product(form, left, right):
    return jnp.einsum(form, left, right, preferred_element_type=jnp.float32)


def rope_tables(row_count, head_width):
    half_width = head_width // 2
    frequency = 10000.0 ** (-(jnp.arange(half_width, dtype=jnp.float32) * (2.0 / head_width)))
    angles = jnp.arange(row_count, dtype=jnp.float32)[:, None] * frequency[None, :]
    return (jnp.cos(angles)[:, None, :], jnp.sin(angles)[:, None, :])


def rotate(values_in, cosine, sine_table):
    half_width = values_in.shape[-1] // 2
    first_half = values_in[..., :half_width]
    second_half = values_in[..., half_width:]
    return jnp.concatenate(
        [
            first_half * cosine - second_half * sine_table,
            second_half * cosine + first_half * sine_table,
        ],
        axis=-1,
    )


def unrotate(grad_in, cosine, sine_table):
    half_width = grad_in.shape[-1] // 2
    first_half = grad_in[..., :half_width]
    second_half = grad_in[..., half_width:]
    return jnp.concatenate(
        [
            first_half * cosine + second_half * sine_table,
            second_half * cosine - first_half * sine_table,
        ],
        axis=-1,
    )


def norm_back(upstream, source, inv_scale, gain_vec):
    scaled = upstream * gain_vec
    gain_grad = jnp.sum(upstream * source * inv_scale, axis=0)
    grad_out = inv_scale * (
        scaled - source * inv_scale * inv_scale * jnp.mean(scaled * source, axis=-1, keepdims=True)
    )
    return (grad_out, gain_grad)


def on_device(
    tokens,
    lengths,
    routes,
    cotangent,
    first_gain,
    query_weight,
    key_matrix,
    value_matrix,
    output_weight,
    second_gain,
    router_weight,
    gate_up_weight,
    down_weight,
):
    seq_len, model_width = tokens.shape
    route_width = routes.shape[1]
    q_heads = query_weight.shape[1] // HEAD_DIM
    kv_heads = key_matrix.shape[1] // HEAD_DIM
    group_size = q_heads // kv_heads
    experts_all = router_weight.shape[1]
    local_experts = gate_up_weight.shape[1]
    inner_width = down_weight.shape[2]
    owners = lax.axis_size(EXPERT)
    slot_count = 8 * max(
        seq_len // 32, (seq_len * route_width + 8 * experts_all - 1) // (8 * experts_all)
    )
    score_factor = HEAD_DIM ** (-0.5)
    gain_one, query_full, key_complete, value_complete, output_full, gain_two, router_full = (
        lax.all_gather(first_gain, SHARD, axis=0, tiled=True),
        lax.all_gather(query_weight, SHARD, axis=0, tiled=True),
        lax.all_gather(key_matrix, SHARD, axis=0, tiled=True),
        lax.all_gather(value_matrix, SHARD, axis=0, tiled=True),
        lax.all_gather(output_weight, SHARD, axis=0, tiled=True),
        lax.all_gather(second_gain, SHARD, axis=0, tiled=True),
        lax.all_gather(router_weight, SHARD, axis=0, tiled=True),
    )
    gate_up_full, down_full = (
        lax.all_gather(gate_up_weight, SHARD, axis=0, tiled=True),
        lax.all_gather(down_weight, SHARD, axis=0, tiled=True),
    )
    gain_one = gain_one.astype(jnp.float32)
    gain_two = gain_two.astype(jnp.float32)
    cosine, sine_table = rope_tables(seq_len, HEAD_DIM)
    source = tokens.astype(jnp.float32)
    first_scale = lax.rsqrt(jnp.mean(source * source, axis=-1, keepdims=True) + norm_eps)
    first_norm_output = (source * first_scale * gain_one).astype(jnp.bfloat16)
    queries = rotate(
        product("za,ao->zo", first_norm_output, query_full).reshape(seq_len, q_heads, HEAD_DIM),
        cosine,
        sine_table,
    )
    queries = queries.astype(jnp.bfloat16).reshape(seq_len, kv_heads, group_size, HEAD_DIM)
    key_row_block = rotate(
        product("za,ao->zo", first_norm_output, key_complete).reshape(seq_len, kv_heads, HEAD_DIM),
        cosine,
        sine_table,
    ).astype(jnp.bfloat16)
    value_row_block = (
        product("za,ao->zo", first_norm_output, value_complete)
        .astype(jnp.bfloat16)
        .reshape(seq_len, kv_heads, HEAD_DIM)
    )
    position = jnp.arange(seq_len, dtype=jnp.int32)
    length = lengths[0]
    allowed = (position[None, :] <= position[:, None]) & (position[None, :] < length)
    scores = jnp.where(
        allowed, product("qhgd,khd->hgqk", queries, key_row_block) * score_factor, -1e30
    )
    row_max = jnp.max(scores, axis=-1, keepdims=True)
    shifted = jnp.exp(scores - row_max)
    row_total = jnp.sum(shifted, axis=-1, keepdims=True)
    log_total = row_max + jnp.log(row_total)
    probs_low = (shifted / row_total).astype(jnp.bfloat16)
    mixed_heads = (
        product("hgqk,khd->qhgd", probs_low, value_row_block)
        .reshape(seq_len, q_heads * HEAD_DIM)
        .astype(jnp.bfloat16)
    )
    hidden = source + product("sf,df->sd", mixed_heads, output_full)
    second_scale = lax.rsqrt(jnp.mean(hidden * hidden, axis=-1, keepdims=True) + norm_eps)
    second_normed = (hidden * second_scale * gain_two).astype(jnp.bfloat16)
    logits = product("sd,de->se", second_normed, router_full)
    chosen = (routes[:, :, None] == jnp.arange(experts_all, dtype=jnp.int32)).astype(jnp.float32)
    picked = jnp.sum(chosen * logits[:, None, :], axis=-1)
    gate_soft = jax.nn.softmax(picked, axis=-1)
    valid_rows = (position < length).astype(jnp.float32)
    routed = jnp.sum(chosen, axis=1) * valid_rows[:, None]
    earlier = (position[None, :] < position[:, None]).astype(jnp.bfloat16)
    rank_rows = product("st,te->se", earlier, routed.astype(jnp.bfloat16))
    slot_ids = jnp.arange(slot_count, dtype=jnp.float32)
    placing = (routed.T[:, None, :] * (rank_rows.T[:, None, :] == slot_ids[None, :, None])).astype(
        jnp.bfloat16
    )
    outgoing = (
        product("ems,sd->emd", placing, second_normed)
        .astype(jnp.bfloat16)
        .reshape(owners, local_experts, slot_count, model_width)
    )
    row_block = lax.all_to_all(outgoing, EXPERT, split_axis=0, concat_axis=0, tiled=True)
    both_pre = product("oemd,def->oemf", row_block, gate_up_full)
    active = (jax.nn.silu(both_pre[..., :inner_width]) * both_pre[..., inner_width:]).astype(
        jnp.bfloat16
    )
    answer = product("oemf,def->oemd", active, down_full).astype(jnp.bfloat16)
    returned = lax.all_to_all(answer, EXPERT, split_axis=0, concat_axis=0, tiled=True).reshape(
        experts_all, slot_count, model_width
    )
    gate_full = product("ske,sk->se", chosen.astype(jnp.bfloat16), gate_soft.astype(jnp.bfloat16))
    placing_float = placing.astype(jnp.float32)
    combine = (placing_float * gate_full.T[:, None, :]).astype(jnp.bfloat16)
    output = (hidden + product("ems,emd->sd", combine, returned)).astype(jnp.bfloat16)
    dout_full = cotangent.astype(jnp.float32) * valid_rows[:, None]
    dout_low = dout_full.astype(jnp.bfloat16)
    grad_rows = (
        product("ems,sd->emd", combine, dout_low)
        .astype(jnp.bfloat16)
        .reshape(owners, local_experts, slot_count, model_width)
    )
    incoming = lax.all_to_all(grad_rows, EXPERT, split_axis=0, concat_axis=0, tiled=True)
    answer_dot = product("emd,sd->ems", returned, dout_low)
    gate_grad_full = jnp.sum(placing_float * answer_dot, axis=1)
    gate_grad = jnp.sum(chosen * gate_grad_full.T[:, None, :], axis=-1)
    inner_sum = jnp.sum(gate_soft * gate_grad, axis=-1, keepdims=True)
    picked_grad = gate_soft * (gate_grad - inner_sum)
    logits_grad = jnp.sum(chosen * picked_grad[:, :, None], axis=1).astype(jnp.bfloat16)
    router_term = product("sd,se->de", second_normed, logits_grad)
    gate_up_full, down_full = (
        lax.all_gather(gate_up_weight, SHARD, axis=0, tiled=True),
        lax.all_gather(down_weight, SHARD, axis=0, tiled=True),
    )
    gate_part = both_pre[..., :inner_width]
    up_part = both_pre[..., inner_width:]
    sigmoid_gate = jax.nn.sigmoid(gate_part)
    silu_gate = gate_part * sigmoid_gate
    active_again = (silu_gate * up_part).astype(jnp.bfloat16)
    active_grad = product("oemd,def->oemf", incoming, down_full)
    both_grad = jnp.concatenate(
        [
            active_grad * up_part * sigmoid_gate * (1.0 + gate_part * (1.0 - sigmoid_gate)),
            active_grad * silu_gate,
        ],
        axis=-1,
    ).astype(jnp.bfloat16)
    row_grad = product("oemf,def->oemd", both_grad, gate_up_full).astype(jnp.bfloat16)
    gate_up_term = product("oemd,oemf->def", row_block, both_grad)
    down_term = product("oemd,oemf->def", incoming, active_again)
    back_rows = lax.all_to_all(row_grad, EXPERT, split_axis=0, concat_axis=0, tiled=True).reshape(
        experts_all, slot_count, model_width
    )
    gate_up_total, down_total = (
        lax.psum_scatter(
            gate_up_term.astype(jnp.bfloat16), SHARD, scatter_dimension=0, tiled=True
        ).astype(jnp.float32),
        lax.psum_scatter(
            down_term.astype(jnp.bfloat16), SHARD, scatter_dimension=0, tiled=True
        ).astype(jnp.float32),
    )
    normed_grad = product("ems,emd->sd", placing, back_rows) + product(
        "se,de->sd", logits_grad, router_full
    )
    hidden_grad, second_gain_term = norm_back(normed_grad, hidden, second_scale, gain_two)
    hidden_grad = hidden_grad + dout_full
    attn_grad = hidden_grad.astype(jnp.bfloat16)
    output_term = product("sd,sf->df", attn_grad, mixed_heads)
    mixed_grad = (
        product("za,ao->zo", attn_grad, output_full)
        .astype(jnp.bfloat16)
        .reshape(seq_len, kv_heads, group_size, HEAD_DIM)
    )
    scores_again = jnp.where(
        allowed, product("qhgd,khd->hgqk", queries, key_row_block) * score_factor, -1e30
    )
    probs_again = jnp.exp(scores_again - log_total)
    probs_grad = product("qhgd,khd->hgqk", mixed_grad, value_row_block)
    row_inner = jnp.sum(probs_again * probs_grad, axis=-1, keepdims=True)
    scores_grad = (probs_again * (probs_grad - row_inner)).astype(jnp.bfloat16)
    query_back = product("hgqk,khd->qhgd", scores_grad, key_row_block) * score_factor
    key_back = product("hgqk,qhgd->khd", scores_grad, queries) * score_factor
    value_back = product("hgqk,qhgd->khd", probs_again.astype(jnp.bfloat16), mixed_grad)
    query_pre = (
        unrotate(query_back.reshape(seq_len, q_heads, HEAD_DIM), cosine, sine_table)
        .astype(jnp.bfloat16)
        .reshape(seq_len, q_heads * HEAD_DIM)
    )
    key_pre = (
        unrotate(key_back, cosine, sine_table)
        .astype(jnp.bfloat16)
        .reshape(seq_len, kv_heads * HEAD_DIM)
    )
    value_pre = value_back.astype(jnp.bfloat16).reshape(seq_len, kv_heads * HEAD_DIM)
    query_term = product("sd,sf->df", first_norm_output, query_pre)
    key_term = product("sd,sf->df", first_norm_output, key_pre)
    value_term = product("sd,sf->df", first_norm_output, value_pre)
    normed1_grad = (
        product("sf,df->sd", query_pre, query_full)
        + product("sf,df->sd", key_pre, key_complete)
        + product("sf,df->sd", value_pre, value_complete)
    )
    tokens_grad, first_gain_term = norm_back(normed1_grad, source, first_scale, gain_one)
    tokens_grad = tokens_grad + hidden_grad
    mixer_sums = (
        lax.psum_scatter(
            first_gain_term.astype(jnp.bfloat16), SHARD, scatter_dimension=0, tiled=True
        ).astype(jnp.float32),
        lax.psum_scatter(
            query_term.astype(jnp.bfloat16), SHARD, scatter_dimension=0, tiled=True
        ).astype(jnp.float32),
        lax.psum_scatter(
            key_term.astype(jnp.bfloat16), SHARD, scatter_dimension=0, tiled=True
        ).astype(jnp.float32),
        lax.psum_scatter(
            value_term.astype(jnp.bfloat16), SHARD, scatter_dimension=0, tiled=True
        ).astype(jnp.float32),
        lax.psum_scatter(
            output_term.astype(jnp.bfloat16), SHARD, scatter_dimension=0, tiled=True
        ).astype(jnp.float32),
        lax.psum_scatter(
            second_gain_term.astype(jnp.bfloat16), SHARD, scatter_dimension=0, tiled=True
        ).astype(jnp.float32),
        lax.psum_scatter(
            router_term.astype(jnp.bfloat16), SHARD, scatter_dimension=0, tiled=True
        ).astype(jnp.float32),
    )
    mixer_sums = (
        lax.psum(mixer_sums[0].astype(jnp.bfloat16), EXPERT).astype(jnp.float32),
        lax.psum(mixer_sums[1].astype(jnp.bfloat16), EXPERT).astype(jnp.float32),
        lax.psum(mixer_sums[2].astype(jnp.bfloat16), EXPERT).astype(jnp.float32),
        lax.psum(mixer_sums[3].astype(jnp.bfloat16), EXPERT).astype(jnp.float32),
        lax.psum(mixer_sums[4].astype(jnp.bfloat16), EXPERT).astype(jnp.float32),
        lax.psum(mixer_sums[5].astype(jnp.bfloat16), EXPERT).astype(jnp.float32),
        lax.psum(mixer_sums[6].astype(jnp.bfloat16), EXPERT).astype(jnp.float32),
    )
    return (
        output,
        tokens_grad,
        mixer_sums[0],
        mixer_sums[1],
        mixer_sums[2],
        mixer_sums[3],
        mixer_sums[4],
        mixer_sums[5],
        mixer_sums[6],
        gate_up_total,
        down_total,
    )


MESH_IDS = pl.DeviceIdType.MESH


class Place:
    def __init__(self):
        e, s = lax.axis_index(EXPERT), lax.axis_index(SHARD)
        self.y, self.c = lax.div(e, 2), lax.rem(e, 2)
        self.z, self.x = lax.div(s, 2), lax.rem(s, 2)
        self.ox, self.oy, self.oc = 1 - self.x, 1 - self.y, 1 - self.c
        self.to_x = (e, s + 1 - 2 * self.x)
        self.to_y = (e + 2 - 4 * self.y, s)
        self.to_c = (e + 1 - 2 * self.c, s)
        z = self.z
        self.zs = (z, z + 1 - 2 * lax.rem(z, 2), lax.rem(z + 2, 4), 3 - z)
        self.to_z = [None] + [(e, self.zs[d] * 2 + self.x) for d in (1, 2, 3)]


class Sender:
    def __init__(self, send_sem, recv_sem):
        self.send_sem, self.recv_sem, self.started = send_sem, recv_sem, []

    def __call__(self, source, target, device):
        number = len(self.started)
        assert number < self.send_sem.shape[0]
        copy = pltpu.make_async_remote_copy(
            src_ref=source,
            dst_ref=target,
            send_sem=self.send_sem.at[number],
            recv_sem=self.recv_sem.at[number],
            device_id=device,
            device_id_type=MESH_IDS,
        )
        copy.start()
        self.started.append(copy)
        return copy

    def finish(self):
        for copy in self.started:
            copy.wait_send()


def greet(devices):
    barrier = pltpu.get_barrier_semaphore()
    for device in devices:
        pl.semaphore_signal(barrier, inc=1, device_id=device, device_id_type=MESH_IDS)
    pl.semaphore_wait(barrier, len(devices))


def gather_in_plane(place, send, items, beside=lambda: None):
    x, y, c = place.x, place.y, place.c
    ox, oy = place.ox, place.oy
    first = []
    for view, source, ready, own in items:
        for copy in ready:
            copy.wait_recv()
        block = source(y, None)
        by_x = send(block, view(x, y, c, None), place.to_x)
        by_y, back = None, None
        if own:
            back = send(source(oy, 1), view(x, oy, c, 1), place.to_x)
        else:
            by_y = send(block, view(x, y, c, None), place.to_y)
        first.append((by_x, by_y, back))
    result = beside()
    landed = []
    for (view, source, ready, own), (by_x, by_y, back) in zip(items, first):
        if not own:
            landed.append(send(source(y, None), view(x, y, c, None), place.to_c))
        by_x.wait_recv()
        over_y = send(view(ox, y, c, 0), view(ox, y, c, 0), place.to_y)
        landed.append(send(view(ox, y, c, None), view(ox, y, c, None), place.to_c))
        if not own:
            by_y.wait_recv()
            back = send(view(x, oy, c, 1), view(x, oy, c, 1), place.to_x)
            landed.append(send(view(x, oy, c, None), view(x, oy, c, None), place.to_c))
        landed.append((view, over_y, back))
    final = []
    for entry in landed:
        if isinstance(entry, tuple):
            view, over_y, back = entry
            over_y.wait_recv()
            back.wait_recv()
            final.append(send(view(ox, oy, c, None), view(ox, oy, c, None), place.to_c))
        else:
            final.append(entry)
    for copy in final:
        copy.wait_recv()
    return result


def half_rows(half, rows):
    return pl.ds(0, rows) if half is None else pl.ds(half * (rows // 2), rows // 2)


def halves_kernel(first, count, *refs):
    up_ref, down_ref = refs[:2]
    outs, (send_sem, recv_sem, copy_sem) = refs[2 : 2 + count], refs[2 + count :]
    place = Place()
    send = Sender(send_sem, recv_sem)
    greet([place.to_x])
    sent, local = start_halves(place, send, copy_sem, up_ref, down_ref, outs, first)
    for copy in sent:
        copy.wait_recv()
    for copy in local:
        copy.wait()
    send.finish()


def start_halves(place, send, copy_sem, up_ref, down_ref, outs, first):
    x, ox = place.x, place.ox
    half = down_ref.shape[2] // 2
    sent, local = [], []
    for number, out in enumerate(outs):
        expert = first + number

        def pieces(xx):
            at = pl.ds(pl.multiple_of(xx * half, half), half)
            later = pl.ds(pl.multiple_of((xx + 2) * half, half), half)
            return (up_ref.at[expert, :, at], up_ref.at[expert, :, later], down_ref.at[expert, :, at])

        for index, piece in enumerate(pieces(ox)):
            sent.append(send(piece, out.at[x, :, index * half : (index + 1) * half], place.to_x))
        for index, piece in enumerate(pieces(x)):
            copy = pltpu.make_async_copy(
                piece, out.at[x, :, index * half : (index + 1) * half], copy_sem.at[3 * number + index]
            )
            copy.start()
            local.append(copy)
    return sent, local


def exchange_halves(up, down, count):
    depth, inner = down.shape[1:]
    return pl.pallas_call(
        functools.partial(halves_kernel, 0, count),
        out_shape=(jax.ShapeDtypeStruct((2, depth, 3 * inner // 2), up.dtype),) * count,
        in_specs=[pl.BlockSpec(memory_space=pltpu.VMEM)] * 2,
        out_specs=(pl.BlockSpec(memory_space=pl.ANY),) * count,
        scratch_shapes=[pltpu.SemaphoreType.DMA((3 * count,))] * 3,
        compiler_params=pltpu.CompilerParams(collective_id=4, has_side_effects=True),
        cost_estimate=pl.CostEstimate(flops=0, bytes_accessed=40_000_000, transcendentals=0),
        name="exchange_halves",
    )(up, down)


def weights_kernel(
    first, count, up_ref, down_ref, w_ref, o_ref, small_ref, rows_ref, w_out, o_out, small_out, rows_out, *refs
):
    outs, (send_sem, recv_sem, copy_sem, half_sem) = refs[:count], refs[count:]
    place = Place()
    send = Sender(send_sem, recv_sem)
    x, y, c, z = place.x, place.y, place.c, place.z
    depth = w_ref.shape[0]
    piece = depth // 4
    blocks = rows_ref.shape[0]
    greet([place.to_x, place.to_y, place.to_c] + place.to_z[1:])

    def columns(ref, yy, cc):
        part = ref.shape[1] // 4
        return pl.ds(pl.multiple_of((yy * 2 + cc) * part, part), part)

    def pieces(yy, cc, half):
        start = (yy * 2 + cc) * piece
        if half is None:
            return pl.ds(pl.multiple_of(start, piece), piece)
        return pl.ds(pl.multiple_of(start + half * (piece // 2), piece // 2), piece // 2)

    wide = [(w_ref, w_out), (o_ref, o_out)]
    from_z = {}
    for d in (1, 2, 3):
        from_z[d] = [
            send(ref.at[:, columns(ref, y, c)], out.at[z, x, :, columns(ref, y, c)], place.to_z[d])
            for ref, out in wide
        ] + [send(small_ref.at[pieces(y, c, None)], small_out.at[z, x, pieces(y, c, None)], place.to_z[d])]
    local = [
        pltpu.make_async_copy(w_ref, w_out.at[z, x], copy_sem.at[0]),
        pltpu.make_async_copy(o_ref, o_out.at[z, x], copy_sem.at[1]),
        pltpu.make_async_copy(small_ref, small_out.at[z, x], copy_sem.at[2]),
        pltpu.make_async_copy(rows_ref, rows_out.at[c, x, y], copy_sem.at[3]),
    ]
    for copy in local:
        copy.start()

    def wide_view(ref, out, zz):
        return lambda xx, yy, cc, half: out.at[zz, xx, half_rows(half, depth), columns(ref, yy, cc)]

    def small_view(zz):
        return lambda xx, yy, cc, half: small_out.at[zz, xx, pieces(yy, cc, half)]

    def rows_view(xx, yy, cc, half):
        return rows_out.at[cc, xx, yy, half_rows(half, blocks)]

    items = [
        (
            wide_view(ref, out, z),
            lambda yy, half, ref=ref: ref.at[half_rows(half, depth), columns(ref, yy, c)],
            [],
            True,
        )
        for ref, out in wide
    ]
    items.append((small_view(z), lambda yy, half: small_ref.at[pieces(yy, c, half)], [], True))
    for d in (1, 2, 3):
        zz = place.zs[d]
        views = [wide_view(ref, out, zz) for ref, out in wide] + [small_view(zz)]
        for view, copy in zip(views, from_z[d]):
            items.append((view, lambda yy, half, view=view: view(x, yy, c, half), [copy], False))
    items.append((rows_view, lambda yy, half: rows_ref.at[half_rows(half, blocks)], [], False))
    sent, kept = gather_in_plane(
        place, send, items, lambda: start_halves(place, send, half_sem, up_ref, down_ref, outs, first)
    )
    for copy in sent:
        copy.wait_recv()
    for copy in local + kept:
        copy.wait()
    send.finish()


def gather_weights(w, o, small, rows, up, down, first):
    depth, inner = down.shape[1:]
    count = up.shape[0] - first
    copies = 128
    arrays = (w, o, small)
    return pl.pallas_call(
        functools.partial(weights_kernel, first, count),
        out_shape=tuple(jax.ShapeDtypeStruct((4, 2) + a.shape, a.dtype) for a in arrays)
        + (jax.ShapeDtypeStruct((2, 2, 2) + rows.shape, rows.dtype),)
        + (jax.ShapeDtypeStruct((2, depth, 3 * inner // 2), up.dtype),) * count,
        in_specs=[pl.BlockSpec(memory_space=pltpu.VMEM)] * 6,
        out_specs=(pl.BlockSpec(memory_space=pl.ANY),) * (4 + count),
        scratch_shapes=[
            pltpu.SemaphoreType.DMA((copies,)),
            pltpu.SemaphoreType.DMA((copies,)),
            pltpu.SemaphoreType.DMA((4,)),
            pltpu.SemaphoreType.DMA((3 * count,)),
        ],
        compiler_params=pltpu.CompilerParams(collective_id=0, has_side_effects=True),
        cost_estimate=pl.CostEstimate(flops=0, bytes_accessed=200_000_000, transcendentals=0),
        name="gather_weights",
    )(up, down, w, o, small, rows)


def rows_kernel(a_ref, b_ref, a_out, b_out, send_sem, recv_sem, copy_sem):
    place = Place()
    send = Sender(send_sem, recv_sem)
    x, y, c = place.x, place.y, place.c
    rows = a_ref.shape[0]
    greet([place.to_x, place.to_y, place.to_c])
    local = [
        pltpu.make_async_copy(a_ref, a_out.at[c, x, y], copy_sem.at[0]),
        pltpu.make_async_copy(b_ref, b_out.at[c, x, y], copy_sem.at[1]),
    ]
    for copy in local:
        copy.start()

    def item(source, out):
        return (
            lambda xx, yy, cc, half: out.at[cc, xx, yy, half_rows(half, rows)],
            lambda yy, half: source.at[half_rows(half, rows)],
            [],
            False,
        )

    gather_in_plane(place, send, [item(b_ref, b_out), item(a_ref, a_out)])
    for copy in local:
        copy.wait()
    send.finish()


def gather_rows(a, b):
    return pl.pallas_call(
        rows_kernel,
        out_shape=(
            jax.ShapeDtypeStruct((2, 2, 2) + a.shape, a.dtype),
            jax.ShapeDtypeStruct((2, 2, 2) + b.shape, b.dtype),
        ),
        in_specs=[pl.BlockSpec(memory_space=pltpu.VMEM)] * 2,
        out_specs=(pl.BlockSpec(memory_space=pl.ANY),) * 2,
        scratch_shapes=[
            pltpu.SemaphoreType.DMA((16,)),
            pltpu.SemaphoreType.DMA((16,)),
            pltpu.SemaphoreType.DMA((2,)),
        ],
        compiler_params=pltpu.CompilerParams(collective_id=1, has_side_effects=True),
        cost_estimate=pl.CostEstimate(flops=0, bytes_accessed=90_000_000, transcendentals=0),
        name="gather_rows",
    )(a, b)


def add_into(target, left, right):
    lead = target.shape[:-2]
    rows = target.shape[-2]
    step = 16 if rows % 16 == 0 else 8
    count = rows // step

    def body(i, carry):
        at = pl.ds(pl.multiple_of(i * step, step), step)
        for index in itertools.product(*(range(n) for n in lead)):
            at_all = index + (at,)
            total = left[at_all].astype(jnp.float32) + right[at_all].astype(jnp.float32)
            target[at_all] = total.astype(target.dtype)
        return carry

    lax.fori_loop(0, count, body, 0)


class Part:
    def __init__(self, take, half, held, from_c, from_first, from_second):
        self.take, self.half, self.held, self.from_c = take, half, held, from_c
        self.from_first, self.from_second = from_first, from_second


def add_in_plane(place, send, parts, finish):
    x, y, c = place.x, place.y, place.c
    ox, oy, oc = place.ox, place.oy, place.oc
    from_core = []
    for part in parts:
        copies = {}
        for dx, dy in ((1, 1), (1, 0), (0, 1), (0, 0)):
            xx, yy = (ox if dx else x), (oy if dy else y)
            copies[dx, dy] = send(part.take(xx, yy, oc), part.from_c.at[xx, yy], place.to_c)
        from_core.append(copies)
    over = []
    for part, copies in zip(parts, from_core):
        for dx, dy in ((1, 1), (1, 0), (0, 1), (0, 0)):
            xx, yy = (ox if dx else x), (oy if dy else y)
            copies[dx, dy].wait_recv()
            add_into(part.held.at[xx, yy], part.take(xx, yy, c), part.from_c.at[xx, yy])
            if (dx, dy) == (1, 1):
                a0 = send(part.half(xx, yy, 0), part.from_first.at[0, 1], place.to_y)
                b0 = send(part.half(xx, yy, 1), part.from_first.at[1, 1], place.to_x)
            elif (dx, dy) == (1, 0):
                b1 = send(part.half(xx, yy, 1), part.from_first.at[1, 0], place.to_x)
            elif (dx, dy) == (0, 1):
                a1 = send(part.half(xx, yy, 0), part.from_first.at[0, 0], place.to_y)
        over.append((a0, b0, a1, b1))
    second = []
    for part, (a0, b0, a1, b1) in zip(parts, over):
        a0.wait_recv()
        add_into(part.half(ox, y, 0), part.half(ox, y, 0), part.from_first.at[0, 1])
        a2 = send(part.half(ox, y, 0), part.from_second.at[0], place.to_x)
        b0.wait_recv()
        add_into(part.half(x, oy, 1), part.half(x, oy, 1), part.from_first.at[1, 1])
        b2 = send(part.half(x, oy, 1), part.from_second.at[1], place.to_y)
        a1.wait_recv()
        add_into(part.half(x, y, 0), part.half(x, y, 0), part.from_first.at[0, 0])
        b1.wait_recv()
        add_into(part.half(x, y, 1), part.half(x, y, 1), part.from_first.at[1, 0])
        second.append((a2, b2))
    results = []
    for number, (part, (a2, b2)) in enumerate(zip(parts, second)):
        a2.wait_recv()
        b2.wait_recv()
        results.append(finish(number, part))
    return results


def rows_sum_kernel(
    grad_ref, value_ref, dots_ref, grad_out, value_out, dots_out,
    grad_held, value_held, dots_held, grad_c, value_c, dots_c,
    grad_first, value_first, dots_first, grad_second, value_second, dots_second,
    send_sem, recv_sem,
):
    place = Place()
    send = Sender(send_sem, recv_sem)
    x, y = place.x, place.y
    rows = grad_out.shape[0]
    greet([place.to_x, place.to_y, place.to_c])

    def part(ref, held, from_c, from_first, from_second):
        return Part(
            lambda xx, yy, cc: ref.at[cc, xx, yy],
            lambda xx, yy, half: held.at[xx, yy, half_rows(half, rows)],
            held, from_c, from_first, from_second,
        )

    parts = [
        part(dots_ref, dots_held, dots_c, dots_first, dots_second),
        part(grad_ref, grad_held, grad_c, grad_first, grad_second),
        part(value_ref, value_held, value_c, value_first, value_second),
    ]
    outs = [dots_out, grad_out, value_out]

    def finish(number, part):
        for half in (0, 1):
            add_into(outs[number].at[half_rows(half, rows)], part.half(x, y, half), part.from_second.at[half])

    add_in_plane(place, send, parts, finish)
    send.finish()


def sum_rows(grad, value, dots):
    rows = grad.shape[3]
    arrays = (grad, value, dots)

    def scratch(lead, height):
        return [pltpu.VMEM(lead + (height, a.shape[4]), a.dtype) for a in arrays]

    return pl.pallas_call(
        rows_sum_kernel,
        out_shape=tuple(jax.ShapeDtypeStruct(a.shape[3:], jnp.float32) for a in arrays),
        in_specs=[pl.BlockSpec(memory_space=pltpu.VMEM)] * 3,
        out_specs=(pl.BlockSpec(memory_space=pltpu.VMEM),) * 3,
        scratch_shapes=scratch((2, 2), rows)
        + scratch((2, 2), rows)
        + scratch((2, 2), rows // 2)
        + scratch((2,), rows // 2)
        + [pltpu.SemaphoreType.DMA((32,)), pltpu.SemaphoreType.DMA((32,))],
        compiler_params=pltpu.CompilerParams(
            collective_id=2, has_side_effects=True, vmem_limit_bytes=60 * 2**20
        ),
        cost_estimate=pl.CostEstimate(flops=0, bytes_accessed=150_000_000, transcendentals=0),
        name="sum_rows",
    )(*arrays)


def grads_kernel(count, *refs):
    total_refs, refs = refs[:count], refs[count:]
    ins, refs = refs[:3], refs[3:]
    outs, got_refs, refs = refs[:3], refs[3 : 3 + count], refs[3 + count :]
    held, from_c, from_first, from_second, own, from_z, alls = (refs[3 * i : 3 * i + 3] for i in range(7))
    send_sem, recv_sem = refs[21:]
    place = Place()
    send = Sender(send_sem, recv_sem)
    x, y, c, z = place.x, place.y, place.c, place.z
    greet([place.to_x, place.to_y, place.to_c] + place.to_z[1:])
    depth = ins[1].shape[2]
    piece = depth // 4
    heights = [piece, depth, depth]

    def take(number):
        ref = ins[number]
        if number == 0:
            return lambda xx, yy, cc: ref.at[:, xx, pl.ds(pl.multiple_of((yy * 2 + cc) * piece, piece), piece)]
        wide = ref.shape[3] // 4
        return lambda xx, yy, cc: ref.at[:, xx, :, pl.ds(pl.multiple_of((yy * 2 + cc) * wide, wide), wide)]

    def half_of(number):
        return lambda xx, yy, half: held[number].at[xx, yy, :, half_rows(half, heights[number])]

    parts = [
        Part(take(i), half_of(i), held[i], from_c[i], from_first[i], from_second[i]) for i in range(3)
    ]

    def finish(number, part):
        for half in (0, 1):
            add_into(
                own[number].at[:, half_rows(half, heights[number])],
                part.half(x, y, half),
                part.from_second.at[half],
            )
        return [send(own[number].at[place.zs[d]], from_z[number].at[d - 1], place.to_z[d]) for d in (1, 2, 3)]

    arriving = add_in_plane(place, send, parts, finish)
    swapped = [send(total.at[place.ox], got, place.to_x) for total, got in zip(total_refs, got_refs)]
    spread = []
    for number in range(3):
        mine, arrived = alls[number].at[y, c], from_z[number]
        for copy in arriving[number]:
            copy.wait_recv()
        add_into(arrived.at[0], arrived.at[0], arrived.at[1])
        add_into(arrived.at[2], arrived.at[2], own[number].at[z])
        add_into(mine, arrived.at[0], arrived.at[2])
        over_y = send(mine, mine, place.to_y)
        spread.append((over_y, send(mine, mine, place.to_c)))
    last = []
    for number in range(3):
        over_y, over_c = spread[number]
        over_y.wait_recv()
        other = alls[number].at[place.oy, c]
        last.append((over_c, send(other, other, place.to_c)))
    for number in range(3):
        for copy in last[number]:
            copy.wait_recv()
        for yy, cc in itertools.product((0, 1), (0, 1)):
            if number == 0:
                at = (yy * 2 + cc) * piece
                outs[0][at : at + piece, :] = alls[0][yy, cc]
                continue
            wide = alls[number].shape[3]
            at = (yy * 2 + cc) * wide

            def body(i, carry, number=number, at=at, yy=yy, cc=cc, wide=wide):
                rows = pl.ds(pl.multiple_of(i * 16, 16), 16)
                outs[number][rows, at : at + wide] = alls[number][yy, cc, rows, :].astype(jnp.float32)
                return carry

            lax.fori_loop(0, depth // 16, body, 0)
    for copy in swapped:
        copy.wait_recv()
    send.finish()


def sum_grads(small, output, mixer, totals):
    depth = output.shape[2]
    arrays = (small, output, mixer)
    shapes = [((depth // 4, small.shape[3]), small.dtype)]
    shapes += [((depth, a.shape[3] // 4), a.dtype) for a in arrays[1:]]
    count = len(totals)

    def scratch(lead, cut=1):
        return [pltpu.VMEM(lead + (height // cut, wide), kind) for (height, wide), kind in shapes]

    return pl.pallas_call(
        functools.partial(grads_kernel, count),
        out_shape=tuple(jax.ShapeDtypeStruct(a.shape[2:], jnp.float32) for a in arrays)
        + tuple(jax.ShapeDtypeStruct(t.shape[1:], t.dtype) for t in totals),
        in_specs=[pl.BlockSpec(memory_space=pl.ANY)] * count + [pl.BlockSpec(memory_space=pltpu.VMEM)] * 3,
        out_specs=(pl.BlockSpec(memory_space=pltpu.VMEM),) * 3 + (pl.BlockSpec(memory_space=pl.ANY),) * count,
        scratch_shapes=scratch((2, 2, 4))
        + scratch((2, 2, 4))
        + scratch((2, 2, 4), 2)
        + scratch((2, 4), 2)
        + scratch((4,))
        + scratch((3,))
        + scratch((2, 2))
        + [pltpu.SemaphoreType.DMA((64,)), pltpu.SemaphoreType.DMA((64,))],
        compiler_params=pltpu.CompilerParams(
            collective_id=3, has_side_effects=True, vmem_limit_bytes=60 * 2**20
        ),
        cost_estimate=pl.CostEstimate(flops=0, bytes_accessed=300_000_000, transcendentals=0),
        name="sum_grads",
    )(*totals, *arrays)


def swap_kernel(count, *refs):
    total_refs, got_refs, (send_sem, recv_sem) = refs[:count], refs[count : 2 * count], refs[2 * count :]
    place = Place()
    send = Sender(send_sem, recv_sem)
    greet([place.to_x])
    for total, got in zip(total_refs, got_refs):
        send(total.at[place.ox], got, place.to_x)
    for copy in send.started:
        copy.wait_recv()
    send.finish()


def swap_totals(totals):
    count = len(totals)
    return pl.pallas_call(
        functools.partial(swap_kernel, count),
        out_shape=tuple(jax.ShapeDtypeStruct(t.shape[1:], t.dtype) for t in totals),
        in_specs=[pl.BlockSpec(memory_space=pl.ANY)] * count,
        out_specs=(pl.BlockSpec(memory_space=pl.ANY),) * count,
        scratch_shapes=[pltpu.SemaphoreType.DMA((count,))] * 2,
        compiler_params=pltpu.CompilerParams(collective_id=5, has_side_effects=True),
        cost_estimate=pl.CostEstimate(flops=0, bytes_accessed=40_000_000, transcendentals=0),
        name="swap_totals",
    )(*totals)


def place_kernel(count, side_ref, *refs):
    kept_refs, got_refs = refs[:count], refs[count : 2 * count]
    up_out, down_out = refs[2 * count :]
    half = down_out.shape[2] // 2
    first = side_ref[0] == 0
    for expert in range(count):
        kept = kept_refs[expert][0].astype(jnp.float32)
        got = got_refs[expert][...].astype(jnp.float32)
        low, high = jnp.where(first, kept, got), jnp.where(first, got, kept)
        for index, part in enumerate((low, high)):
            for group in (0, 1):
                at = (2 * group + index) * half
                up_out[expert, :, at : at + half] = part[:, group * half : (group + 1) * half]
            down_out[expert, :, index * half : (index + 1) * half] = part[:, 2 * half :]


def place_sums(side, totals, got):
    count = len(totals)
    depth, width = got[0].shape
    step = depth // 4
    half = width // 3
    return pl.pallas_call(
        functools.partial(place_kernel, count),
        out_shape=(
            jax.ShapeDtypeStruct((count, depth, 4 * half), jnp.float32),
            jax.ShapeDtypeStruct((count, depth, 2 * half), jnp.float32),
        ),
        grid_spec=pltpu.PrefetchScalarGridSpec(
            num_scalar_prefetch=1,
            grid=(4,),
            in_specs=[pl.BlockSpec((1, step, width), lambda i, side: (side[0], i, 0))] * count
            + [pl.BlockSpec((step, width), lambda i, side: (i, 0))] * count,
            out_specs=(
                pl.BlockSpec((count, step, 4 * half), lambda i, side: (0, i, 0)),
                pl.BlockSpec((count, step, 2 * half), lambda i, side: (0, i, 0)),
            ),
        ),
        cost_estimate=pl.CostEstimate(flops=0, bytes_accessed=9_000_000, transcendentals=0),
        name="place_sums",
    )(side, *totals, *got)


def expert_kernel(slots_ref, gates_ref, rows_ref, dout_ref, w_ref, answer_ref, row_ref, w_out, dots_ref, total, picked, picked_dout):
    group, slot_rows, width = answer_ref.shape
    half = w_ref.shape[1] // 3
    seq_len = rows_ref.shape[1]
    step = pl.program_id(0)
    slot_ids = lax.broadcasted_iota(jnp.int32, (slot_rows, seq_len), 0).astype(jnp.float32)
    gate_parts = []
    for q in range(group):
        placing = (slot_ids == slots_ref[q]).astype(jnp.float32)
        gate_parts.append(jnp.sum(placing * gates_ref[q], axis=1, keepdims=True))
        low = placing.astype(jnp.bfloat16)
        at = slice(q * slot_rows, (q + 1) * slot_rows)
        picked[at, :] = jnp.dot(low, rows_ref[q], preferred_element_type=jnp.float32).astype(jnp.bfloat16)
        picked_dout[at, :] = jnp.dot(low, dout_ref[q], preferred_element_type=jnp.float32).astype(jnp.bfloat16)
    gate = jnp.concatenate(gate_parts, axis=0)
    both = jnp.dot(picked[...], w_ref[:, : 2 * half], preferred_element_type=jnp.float32)
    gate_part, up_part = both[:, :half], both[:, half:]
    sigmoid = 1.0 / (1.0 + jnp.exp(-gate_part))
    silu = gate_part * sigmoid
    active = (silu * up_part).astype(jnp.bfloat16)
    across = (((1,), (1,)), ((), ()))
    down = (((0,), (0,)), ((), ()))
    answer = lax.dot_general(active, w_ref[:, 2 * half :], across, preferred_element_type=jnp.float32)
    answer = answer.astype(jnp.bfloat16)
    dots = jnp.sum(picked_dout[...].astype(jnp.float32) * answer.astype(jnp.float32), axis=1, keepdims=True)
    for q in range(group):
        at = slice(q * slot_rows, (q + 1) * slot_rows)
        answer_ref[q] = answer[at, :]
        placing = (slot_ids == slots_ref[q]).astype(jnp.float32)
        dots_ref[q] = jnp.sum(placing * dots[at, :], axis=0, keepdims=True)
    picked_dout[...] = (picked_dout[...].astype(jnp.float32) * gate).astype(jnp.bfloat16)
    active_grad = jnp.dot(picked_dout[...], w_ref[:, 2 * half :], preferred_element_type=jnp.float32)
    both_grad = jnp.concatenate(
        [
            active_grad * up_part * sigmoid * (1.0 + gate_part * (1.0 - sigmoid)),
            active_grad * silu,
        ],
        axis=1,
    ).astype(jnp.bfloat16)
    row = lax.dot_general(both_grad, w_ref[:, : 2 * half], across, preferred_element_type=jnp.float32)
    row = row.astype(jnp.bfloat16)
    for q in range(group):
        row_ref[q] = row[q * slot_rows : (q + 1) * slot_rows, :]
    up_term = lax.dot_general(picked[...], both_grad, down, preferred_element_type=jnp.float32)
    down_term = lax.dot_general(picked_dout[...], active, down, preferred_element_type=jnp.float32)

    @pl.when(step == 0)
    def _():
        total[:, : 2 * half] = up_term
        total[:, 2 * half :] = down_term

    @pl.when(step > 0)
    def _():
        total[:, : 2 * half] += up_term
        total[:, 2 * half :] += down_term

    @pl.when(step == pl.num_programs(0) - 1)
    def _():
        w_out[...] = total[...].astype(w_out.dtype)


def run_expert(slots, gates, rows, dout, weights, slot_rows):
    count, seq_len, width = rows.shape
    group = count // 2
    wide = weights.shape[1]
    one = pl.BlockSpec((group, 1, seq_len), lambda i: (i, 0, 0))
    tall = pl.BlockSpec((group, seq_len, width), lambda i: (i, 0, 0))
    slot = pl.BlockSpec((group, slot_rows, width), lambda i: (i, 0, 0))
    whole = pl.BlockSpec(weights.shape, lambda i: (0, 0))
    flops = 2 * count * slot_rows * width * (2 * seq_len + 3 * wide)
    return pl.pallas_call(
        expert_kernel,
        grid=(2,),
        out_shape=(
            jax.ShapeDtypeStruct((count, slot_rows, width), jnp.bfloat16),
            jax.ShapeDtypeStruct((count, slot_rows, width), jnp.bfloat16),
            jax.ShapeDtypeStruct(weights.shape, jnp.bfloat16),
            jax.ShapeDtypeStruct((count, 1, seq_len), jnp.float32),
        ),
        in_specs=[one, one, tall, tall, whole],
        out_specs=(slot, slot, whole, one),
        scratch_shapes=[
            pltpu.VMEM(weights.shape, jnp.float32),
            pltpu.VMEM((group * slot_rows, width), jnp.bfloat16),
            pltpu.VMEM((group * slot_rows, width), jnp.bfloat16),
        ],
        compiler_params=pltpu.CompilerParams(vmem_limit_bytes=60 * 2**20),
        cost_estimate=pl.CostEstimate(flops=flops, bytes_accessed=25_000_000, transcendentals=0),
        name="run_expert",
    )(slots, gates, rows, dout, weights)


def combine_kernel(experts, table_ref, *refs):
    answers, rows = refs[:experts], refs[experts : 2 * experts]
    value_ref, grad_ref = refs[2 * experts :]
    slot_rows = answers[0].shape[1]
    table = table_ref[0]
    seq_len, lanes = table.shape
    slot_ids = lax.broadcasted_iota(jnp.int32, (seq_len, slot_rows), 1).astype(jnp.float32)
    placings, combines = [], []
    for expert in range(experts):
        placing = (slot_ids == table[:, experts + expert : experts + expert + 1]).astype(jnp.float32)
        placings.append(placing)
        combines.append(placing * table[:, expert : expert + 1])
    placing = jnp.concatenate(placings, axis=1).astype(jnp.bfloat16)
    combine = jnp.concatenate(combines, axis=1).astype(jnp.bfloat16)
    answer = jnp.concatenate([ref[0] for ref in answers], axis=0)
    row = jnp.concatenate([ref[0] for ref in rows], axis=0)
    value_ref[0] = jnp.dot(combine, answer, preferred_element_type=jnp.float32).astype(value_ref.dtype)
    grad_ref[0] = jnp.dot(placing, row, preferred_element_type=jnp.float32).astype(grad_ref.dtype)


def combine_experts(table, answers, rows):
    experts = len(answers)
    count, slot_rows, width = answers[0].shape
    seq_len = table.shape[1]
    slot = pl.BlockSpec((1, slot_rows, width), lambda i: (i, 0, 0))
    tall = pl.BlockSpec((1, seq_len, width), lambda i: (i, 0, 0))
    return pl.pallas_call(
        functools.partial(combine_kernel, experts),
        grid=(count,),
        out_shape=(jax.ShapeDtypeStruct((count, seq_len, width), jnp.bfloat16),) * 2,
        in_specs=[pl.BlockSpec((1,) + table.shape[1:], lambda i: (i, 0, 0))] + [slot] * (2 * experts),
        out_specs=(tall, tall),
        compiler_params=pltpu.CompilerParams(vmem_limit_bytes=60 * 2**20),
        cost_estimate=pl.CostEstimate(
            flops=4 * count * seq_len * width * experts * slot_rows, bytes_accessed=40_000_000, transcendentals=0
        ),
        name="combine_experts",
    )(table, *answers, *rows)


def layer_on_device(
    tokens,
    lengths,
    routes,
    cotangent,
    first_gain,
    query_weight,
    key_matrix,
    value_matrix,
    output_weight,
    second_gain,
    router_weight,
    gate_up_weight,
    down_weight,
):
    seq_len, model_width = tokens.shape
    q_heads = query_weight.shape[1] // HEAD_DIM
    kv_heads = key_matrix.shape[1] // HEAD_DIM
    group_size = q_heads // kv_heads
    experts_all = router_weight.shape[1]
    local_experts = gate_up_weight.shape[1]
    inner_width = down_weight.shape[2]
    half_inner = inner_width // 2
    q_width, kv_width = query_weight.shape[1], key_matrix.shape[1]
    slot_count = 8 * max(
        seq_len // 32, (seq_len * routes.shape[1] + 8 * experts_all - 1) // (8 * experts_all)
    )
    score_factor = HEAD_DIM ** (-0.5)
    along_z = [[z * 2 + x for z in range(4)] for x in range(2)]
    expert_at, shard_at = lax.axis_index(EXPERT), lax.axis_index(SHARD)
    x_at = lax.rem(shard_at, 2)
    depth = first_gain.shape[0]

    early = 2
    up_first = gate_up_weight.transpose(1, 0, 2)
    down_first = down_weight.transpose(1, 0, 2)

    def along(halves):
        return lax.all_gather(
            halves.reshape(2 * depth, 3 * half_inner), SHARD, axis=0, tiled=True, axis_index_groups=along_z
        )

    halves = exchange_halves(up_first, down_first, early)
    expert_weights = [along(h) for h in halves]

    position = jnp.arange(seq_len, dtype=jnp.int32)
    length = lengths[0]
    valid_rows = (position < length).astype(jnp.float32)
    dout_full = cotangent.astype(jnp.float32) * valid_rows[:, None]
    dout_low = dout_full.astype(jnp.bfloat16)
    mixer_block = jnp.concatenate([query_weight, key_matrix, value_matrix], axis=1)
    small_block = jnp.concatenate(
        [
            router_weight.astype(jnp.float32),
            first_gain.astype(jnp.float32)[:, None],
            second_gain.astype(jnp.float32)[:, None],
            jnp.zeros((depth, 128 - experts_all - 2), jnp.float32),
        ],
        axis=1,
    )
    mixer_block, output_block, small_block, dout_low = lax.optimization_barrier(
        (mixer_block, output_weight, small_block, dout_low) + tuple(halves)
    )[:4]
    mixer_full, output_full, small_full, dout_plane, *halves = gather_weights(
        mixer_block, output_block, small_block, dout_low, up_first, down_first, early
    )
    expert_weights += [along(h) for h in halves]
    mixer_full = mixer_full.reshape(model_width, mixer_block.shape[1])
    output_full = output_full.reshape(model_width, output_weight.shape[1])
    small_full = small_full.reshape(model_width, 128)
    dout_plane = dout_plane.reshape(8, seq_len, model_width)
    router_full = small_full[:, :experts_all].astype(jnp.bfloat16)
    gain_one, gain_two = small_full[:, experts_all], small_full[:, experts_all + 1]

    cosine, sine_table = rope_tables(seq_len, HEAD_DIM)
    source = tokens.astype(jnp.float32)
    first_scale = lax.rsqrt(jnp.mean(source * source, axis=-1, keepdims=True) + norm_eps)
    first_norm_output = (source * first_scale * gain_one).astype(jnp.bfloat16)
    mixed_in = product("za,ao->zo", first_norm_output, mixer_full)
    queries = rotate(mixed_in[:, :q_width].reshape(seq_len, q_heads, HEAD_DIM), cosine, sine_table)
    queries = queries.astype(jnp.bfloat16).reshape(seq_len, kv_heads, group_size, HEAD_DIM)
    key_row_block = rotate(
        mixed_in[:, q_width : q_width + kv_width].reshape(seq_len, kv_heads, HEAD_DIM), cosine, sine_table
    ).astype(jnp.bfloat16)
    value_row_block = (
        mixed_in[:, q_width + kv_width :].astype(jnp.bfloat16).reshape(seq_len, kv_heads, HEAD_DIM)
    )
    allowed = (position[None, :] <= position[:, None]) & (position[None, :] < length)
    scores = jnp.where(
        allowed, product("qhgd,khd->hgqk", queries, key_row_block) * score_factor, -1e30
    )
    row_max = jnp.max(scores, axis=-1, keepdims=True)
    shifted = jnp.exp(scores - row_max)
    row_total = jnp.sum(shifted, axis=-1, keepdims=True)
    log_total = row_max + jnp.log(row_total)
    probs_low = (shifted / row_total).astype(jnp.bfloat16)
    mixed_heads = (
        product("hgqk,khd->qhgd", probs_low, value_row_block)
        .reshape(seq_len, q_heads * HEAD_DIM)
        .astype(jnp.bfloat16)
    )
    hidden = source + product("sf,df->sd", mixed_heads, output_full)
    second_scale = lax.rsqrt(jnp.mean(hidden * hidden, axis=-1, keepdims=True) + norm_eps)
    second_normed = (hidden * second_scale * gain_two).astype(jnp.bfloat16)
    logits = product("sd,de->se", second_normed, router_full)
    chosen = (routes[:, :, None] == jnp.arange(experts_all, dtype=jnp.int32)).astype(jnp.float32)
    picked = jnp.sum(chosen * logits[:, None, :], axis=-1)
    gate_soft = jax.nn.softmax(picked, axis=-1)
    routed = jnp.sum(chosen, axis=1) * valid_rows[:, None]
    earlier = (position[None, :] < position[:, None]).astype(jnp.bfloat16)
    rank_rows = product("st,te->se", earlier, routed.astype(jnp.bfloat16))
    slot_of = jnp.where(routed > 0, rank_rows, -1.0)
    gate_low = gate_soft.astype(jnp.bfloat16).astype(jnp.float32)
    gate_full = jnp.sum(chosen * gate_low[:, :, None], axis=1)
    table = jnp.concatenate(
        [gate_full, slot_of, jnp.zeros((seq_len, 128 - 2 * experts_all), jnp.float32)], axis=1
    )
    rows_plane, table_plane = gather_rows(second_normed, table)
    rows_plane = rows_plane.reshape(8, seq_len, model_width)
    table_plane = table_plane.reshape(8, seq_len, 128)
    first_own = expert_at * local_experts
    gates = lax.dynamic_slice_in_dim(table_plane, first_own, local_experts, axis=2)
    slots = lax.dynamic_slice_in_dim(table_plane, experts_all + first_own, local_experts, axis=2)
    own_table = jnp.concatenate(
        [gates, slots, jnp.zeros((8, seq_len, 128 - 2 * local_experts), jnp.float32)], axis=2
    )
    gates_by = gates.transpose(2, 0, 1)[:, :, None, :]
    slots_by = slots.transpose(2, 0, 1)[:, :, None, :]
    slot_rows = -(-slot_count // 16) * 16
    answers, row_grads, sums, dots = zip(
        *(
            run_expert(slots_by[e], gates_by[e], rows_plane, dout_plane, expert_weights[e], slot_rows)
            for e in range(local_experts)
        )
    )
    sums = lax.optimization_barrier(tuple(sums) + (expert_weights[-1],))[:-1]
    value_part, grad_part = combine_experts(own_table, answers, row_grads)
    dots = jnp.stack([dot[:, 0, :] for dot in dots], axis=-1)
    dot_part = lax.dynamic_update_slice_in_dim(jnp.zeros((8, seq_len, 128), jnp.float32), dots, first_own, axis=2)
    plane = (2, 2, 2, seq_len)
    grad_rows, value_rows, dot_rows = sum_rows(
        grad_part.reshape(plane + (model_width,)),
        value_part.reshape(plane + (model_width,)),
        dot_part.reshape(plane + (128,)),
    )
    output = (hidden + value_rows).astype(jnp.bfloat16)
    gate_grad = jnp.sum(chosen * dot_rows[:, None, :experts_all], axis=-1)
    inner_sum = jnp.sum(gate_soft * gate_grad, axis=-1, keepdims=True)
    picked_grad = gate_soft * (gate_grad - inner_sum)
    logits_grad = jnp.sum(chosen * picked_grad[:, :, None], axis=1).astype(jnp.bfloat16)
    router_term = product("sd,se->de", second_normed, logits_grad)

    totals = [
        lax.psum_scatter(
            sums[expert], SHARD, scatter_dimension=0, tiled=True, axis_index_groups=along_z
        ).reshape(2, depth, 3 * half_inner)
        for expert in range(local_experts)
    ]

    normed_grad = grad_rows + product("se,de->sd", logits_grad, router_full)
    hidden_grad, second_gain_term = norm_back(normed_grad, hidden, second_scale, gain_two)
    hidden_grad = hidden_grad + dout_full
    attn_grad = hidden_grad.astype(jnp.bfloat16)
    output_term = product("sd,sf->df", attn_grad, mixed_heads)
    mixed_grad = (
        product("za,ao->zo", attn_grad, output_full)
        .astype(jnp.bfloat16)
        .reshape(seq_len, kv_heads, group_size, HEAD_DIM)
    )
    scores_again = jnp.where(
        allowed, product("qhgd,khd->hgqk", queries, key_row_block) * score_factor, -1e30
    )
    probs_again = jnp.exp(scores_again - log_total)
    probs_grad = product("qhgd,khd->hgqk", mixed_grad, value_row_block)
    row_inner = jnp.sum(probs_again * probs_grad, axis=-1, keepdims=True)
    scores_grad = (probs_again * (probs_grad - row_inner)).astype(jnp.bfloat16)
    query_back = product("hgqk,khd->qhgd", scores_grad, key_row_block) * score_factor
    key_back = product("hgqk,qhgd->khd", scores_grad, queries) * score_factor
    value_back = product("hgqk,qhgd->khd", probs_again.astype(jnp.bfloat16), mixed_grad)
    query_pre = (
        unrotate(query_back.reshape(seq_len, q_heads, HEAD_DIM), cosine, sine_table)
        .astype(jnp.bfloat16)
        .reshape(seq_len, q_heads * HEAD_DIM)
    )
    key_pre = (
        unrotate(key_back, cosine, sine_table)
        .astype(jnp.bfloat16)
        .reshape(seq_len, kv_heads * HEAD_DIM)
    )
    value_pre = value_back.astype(jnp.bfloat16).reshape(seq_len, kv_heads * HEAD_DIM)
    mixed_pre = jnp.concatenate([query_pre, key_pre, value_pre], axis=1)
    mixer_term = product("sd,sf->df", first_norm_output, mixed_pre).astype(jnp.bfloat16)
    normed1_grad = product("sf,df->sd", mixed_pre, mixer_full)
    tokens_grad, first_gain_term = norm_back(normed1_grad, source, first_scale, gain_one)
    tokens_grad = tokens_grad + hidden_grad
    small_terms = jnp.concatenate(
        [
            router_term,
            first_gain_term[:, None],
            second_gain_term[:, None],
            jnp.zeros((model_width, 128 - experts_all - 2), jnp.float32),
        ],
        axis=1,
    ).reshape(4, 2, depth, 128)
    swapped = 3
    small_sum, output_sum, mixer_sum, *got = sum_grads(
        small_terms,
        output_term.astype(jnp.bfloat16).reshape(4, 2, depth, output_weight.shape[1]),
        mixer_term.reshape(4, 2, depth, mixer_block.shape[1]),
        totals[:swapped],
    )
    late = lax.optimization_barrier((small_sum,) + tuple(totals[swapped:]))[1:]
    got += swap_totals(late)
    both_sums, down_sums = place_sums(x_at.reshape(1), totals, got)
    return (
        output,
        tokens_grad,
        small_sum[:, experts_all],
        mixer_sum[:, :q_width],
        mixer_sum[:, q_width : q_width + kv_width],
        mixer_sum[:, q_width + kv_width :],
        output_sum,
        small_sum[:, experts_all + 1],
        small_sum[:, :experts_all],
        both_sums.transpose(1, 0, 2),
        down_sums.transpose(1, 0, 2),
    )


def solution(mesh):
    small_slice = mesh.shape[EXPERT] == 4 and mesh.shape[SHARD] == 8
    placed = (
        P((EXPERT, SHARD), None),
        P((EXPERT, SHARD)),
        P((EXPERT, SHARD), None),
        P((EXPERT, SHARD), None),
        P(SHARD),
        P(SHARD, None),
        P(SHARD, None),
        P(SHARD, None),
        P(SHARD, None),
        P(SHARD),
        P(SHARD, None),
        P(SHARD, EXPERT, None),
        P(SHARD, EXPERT, None),
    )
    return jax.shard_map(
        layer_on_device if small_slice else on_device,
        mesh=mesh,
        in_specs=placed,
        out_specs=(
            P((EXPERT, SHARD), None),
            P((EXPERT, SHARD), None),
            P(SHARD),
            P(SHARD, None),
            P(SHARD, None),
            P(SHARD, None),
            P(SHARD, None),
            P(SHARD),
            P(SHARD, None),
            P(SHARD, EXPERT, None),
            P(SHARD, EXPERT, None),
        ),
        check_vma=False,
    )
```

```python
import functools
import itertools

import jax
import jax.numpy as jnp
from jax import lax
from jax.experimental import pallas as pl
from jax.experimental.pallas import tpu as pltpu
from jax.sharding import PartitionSpec as P

HEAD_DIM = 64
EXPERT, SHARD = "expert", "shard"


norm_eps = 1e-06


def product(form, left, right):
    return jnp.einsum(form, left, right, preferred_element_type=jnp.float32)


def rope_tables(row_count, head_width):
    half_width = head_width // 2
    frequency = 10000.0 ** (-(jnp.arange(half_width, dtype=jnp.float32) * (2.0 / head_width)))
    angles = jnp.arange(row_count, dtype=jnp.float32)[:, None] * frequency[None, :]
    return (jnp.cos(angles)[:, None, :], jnp.sin(angles)[:, None, :])


def rotate(values_in, cosine, sine_table):
    half_width = values_in.shape[-1] // 2
    first_half = values_in[..., :half_width]
    second_half = values_in[..., half_width:]
    return jnp.concatenate(
        [
            first_half * cosine - second_half * sine_table,
            second_half * cosine + first_half * sine_table,
        ],
        axis=-1,
    )


def unrotate(grad_in, cosine, sine_table):
    half_width = grad_in.shape[-1] // 2
    first_half = grad_in[..., :half_width]
    second_half = grad_in[..., half_width:]
    return jnp.concatenate(
        [
            first_half * cosine + second_half * sine_table,
            second_half * cosine - first_half * sine_table,
        ],
        axis=-1,
    )


def norm_back(upstream, source, inv_scale, gain_vec):
    scaled = upstream * gain_vec
    gain_grad = jnp.sum(upstream * source * inv_scale, axis=0)
    grad_out = inv_scale * (
        scaled - source * inv_scale * inv_scale * jnp.mean(scaled * source, axis=-1, keepdims=True)
    )
    return (grad_out, gain_grad)


def on_device(
    tokens,
    lengths,
    routes,
    cotangent,
    first_gain,
    query_weight,
    key_matrix,
    value_matrix,
    output_weight,
    second_gain,
    router_weight,
    gate_up_weight,
    down_weight,
):
    seq_len, model_width = tokens.shape
    route_width = routes.shape[1]
    q_heads = query_weight.shape[1] // HEAD_DIM
    kv_heads = key_matrix.shape[1] // HEAD_DIM
    group_size = q_heads // kv_heads
    experts_all = router_weight.shape[1]
    local_experts = gate_up_weight.shape[1]
    inner_width = down_weight.shape[2]
    owners = lax.axis_size(EXPERT)
    slot_count = 8 * max(
        seq_len // 32, (seq_len * route_width + 8 * experts_all - 1) // (8 * experts_all)
    )
    score_factor = HEAD_DIM ** (-0.5)
    gain_one, query_full, key_complete, value_complete, output_full, gain_two, router_full = (
        lax.all_gather(first_gain, SHARD, axis=0, tiled=True),
        lax.all_gather(query_weight, SHARD, axis=0, tiled=True),
        lax.all_gather(key_matrix, SHARD, axis=0, tiled=True),
        lax.all_gather(value_matrix, SHARD, axis=0, tiled=True),
        lax.all_gather(output_weight, SHARD, axis=0, tiled=True),
        lax.all_gather(second_gain, SHARD, axis=0, tiled=True),
        lax.all_gather(router_weight, SHARD, axis=0, tiled=True),
    )
    gate_up_full, down_full = (
        lax.all_gather(gate_up_weight, SHARD, axis=0, tiled=True),
        lax.all_gather(down_weight, SHARD, axis=0, tiled=True),
    )
    gain_one = gain_one.astype(jnp.float32)
    gain_two = gain_two.astype(jnp.float32)
    cosine, sine_table = rope_tables(seq_len, HEAD_DIM)
    source = tokens.astype(jnp.float32)
    first_scale = lax.rsqrt(jnp.mean(source * source, axis=-1, keepdims=True) + norm_eps)
    first_norm_output = (source * first_scale * gain_one).astype(jnp.bfloat16)
    queries = rotate(
        product("za,ao->zo", first_norm_output, query_full).reshape(seq_len, q_heads, HEAD_DIM),
        cosine,
        sine_table,
    )
    queries = queries.astype(jnp.bfloat16).reshape(seq_len, kv_heads, group_size, HEAD_DIM)
    key_row_block = rotate(
        product("za,ao->zo", first_norm_output, key_complete).reshape(seq_len, kv_heads, HEAD_DIM),
        cosine,
        sine_table,
    ).astype(jnp.bfloat16)
    value_row_block = (
        product("za,ao->zo", first_norm_output, value_complete)
        .astype(jnp.bfloat16)
        .reshape(seq_len, kv_heads, HEAD_DIM)
    )
    position = jnp.arange(seq_len, dtype=jnp.int32)
    length = lengths[0]
    allowed = (position[None, :] <= position[:, None]) & (position[None, :] < length)
    scores = jnp.where(
        allowed, product("qhgd,khd->hgqk", queries, key_row_block) * score_factor, -1e30
    )
    row_max = jnp.max(scores, axis=-1, keepdims=True)
    shifted = jnp.exp(scores - row_max)
    row_total = jnp.sum(shifted, axis=-1, keepdims=True)
    log_total = row_max + jnp.log(row_total)
    probs_low = (shifted / row_total).astype(jnp.bfloat16)
    mixed_heads = (
        product("hgqk,khd->qhgd", probs_low, value_row_block)
        .reshape(seq_len, q_heads * HEAD_DIM)
        .astype(jnp.bfloat16)
    )
    hidden = source + product("sf,df->sd", mixed_heads, output_full)
    second_scale = lax.rsqrt(jnp.mean(hidden * hidden, axis=-1, keepdims=True) + norm_eps)
    second_normed = (hidden * second_scale * gain_two).astype(jnp.bfloat16)
    logits = product("sd,de->se", second_normed, router_full)
    chosen = (routes[:, :, None] == jnp.arange(experts_all, dtype=jnp.int32)).astype(jnp.float32)
    picked = jnp.sum(chosen * logits[:, None, :], axis=-1)
    gate_soft = jax.nn.softmax(picked, axis=-1)
    valid_rows = (position < length).astype(jnp.float32)
    routed = jnp.sum(chosen, axis=1) * valid_rows[:, None]
    earlier = (position[None, :] < position[:, None]).astype(jnp.bfloat16)
    rank_rows = product("st,te->se", earlier, routed.astype(jnp.bfloat16))
    slot_ids = jnp.arange(slot_count, dtype=jnp.float32)
    placing = (routed.T[:, None, :] * (rank_rows.T[:, None, :] == slot_ids[None, :, None])).astype(
        jnp.bfloat16
    )
    outgoing = (
        product("ems,sd->emd", placing, second_normed)
        .astype(jnp.bfloat16)
        .reshape(owners, local_experts, slot_count, model_width)
    )
    row_block = lax.all_to_all(outgoing, EXPERT, split_axis=0, concat_axis=0, tiled=True)
    both_pre = product("oemd,def->oemf", row_block, gate_up_full)
    active = (jax.nn.silu(both_pre[..., :inner_width]) * both_pre[..., inner_width:]).astype(
        jnp.bfloat16
    )
    answer = product("oemf,def->oemd", active, down_full).astype(jnp.bfloat16)
    returned = lax.all_to_all(answer, EXPERT, split_axis=0, concat_axis=0, tiled=True).reshape(
        experts_all, slot_count, model_width
    )
    gate_full = product("ske,sk->se", chosen.astype(jnp.bfloat16), gate_soft.astype(jnp.bfloat16))
    placing_float = placing.astype(jnp.float32)
    combine = (placing_float * gate_full.T[:, None, :]).astype(jnp.bfloat16)
    output = (hidden + product("ems,emd->sd", combine, returned)).astype(jnp.bfloat16)
    dout_full = cotangent.astype(jnp.float32) * valid_rows[:, None]
    dout_low = dout_full.astype(jnp.bfloat16)
    grad_rows = (
        product("ems,sd->emd", combine, dout_low)
        .astype(jnp.bfloat16)
        .reshape(owners, local_experts, slot_count, model_width)
    )
    incoming = lax.all_to_all(grad_rows, EXPERT, split_axis=0, concat_axis=0, tiled=True)
    answer_dot = product("emd,sd->ems", returned, dout_low)
    gate_grad_full = jnp.sum(placing_float * answer_dot, axis=1)
    gate_grad = jnp.sum(chosen * gate_grad_full.T[:, None, :], axis=-1)
    inner_sum = jnp.sum(gate_soft * gate_grad, axis=-1, keepdims=True)
    picked_grad = gate_soft * (gate_grad - inner_sum)
    logits_grad = jnp.sum(chosen * picked_grad[:, :, None], axis=1).astype(jnp.bfloat16)
    router_term = product("sd,se->de", second_normed, logits_grad)
    gate_up_full, down_full = (
        lax.all_gather(gate_up_weight, SHARD, axis=0, tiled=True),
        lax.all_gather(down_weight, SHARD, axis=0, tiled=True),
    )
    gate_part = both_pre[..., :inner_width]
    up_part = both_pre[..., inner_width:]
    sigmoid_gate = jax.nn.sigmoid(gate_part)
    silu_gate = gate_part * sigmoid_gate
    active_again = (silu_gate * up_part).astype(jnp.bfloat16)
    active_grad = product("oemd,def->oemf", incoming, down_full)
    both_grad = jnp.concatenate(
        [
            active_grad * up_part * sigmoid_gate * (1.0 + gate_part * (1.0 - sigmoid_gate)),
            active_grad * silu_gate,
        ],
        axis=-1,
    ).astype(jnp.bfloat16)
    row_grad = product("oemf,def->oemd", both_grad, gate_up_full).astype(jnp.bfloat16)
    gate_up_term = product("oemd,oemf->def", row_block, both_grad)
    down_term = product("oemd,oemf->def", incoming, active_again)
    back_rows = lax.all_to_all(row_grad, EXPERT, split_axis=0, concat_axis=0, tiled=True).reshape(
        experts_all, slot_count, model_width
    )
    gate_up_total, down_total = (
        lax.psum_scatter(
            gate_up_term.astype(jnp.bfloat16), SHARD, scatter_dimension=0, tiled=True
        ).astype(jnp.float32),
        lax.psum_scatter(
            down_term.astype(jnp.bfloat16), SHARD, scatter_dimension=0, tiled=True
        ).astype(jnp.float32),
    )
    normed_grad = product("ems,emd->sd", placing, back_rows) + product(
        "se,de->sd", logits_grad, router_full
    )
    hidden_grad, second_gain_term = norm_back(normed_grad, hidden, second_scale, gain_two)
    hidden_grad = hidden_grad + dout_full
    attn_grad = hidden_grad.astype(jnp.bfloat16)
    output_term = product("sd,sf->df", attn_grad, mixed_heads)
    mixed_grad = (
        product("za,ao->zo", attn_grad, output_full)
        .astype(jnp.bfloat16)
        .reshape(seq_len, kv_heads, group_size, HEAD_DIM)
    )
    scores_again = jnp.where(
        allowed, product("qhgd,khd->hgqk", queries, key_row_block) * score_factor, -1e30
    )
    probs_again = jnp.exp(scores_again - log_total)
    probs_grad = product("qhgd,khd->hgqk", mixed_grad, value_row_block)
    row_inner = jnp.sum(probs_again * probs_grad, axis=-1, keepdims=True)
    scores_grad = (probs_again * (probs_grad - row_inner)).astype(jnp.bfloat16)
    query_back = product("hgqk,khd->qhgd", scores_grad, key_row_block) * score_factor
    key_back = product("hgqk,qhgd->khd", scores_grad, queries) * score_factor
    value_back = product("hgqk,qhgd->khd", probs_again.astype(jnp.bfloat16), mixed_grad)
    query_pre = (
        unrotate(query_back.reshape(seq_len, q_heads, HEAD_DIM), cosine, sine_table)
        .astype(jnp.bfloat16)
        .reshape(seq_len, q_heads * HEAD_DIM)
    )
    key_pre = (
        unrotate(key_back, cosine, sine_table)
        .astype(jnp.bfloat16)
        .reshape(seq_len, kv_heads * HEAD_DIM)
    )
    value_pre = value_back.astype(jnp.bfloat16).reshape(seq_len, kv_heads * HEAD_DIM)
    query_term = product("sd,sf->df", first_norm_output, query_pre)
    key_term = product("sd,sf->df", first_norm_output, key_pre)
    value_term = product("sd,sf->df", first_norm_output, value_pre)
    normed1_grad = (
        product("sf,df->sd", query_pre, query_full)
        + product("sf,df->sd", key_pre, key_complete)
        + product("sf,df->sd", value_pre, value_complete)
    )
    tokens_grad, first_gain_term = norm_back(normed1_grad, source, first_scale, gain_one)
    tokens_grad = tokens_grad + hidden_grad
    mixer_sums = (
        lax.psum_scatter(
            first_gain_term.astype(jnp.bfloat16), SHARD, scatter_dimension=0, tiled=True
        ).astype(jnp.float32),
        lax.psum_scatter(
            query_term.astype(jnp.bfloat16), SHARD, scatter_dimension=0, tiled=True
        ).astype(jnp.float32),
        lax.psum_scatter(
            key_term.astype(jnp.bfloat16), SHARD, scatter_dimension=0, tiled=True
        ).astype(jnp.float32),
        lax.psum_scatter(
            value_term.astype(jnp.bfloat16), SHARD, scatter_dimension=0, tiled=True
        ).astype(jnp.float32),
        lax.psum_scatter(
            output_term.astype(jnp.bfloat16), SHARD, scatter_dimension=0, tiled=True
        ).astype(jnp.float32),
        lax.psum_scatter(
            second_gain_term.astype(jnp.bfloat16), SHARD, scatter_dimension=0, tiled=True
        ).astype(jnp.float32),
        lax.psum_scatter(
            router_term.astype(jnp.bfloat16), SHARD, scatter_dimension=0, tiled=True
        ).astype(jnp.float32),
    )
    mixer_sums = (
        lax.psum(mixer_sums[0].astype(jnp.bfloat16), EXPERT).astype(jnp.float32),
        lax.psum(mixer_sums[1].astype(jnp.bfloat16), EXPERT).astype(jnp.float32),
        lax.psum(mixer_sums[2].astype(jnp.bfloat16), EXPERT).astype(jnp.float32),
        lax.psum(mixer_sums[3].astype(jnp.bfloat16), EXPERT).astype(jnp.float32),
        lax.psum(mixer_sums[4].astype(jnp.bfloat16), EXPERT).astype(jnp.float32),
        lax.psum(mixer_sums[5].astype(jnp.bfloat16), EXPERT).astype(jnp.float32),
        lax.psum(mixer_sums[6].astype(jnp.bfloat16), EXPERT).astype(jnp.float32),
    )
    return (
        output,
        tokens_grad,
        mixer_sums[0],
        mixer_sums[1],
        mixer_sums[2],
        mixer_sums[3],
        mixer_sums[4],
        mixer_sums[5],
        mixer_sums[6],
        gate_up_total,
        down_total,
    )


MESH_IDS = pl.DeviceIdType.MESH


class Place:
    def __init__(self):
        e, s = lax.axis_index(EXPERT), lax.axis_index(SHARD)
        self.y, self.c = lax.div(e, 2), lax.rem(e, 2)
        self.z, self.x = lax.div(s, 2), lax.rem(s, 2)
        self.ox, self.oy, self.oc = 1 - self.x, 1 - self.y, 1 - self.c
        self.to_x = (e, s + 1 - 2 * self.x)
        self.to_y = (e + 2 - 4 * self.y, s)
        self.to_c = (e + 1 - 2 * self.c, s)
        z = self.z
        self.zs = (z, z + 1 - 2 * lax.rem(z, 2), lax.rem(z + 2, 4), 3 - z)
        self.to_z = [None] + [(e, self.zs[d] * 2 + self.x) for d in (1, 2, 3)]


class Sender:
    def __init__(self, send_sem, recv_sem):
        self.send_sem, self.recv_sem, self.started = send_sem, recv_sem, []

    def __call__(self, source, target, device):
        number = len(self.started)
        assert number < self.send_sem.shape[0]
        copy = pltpu.make_async_remote_copy(
            src_ref=source,
            dst_ref=target,
            send_sem=self.send_sem.at[number],
            recv_sem=self.recv_sem.at[number],
            device_id=device,
            device_id_type=MESH_IDS,
        )
        copy.start()
        self.started.append(copy)
        return copy

    def finish(self):
        for copy in self.started:
            copy.wait_send()


def greet(devices):
    barrier = pltpu.get_barrier_semaphore()
    for device in devices:
        pl.semaphore_signal(barrier, inc=1, device_id=device, device_id_type=MESH_IDS)
    pl.semaphore_wait(barrier, len(devices))


def gather_in_plane(place, send, items, beside=lambda: None):
    x, y, c = place.x, place.y, place.c
    ox, oy = place.ox, place.oy
    first = []
    for view, source, ready, own in items:
        for copy in ready:
            copy.wait_recv()
        block = source(y, None)
        by_x = send(block, view(x, y, c, None), place.to_x)
        by_y, back = None, None
        if own:
            back = send(source(oy, 1), view(x, oy, c, 1), place.to_x)
        else:
            by_y = send(block, view(x, y, c, None), place.to_y)
        first.append((by_x, by_y, back))
    result = beside()
    landed = []
    for (view, source, ready, own), (by_x, by_y, back) in zip(items, first):
        if not own:
            landed.append(send(source(y, None), view(x, y, c, None), place.to_c))
        by_x.wait_recv()
        over_y = send(view(ox, y, c, 0), view(ox, y, c, 0), place.to_y)
        landed.append(send(view(ox, y, c, None), view(ox, y, c, None), place.to_c))
        if not own:
            by_y.wait_recv()
            back = send(view(x, oy, c, 1), view(x, oy, c, 1), place.to_x)
            landed.append(send(view(x, oy, c, None), view(x, oy, c, None), place.to_c))
        landed.append((view, over_y, back))
    final = []
    for entry in landed:
        if isinstance(entry, tuple):
            view, over_y, back = entry
            over_y.wait_recv()
            back.wait_recv()
            final.append(send(view(ox, oy, c, None), view(ox, oy, c, None), place.to_c))
        else:
            final.append(entry)
    for copy in final:
        copy.wait_recv()
    return result


def half_rows(half, rows):
    return pl.ds(0, rows) if half is None else pl.ds(half * (rows // 2), rows // 2)


def halves_kernel(first, count, *refs):
    up_ref, down_ref = refs[:2]
    outs, (send_sem, recv_sem, copy_sem) = refs[2 : 2 + count], refs[2 + count :]
    place = Place()
    send = Sender(send_sem, recv_sem)
    greet([place.to_x])
    sent, local = start_halves(place, send, copy_sem, up_ref, down_ref, outs, first)
    for copy in sent:
        copy.wait_recv()
    for copy in local:
        copy.wait()
    send.finish()


def start_halves(place, send, copy_sem, up_ref, down_ref, outs, first):
    x, ox = place.x, place.ox
    half = down_ref.shape[2] // 2
    sent, local = [], []
    for number, out in enumerate(outs):
        expert = first + number

        def pieces(xx):
            at = pl.ds(pl.multiple_of(xx * half, half), half)
            later = pl.ds(pl.multiple_of((xx + 2) * half, half), half)
            return (up_ref.at[expert, :, at], up_ref.at[expert, :, later], down_ref.at[expert, :, at])

        for index, piece in enumerate(pieces(ox)):
            sent.append(send(piece, out.at[x, :, index * half : (index + 1) * half], place.to_x))
        for index, piece in enumerate(pieces(x)):
            copy = pltpu.make_async_copy(
                piece, out.at[x, :, index * half : (index + 1) * half], copy_sem.at[3 * number + index]
            )
            copy.start()
            local.append(copy)
    return sent, local


def exchange_halves(up, down, first, count):
    depth, inner = down.shape[1:]
    return pl.pallas_call(
        functools.partial(halves_kernel, first, count),
        out_shape=(jax.ShapeDtypeStruct((2, depth, 3 * inner // 2), up.dtype),) * count,
        in_specs=[pl.BlockSpec(memory_space=pltpu.VMEM)] * 2,
        out_specs=(pl.BlockSpec(memory_space=pl.ANY),) * count,
        scratch_shapes=[pltpu.SemaphoreType.DMA((3 * count,))] * 3,
        compiler_params=pltpu.CompilerParams(collective_id=4 if first == 0 else 6, has_side_effects=True),
        cost_estimate=pl.CostEstimate(flops=0, bytes_accessed=40_000_000, transcendentals=0),
        name="exchange_halves",
    )(up, down)


def weights_kernel(
    first, count, up_ref, down_ref, w_ref, o_ref, small_ref, rows_ref, w_out, o_out, small_out, rows_out, *refs
):
    outs, (send_sem, recv_sem, copy_sem, half_sem) = refs[:count], refs[count:]
    place = Place()
    send = Sender(send_sem, recv_sem)
    x, y, c, z = place.x, place.y, place.c, place.z
    depth = w_ref.shape[0]
    piece = depth // 4
    blocks = rows_ref.shape[0]
    greet([place.to_x, place.to_y, place.to_c] + place.to_z[1:])

    def columns(ref, yy, cc):
        part = ref.shape[1] // 4
        return pl.ds(pl.multiple_of((yy * 2 + cc) * part, part), part)

    def pieces(yy, cc, half):
        start = (yy * 2 + cc) * piece
        if half is None:
            return pl.ds(pl.multiple_of(start, piece), piece)
        return pl.ds(pl.multiple_of(start + half * (piece // 2), piece // 2), piece // 2)

    wide = [(w_ref, w_out), (o_ref, o_out)]
    from_z = {}
    for d in (1, 2, 3):
        from_z[d] = [
            send(ref.at[:, columns(ref, y, c)], out.at[z, x, :, columns(ref, y, c)], place.to_z[d])
            for ref, out in wide
        ] + [send(small_ref.at[pieces(y, c, None)], small_out.at[z, x, pieces(y, c, None)], place.to_z[d])]
    local = [
        pltpu.make_async_copy(w_ref, w_out.at[z, x], copy_sem.at[0]),
        pltpu.make_async_copy(o_ref, o_out.at[z, x], copy_sem.at[1]),
        pltpu.make_async_copy(small_ref, small_out.at[z, x], copy_sem.at[2]),
        pltpu.make_async_copy(rows_ref, rows_out.at[c, x, y], copy_sem.at[3]),
    ]
    for copy in local:
        copy.start()

    def wide_view(ref, out, zz):
        return lambda xx, yy, cc, half: out.at[zz, xx, half_rows(half, depth), columns(ref, yy, cc)]

    def small_view(zz):
        return lambda xx, yy, cc, half: small_out.at[zz, xx, pieces(yy, cc, half)]

    def rows_view(xx, yy, cc, half):
        return rows_out.at[cc, xx, yy, half_rows(half, blocks)]

    items = [
        (
            wide_view(ref, out, z),
            lambda yy, half, ref=ref: ref.at[half_rows(half, depth), columns(ref, yy, c)],
            [],
            True,
        )
        for ref, out in wide
    ]
    items.append((small_view(z), lambda yy, half: small_ref.at[pieces(yy, c, half)], [], True))
    for d in (1, 2, 3):
        zz = place.zs[d]
        views = [wide_view(ref, out, zz) for ref, out in wide] + [small_view(zz)]
        for view, copy in zip(views, from_z[d]):
            items.append((view, lambda yy, half, view=view: view(x, yy, c, half), [copy], False))
    items.append((rows_view, lambda yy, half: rows_ref.at[half_rows(half, blocks)], [], False))
    sent, kept = gather_in_plane(
        place, send, items, lambda: start_halves(place, send, half_sem, up_ref, down_ref, outs, first)
    )
    for copy in sent:
        copy.wait_recv()
    for copy in local + kept:
        copy.wait()
    send.finish()


def gather_weights(w, o, small, rows, up, down, first):
    depth, inner = down.shape[1:]
    count = up.shape[0] - first
    copies = 128
    arrays = (w, o, small)
    return pl.pallas_call(
        functools.partial(weights_kernel, first, count),
        out_shape=tuple(jax.ShapeDtypeStruct((4, 2) + a.shape, a.dtype) for a in arrays)
        + (jax.ShapeDtypeStruct((2, 2, 2) + rows.shape, rows.dtype),)
        + (jax.ShapeDtypeStruct((2, depth, 3 * inner // 2), up.dtype),) * count,
        in_specs=[pl.BlockSpec(memory_space=pltpu.VMEM)] * 6,
        out_specs=(pl.BlockSpec(memory_space=pl.ANY),) * (4 + count),
        scratch_shapes=[
            pltpu.SemaphoreType.DMA((copies,)),
            pltpu.SemaphoreType.DMA((copies,)),
            pltpu.SemaphoreType.DMA((4,)),
            pltpu.SemaphoreType.DMA((3 * count,)),
        ],
        compiler_params=pltpu.CompilerParams(collective_id=0, has_side_effects=True),
        cost_estimate=pl.CostEstimate(flops=0, bytes_accessed=200_000_000, transcendentals=0),
        name="gather_weights",
    )(up, down, w, o, small, rows)


def rows_kernel(a_ref, b_ref, a_out, b_out, send_sem, recv_sem, copy_sem):
    place = Place()
    send = Sender(send_sem, recv_sem)
    x, y, c = place.x, place.y, place.c
    greet([place.to_x, place.to_y, place.to_c])
    local = [
        pltpu.make_async_copy(a_ref, a_out.at[c, x, y], copy_sem.at[0]),
        pltpu.make_async_copy(b_ref, b_out.at[c, x, y], copy_sem.at[1]),
    ]
    for copy in local:
        copy.start()

    def item(source, out):
        rows = source.shape[0]
        return (
            lambda xx, yy, cc, half: out.at[cc, xx, yy, half_rows(half, rows)],
            lambda yy, half: source.at[half_rows(half, rows)],
            [],
            False,
        )

    gather_in_plane(place, send, [item(b_ref, b_out), item(a_ref, a_out)])
    for copy in local:
        copy.wait()
    send.finish()


def gather_rows(a, b):
    return pl.pallas_call(
        rows_kernel,
        out_shape=(
            jax.ShapeDtypeStruct((2, 2, 2) + a.shape, a.dtype),
            jax.ShapeDtypeStruct((2, 2, 2) + b.shape, b.dtype),
        ),
        in_specs=[pl.BlockSpec(memory_space=pltpu.VMEM)] * 2,
        out_specs=(pl.BlockSpec(memory_space=pl.ANY),) * 2,
        scratch_shapes=[
            pltpu.SemaphoreType.DMA((16,)),
            pltpu.SemaphoreType.DMA((16,)),
            pltpu.SemaphoreType.DMA((2,)),
        ],
        compiler_params=pltpu.CompilerParams(collective_id=1, has_side_effects=True),
        cost_estimate=pl.CostEstimate(flops=0, bytes_accessed=90_000_000, transcendentals=0),
        name="gather_rows",
    )(a, b)


def add_into(target, left, right):
    lead = target.shape[:-2]
    rows = target.shape[-2]
    step = 16 if rows % 16 == 0 else 8
    count = rows // step

    def body(i, carry):
        at = pl.ds(pl.multiple_of(i * step, step), step)
        for index in itertools.product(*(range(n) for n in lead)):
            at_all = index + (at,)
            total = left[at_all].astype(jnp.float32) + right[at_all].astype(jnp.float32)
            target[at_all] = total.astype(target.dtype)
        return carry

    lax.fori_loop(0, count, body, 0)


class Part:
    def __init__(self, take, half, held, from_c, from_first, from_second):
        self.take, self.half, self.held, self.from_c = take, half, held, from_c
        self.from_first, self.from_second = from_first, from_second


def add_in_plane(place, send, parts, finish):
    x, y, c = place.x, place.y, place.c
    ox, oy, oc = place.ox, place.oy, place.oc
    from_core = []
    for part in parts:
        copies = {}
        for dx, dy in ((1, 1), (1, 0), (0, 1), (0, 0)):
            xx, yy = (ox if dx else x), (oy if dy else y)
            copies[dx, dy] = send(part.take(xx, yy, oc), part.from_c.at[xx, yy], place.to_c)
        from_core.append(copies)
    over = []
    for part, copies in zip(parts, from_core):
        for dx, dy in ((1, 1), (1, 0), (0, 1), (0, 0)):
            xx, yy = (ox if dx else x), (oy if dy else y)
            copies[dx, dy].wait_recv()
            add_into(part.held.at[xx, yy], part.take(xx, yy, c), part.from_c.at[xx, yy])
            if (dx, dy) == (1, 1):
                a0 = send(part.half(xx, yy, 0), part.from_first.at[0, 1], place.to_y)
                b0 = send(part.half(xx, yy, 1), part.from_first.at[1, 1], place.to_x)
            elif (dx, dy) == (1, 0):
                b1 = send(part.half(xx, yy, 1), part.from_first.at[1, 0], place.to_x)
            elif (dx, dy) == (0, 1):
                a1 = send(part.half(xx, yy, 0), part.from_first.at[0, 0], place.to_y)
        over.append((a0, b0, a1, b1))
    second = []
    for part, (a0, b0, a1, b1) in zip(parts, over):
        a0.wait_recv()
        add_into(part.half(ox, y, 0), part.half(ox, y, 0), part.from_first.at[0, 1])
        a2 = send(part.half(ox, y, 0), part.from_second.at[0], place.to_x)
        b0.wait_recv()
        add_into(part.half(x, oy, 1), part.half(x, oy, 1), part.from_first.at[1, 1])
        b2 = send(part.half(x, oy, 1), part.from_second.at[1], place.to_y)
        a1.wait_recv()
        add_into(part.half(x, y, 0), part.half(x, y, 0), part.from_first.at[0, 0])
        b1.wait_recv()
        add_into(part.half(x, y, 1), part.half(x, y, 1), part.from_first.at[1, 0])
        second.append((a2, b2))
    results = []
    for number, (part, (a2, b2)) in enumerate(zip(parts, second)):
        a2.wait_recv()
        b2.wait_recv()
        results.append(finish(number, part))
    return results


def combine_kernel(experts, experts_all, first_ref, *refs):
    answer_refs, row_refs, dots_refs = (refs[i * experts : (i + 1) * experts] for i in range(3))
    table_ref, outs, refs = refs[3 * experts], refs[3 * experts + 1 : 3 * experts + 4], refs[3 * experts + 4 :]
    away, held, from_c, from_first, from_second = (refs[3 * i : 3 * i + 3] for i in range(5))
    answer_buf, row_buf, fetch_sem, send_sem, recv_sem = refs[15:]
    place = Place()
    send = Sender(send_sem, recv_sem)
    x, y, c = place.x, place.y, place.c
    ox, oy, oc = place.ox, place.oy, place.oc
    slot_rows = answer_refs[0].shape[1]
    seq_len, width = outs[1].shape
    dot_rows = outs[0].shape[0]
    first = first_ref[0]
    order = []
    for dx, dy in ((1, 1), (1, 0), (0, 1), (0, 0)):
        xx, yy = (ox if dx else x), (oy if dy else y)
        order += [(xx, yy, oc), (xx, yy, c)]

    def fetch(number):
        xx, yy, cc = order[number]
        seq = cc * 4 + xx * 2 + yy
        slot = number % 2
        copies = []
        for expert in range(experts):
            at = slice(expert * slot_rows, (expert + 1) * slot_rows)
            for which, (source, buf) in enumerate(((row_refs, row_buf), (answer_refs, answer_buf))):
                copies.append(
                    pltpu.make_async_copy(
                        source[expert].at[seq], buf.at[slot, at], fetch_sem.at[slot, 2 * expert + which]
                    )
                )
        for copy in copies:
            copy.start()
        return copies

    def compute(number, targets):
        xx, yy, cc = order[number]
        seq = cc * 4 + xx * 2 + yy
        slot = number % 2
        slot_ids = lax.broadcasted_iota(jnp.int32, (slot_rows, seq_len), 0).astype(jnp.float32)
        dot_ids = lax.broadcasted_iota(jnp.int32, (dot_rows, seq_len), 0)
        placings, combines = [], []
        dots = jnp.zeros((dot_rows, seq_len), jnp.float32)
        for expert in range(experts):
            placing = (slot_ids == table_ref[seq, pl.ds(experts_all + first + expert, 1), :]).astype(jnp.float32)
            placings.append(placing)
            combines.append(placing * table_ref[seq, pl.ds(first + expert, 1), :])
            dots = jnp.where(dot_ids == first + expert, dots_refs[expert][seq], dots)
        placing = jnp.concatenate(placings, axis=0).astype(jnp.bfloat16)
        combine = jnp.concatenate(combines, axis=0).astype(jnp.bfloat16)
        targets[0][...] = dots
        down = (((0,), (0,)), ((), ()))
        for left, buf, target in ((placing, row_buf, targets[1]), (combine, answer_buf, targets[2])):
            total = lax.dot_general(left, buf[slot], down, preferred_element_type=jnp.float32)
            target[...] = total.astype(target.dtype)

    heights = [out.shape[0] for out in outs]

    def half(part, xx, yy, which):
        return held[part].at[xx, yy, half_rows(which, heights[part])]

    fetched = {0: fetch(0)}
    greet([place.to_x, place.to_y, place.to_c])
    over = [[] for _ in outs]
    for step in range(4):
        for number in (2 * step, 2 * step + 1):
            xx, yy, cc = order[number]
            if number + 1 < len(order):
                fetched[number + 1] = fetch(number + 1)
            for copy in fetched.pop(number):
                copy.wait()
            if number % 2 == 0:
                compute(number, [ref.at[xx, yy] for ref in away])
                crossed = [
                    send(away[part].at[xx, yy], from_c[part].at[xx, yy], place.to_c) for part in range(3)
                ]
            else:
                compute(number, [ref.at[xx, yy] for ref in held])
        for part in range(3):
            crossed[part].wait_recv()
            add_into(held[part].at[xx, yy], held[part].at[xx, yy], from_c[part].at[xx, yy])
            first_got = from_first[part]
            if step == 0:
                over[part].append(send(half(part, xx, yy, 0), first_got.at[0, 1], place.to_y))
                over[part].append(send(half(part, xx, yy, 1), first_got.at[1, 1], place.to_x))
            elif step == 1:
                over[part].append(send(half(part, xx, yy, 1), first_got.at[1, 0], place.to_x))
            elif step == 2:
                over[part].append(send(half(part, xx, yy, 0), first_got.at[0, 0], place.to_y))
    second = []
    for part in range(3):
        a0, b0, b1, a1 = over[part]
        a0.wait_recv()
        add_into(half(part, ox, y, 0), half(part, ox, y, 0), from_first[part].at[0, 1])
        a2 = send(half(part, ox, y, 0), from_second[part].at[0], place.to_x)
        b0.wait_recv()
        add_into(half(part, x, oy, 1), half(part, x, oy, 1), from_first[part].at[1, 1])
        b2 = send(half(part, x, oy, 1), from_second[part].at[1], place.to_y)
        second.append((a2, b2))
    for part in range(3):
        a0, b0, b1, a1 = over[part]
        a1.wait_recv()
        add_into(half(part, x, y, 0), half(part, x, y, 0), from_first[part].at[0, 0])
        b1.wait_recv()
        add_into(half(part, x, y, 1), half(part, x, y, 1), from_first[part].at[1, 0])
    for part, (a2, b2) in enumerate(second):
        for which, copy in enumerate((a2, b2)):
            copy.wait_recv()
            at = half_rows(which, heights[part])
            add_into(outs[part].at[at], half(part, x, y, which), from_second[part].at[which])
    send.finish()


def combine_rows(first_own, answers, row_grads, dots, table, experts_all):
    experts = len(answers)
    seq_len = table.shape[2]
    _, slot_rows, width = answers[0].shape
    kinds = [
        ((-(-experts_all // 32) * 32, seq_len), jnp.float32),
        ((seq_len, width), jnp.bfloat16),
        ((seq_len, width), jnp.bfloat16),
    ]

    def scratch(lead, cut=1):
        return [pltpu.VMEM(lead + (shape[0] // cut, shape[1]), kind) for shape, kind in kinds]

    return pl.pallas_call(
        functools.partial(combine_kernel, experts, experts_all),
        out_shape=tuple(jax.ShapeDtypeStruct(shape, jnp.float32) for shape, _ in kinds),
        in_specs=[pl.BlockSpec(memory_space=pltpu.SMEM)]
        + [pl.BlockSpec(memory_space=pl.ANY)] * (2 * experts)
        + [pl.BlockSpec(memory_space=pltpu.VMEM)] * (experts + 1),
        out_specs=(pl.BlockSpec(memory_space=pltpu.VMEM),) * 3,
        scratch_shapes=scratch((2, 2))
        + scratch((2, 2))
        + scratch((2, 2))
        + scratch((2, 2), 2)
        + scratch((2,), 2)
        + [pltpu.VMEM((2, experts * slot_rows, width), jnp.bfloat16)] * 2
        + [
            pltpu.SemaphoreType.DMA((2, 2 * experts)),
            pltpu.SemaphoreType.DMA((32,)),
            pltpu.SemaphoreType.DMA((32,)),
        ],
        compiler_params=pltpu.CompilerParams(
            collective_id=2, has_side_effects=True, vmem_limit_bytes=60 * 2**20
        ),
        cost_estimate=pl.CostEstimate(
            flops=32 * seq_len * width * experts * slot_rows, bytes_accessed=150_000_000, transcendentals=0
        ),
        name="combine_rows",
    )(first_own, *answers, *row_grads, *dots, table)


def grads_kernel(count, *refs):
    total_refs, refs = refs[:count], refs[count:]
    ins, refs = refs[:3], refs[3:]
    outs, got_refs, refs = refs[:3], refs[3 : 3 + count], refs[3 + count :]
    held, from_c, from_first, from_second, own, from_z, alls = (refs[3 * i : 3 * i + 3] for i in range(7))
    send_sem, recv_sem = refs[21:]
    place = Place()
    send = Sender(send_sem, recv_sem)
    x, y, c, z = place.x, place.y, place.c, place.z
    greet([place.to_x, place.to_y, place.to_c] + place.to_z[1:])
    depth = ins[1].shape[2]
    piece = depth // 4
    heights = [piece, depth, depth]

    def take(number):
        ref = ins[number]
        if number == 0:
            return lambda xx, yy, cc: ref.at[:, xx, pl.ds(pl.multiple_of((yy * 2 + cc) * piece, piece), piece)]
        wide = ref.shape[3] // 4
        return lambda xx, yy, cc: ref.at[:, xx, :, pl.ds(pl.multiple_of((yy * 2 + cc) * wide, wide), wide)]

    def half_of(number):
        return lambda xx, yy, half: held[number].at[xx, yy, :, half_rows(half, heights[number])]

    parts = [
        Part(take(i), half_of(i), held[i], from_c[i], from_first[i], from_second[i]) for i in range(3)
    ]

    def finish(number, part):
        for half in (0, 1):
            add_into(
                own[number].at[:, half_rows(half, heights[number])],
                part.half(x, y, half),
                part.from_second.at[half],
            )
        return [send(own[number].at[place.zs[d]], from_z[number].at[d - 1], place.to_z[d]) for d in (1, 2, 3)]

    arriving = add_in_plane(place, send, parts, finish)
    swapped = [send(total.at[place.ox], got, place.to_x) for total, got in zip(total_refs, got_refs)]
    spread = []
    for number in range(3):
        mine, arrived = alls[number].at[y, c], from_z[number]
        for copy in arriving[number]:
            copy.wait_recv()
        add_into(arrived.at[0], arrived.at[0], arrived.at[1])
        add_into(arrived.at[2], arrived.at[2], own[number].at[z])
        add_into(mine, arrived.at[0], arrived.at[2])
        over_y = send(mine, mine, place.to_y)
        spread.append((over_y, send(mine, mine, place.to_c)))
    last = []
    for number in range(3):
        over_y, over_c = spread[number]
        over_y.wait_recv()
        other = alls[number].at[place.oy, c]
        last.append((over_c, send(other, other, place.to_c)))
    for number in range(3):
        for copy in last[number]:
            copy.wait_recv()
        for yy, cc in itertools.product((0, 1), (0, 1)):
            if number == 0:
                at = (yy * 2 + cc) * piece
                outs[0][at : at + piece, :] = alls[0][yy, cc]
                continue
            wide = alls[number].shape[3]
            at = (yy * 2 + cc) * wide

            def body(i, carry, number=number, at=at, yy=yy, cc=cc, wide=wide):
                rows = pl.ds(pl.multiple_of(i * 16, 16), 16)
                outs[number][rows, at : at + wide] = alls[number][yy, cc, rows, :].astype(jnp.float32)
                return carry

            lax.fori_loop(0, depth // 16, body, 0)
    for copy in swapped:
        copy.wait_recv()
    send.finish()


def sum_grads(small, output, mixer, totals):
    depth = output.shape[2]
    arrays = (small, output, mixer)
    shapes = [((depth // 4, small.shape[3]), small.dtype)]
    shapes += [((depth, a.shape[3] // 4), a.dtype) for a in arrays[1:]]
    count = len(totals)

    def scratch(lead, cut=1):
        return [pltpu.VMEM(lead + (height // cut, wide), kind) for (height, wide), kind in shapes]

    return pl.pallas_call(
        functools.partial(grads_kernel, count),
        out_shape=tuple(jax.ShapeDtypeStruct(a.shape[2:], jnp.float32) for a in arrays)
        + tuple(jax.ShapeDtypeStruct(t.shape[1:], t.dtype) for t in totals),
        in_specs=[pl.BlockSpec(memory_space=pl.ANY)] * count + [pl.BlockSpec(memory_space=pltpu.VMEM)] * 3,
        out_specs=(pl.BlockSpec(memory_space=pltpu.VMEM),) * 3 + (pl.BlockSpec(memory_space=pl.ANY),) * count,
        scratch_shapes=scratch((2, 2, 4))
        + scratch((2, 2, 4))
        + scratch((2, 2, 4), 2)
        + scratch((2, 4), 2)
        + scratch((4,))
        + scratch((3,))
        + scratch((2, 2))
        + [pltpu.SemaphoreType.DMA((64,)), pltpu.SemaphoreType.DMA((64,))],
        compiler_params=pltpu.CompilerParams(
            collective_id=3, has_side_effects=True, vmem_limit_bytes=60 * 2**20
        ),
        cost_estimate=pl.CostEstimate(flops=0, bytes_accessed=300_000_000, transcendentals=0),
        name="sum_grads",
    )(*totals, *arrays)


def swap_kernel(count, *refs):
    total_refs, got_refs, (send_sem, recv_sem) = refs[:count], refs[count : 2 * count], refs[2 * count :]
    place = Place()
    send = Sender(send_sem, recv_sem)
    greet([place.to_x])
    for total, got in zip(total_refs, got_refs):
        send(total.at[place.ox], got, place.to_x)
    for copy in send.started:
        copy.wait_recv()
    send.finish()


def swap_totals(totals, collective):
    count = len(totals)
    return pl.pallas_call(
        functools.partial(swap_kernel, count),
        out_shape=tuple(jax.ShapeDtypeStruct(t.shape[1:], t.dtype) for t in totals),
        in_specs=[pl.BlockSpec(memory_space=pl.ANY)] * count,
        out_specs=(pl.BlockSpec(memory_space=pl.ANY),) * count,
        scratch_shapes=[pltpu.SemaphoreType.DMA((count,))] * 2,
        compiler_params=pltpu.CompilerParams(collective_id=collective, has_side_effects=True),
        cost_estimate=pl.CostEstimate(flops=0, bytes_accessed=40_000_000, transcendentals=0),
        name="swap_totals",
    )(*totals)


def place_kernel(count, side_ref, *refs):
    kept_refs, got_refs = refs[:count], refs[count : 2 * count]
    up_out, down_out = refs[2 * count :]
    half = down_out.shape[2] // 2
    first = side_ref[0] == 0
    for expert in range(count):
        kept = kept_refs[expert][0].astype(jnp.float32)
        got = got_refs[expert][...].astype(jnp.float32)
        low, high = jnp.where(first, kept, got), jnp.where(first, got, kept)
        for index, part in enumerate((low, high)):
            for group in (0, 1):
                at = (2 * group + index) * half
                up_out[expert, :, at : at + half] = part[:, group * half : (group + 1) * half]
            down_out[expert, :, index * half : (index + 1) * half] = part[:, 2 * half :]


def place_sums(side, totals, got):
    count = len(totals)
    depth, width = got[0].shape
    step = depth // 4
    half = width // 3
    return pl.pallas_call(
        functools.partial(place_kernel, count),
        out_shape=(
            jax.ShapeDtypeStruct((count, depth, 4 * half), jnp.float32),
            jax.ShapeDtypeStruct((count, depth, 2 * half), jnp.float32),
        ),
        grid_spec=pltpu.PrefetchScalarGridSpec(
            num_scalar_prefetch=1,
            grid=(4,),
            in_specs=[pl.BlockSpec((1, step, width), lambda i, side: (side[0], i, 0))] * count
            + [pl.BlockSpec((step, width), lambda i, side: (i, 0))] * count,
            out_specs=(
                pl.BlockSpec((count, step, 4 * half), lambda i, side: (0, i, 0)),
                pl.BlockSpec((count, step, 2 * half), lambda i, side: (0, i, 0)),
            ),
        ),
        cost_estimate=pl.CostEstimate(flops=0, bytes_accessed=9_000_000, transcendentals=0),
        name="place_sums",
    )(side, *totals, *got)


def expert_kernel(
    expert, experts_all, first_ref, table_ref, rows_ref, dout_ref, w_ref, answer_ref, row_ref, w_out, dots_ref,
    total, picked, picked_dout,
):
    group, slot_rows, width = answer_ref.shape
    half = w_ref.shape[1] // 3
    seq_len = rows_ref.shape[1]
    step = pl.program_id(0)
    slot_ids = lax.broadcasted_iota(jnp.int32, (slot_rows, seq_len), 0).astype(jnp.float32)
    gate_parts = []

    def own_row(q, at):
        return table_ref[q, pl.ds(at + first_ref[0] + expert, 1), :]

    for q in range(group):
        placing = (slot_ids == own_row(q, experts_all)).astype(jnp.float32)
        gate_parts.append(jnp.sum(placing * own_row(q, 0), axis=1, keepdims=True))
        low = placing.astype(jnp.bfloat16)
        at = slice(q * slot_rows, (q + 1) * slot_rows)
        picked[at, :] = jnp.dot(low, rows_ref[q], preferred_element_type=jnp.float32).astype(jnp.bfloat16)
        picked_dout[at, :] = jnp.dot(low, dout_ref[q], preferred_element_type=jnp.float32).astype(jnp.bfloat16)
    gate = jnp.concatenate(gate_parts, axis=0)
    both = jnp.dot(picked[...], w_ref[:, : 2 * half], preferred_element_type=jnp.float32)
    gate_part, up_part = both[:, :half], both[:, half:]
    sigmoid = 1.0 / (1.0 + jnp.exp(-gate_part))
    silu = gate_part * sigmoid
    active = (silu * up_part).astype(jnp.bfloat16)
    across = (((1,), (1,)), ((), ()))
    down = (((0,), (0,)), ((), ()))
    answer = lax.dot_general(active, w_ref[:, 2 * half :], across, preferred_element_type=jnp.float32)
    answer = answer.astype(jnp.bfloat16)
    dots = jnp.sum(picked_dout[...].astype(jnp.float32) * answer.astype(jnp.float32), axis=1, keepdims=True)
    for q in range(group):
        at = slice(q * slot_rows, (q + 1) * slot_rows)
        answer_ref[q] = answer[at, :]
        placing = (slot_ids == own_row(q, experts_all)).astype(jnp.float32)
        dots_ref[q] = jnp.sum(placing * dots[at, :], axis=0, keepdims=True)
    picked_dout[...] = (picked_dout[...].astype(jnp.float32) * gate).astype(jnp.bfloat16)
    active_grad = jnp.dot(picked_dout[...], w_ref[:, 2 * half :], preferred_element_type=jnp.float32)
    both_grad = jnp.concatenate(
        [
            active_grad * up_part * sigmoid * (1.0 + gate_part * (1.0 - sigmoid)),
            active_grad * silu,
        ],
        axis=1,
    ).astype(jnp.bfloat16)
    row = lax.dot_general(both_grad, w_ref[:, : 2 * half], across, preferred_element_type=jnp.float32)
    row = row.astype(jnp.bfloat16)
    for q in range(group):
        row_ref[q] = row[q * slot_rows : (q + 1) * slot_rows, :]
    up_term = lax.dot_general(picked[...], both_grad, down, preferred_element_type=jnp.float32)
    down_term = lax.dot_general(picked_dout[...], active, down, preferred_element_type=jnp.float32)

    @pl.when(step == 0)
    def _():
        total[:, : 2 * half] = up_term
        total[:, 2 * half :] = down_term

    @pl.when(step > 0)
    def _():
        total[:, : 2 * half] += up_term
        total[:, 2 * half :] += down_term

    @pl.when(step == pl.num_programs(0) - 1)
    def _():
        w_out[...] = total[...].astype(w_out.dtype)


def run_expert(first_own, table, rows, dout, weights, expert, experts_all, slot_rows):
    count, seq_len, width = rows.shape
    group = count // 2
    wide = weights.shape[1]
    one = pl.BlockSpec((group, 1, seq_len), lambda i: (i, 0, 0))
    listed = pl.BlockSpec((group,) + table.shape[1:], lambda i: (i, 0, 0))
    tall = pl.BlockSpec((group, seq_len, width), lambda i: (i, 0, 0))
    slot = pl.BlockSpec((group, slot_rows, width), lambda i: (i, 0, 0))
    whole = pl.BlockSpec(weights.shape, lambda i: (0, 0))
    flops = 2 * count * slot_rows * width * (2 * seq_len + 3 * wide)
    return pl.pallas_call(
        functools.partial(expert_kernel, expert, experts_all),
        grid=(2,),
        out_shape=(
            jax.ShapeDtypeStruct((count, slot_rows, width), jnp.bfloat16),
            jax.ShapeDtypeStruct((count, slot_rows, width), jnp.bfloat16),
            jax.ShapeDtypeStruct(weights.shape, jnp.bfloat16),
            jax.ShapeDtypeStruct((count, 1, seq_len), jnp.float32),
        ),
        in_specs=[pl.BlockSpec(memory_space=pltpu.SMEM), listed, tall, tall, whole],
        out_specs=(slot, slot, whole, one),
        scratch_shapes=[
            pltpu.VMEM(weights.shape, jnp.float32),
            pltpu.VMEM((group * slot_rows, width), jnp.bfloat16),
            pltpu.VMEM((group * slot_rows, width), jnp.bfloat16),
        ],
        compiler_params=pltpu.CompilerParams(vmem_limit_bytes=60 * 2**20),
        cost_estimate=pl.CostEstimate(flops=flops, bytes_accessed=25_000_000, transcendentals=0),
        name="run_expert",
    )(first_own, table, rows, dout, weights)


def layer_on_device(
    tokens,
    lengths,
    routes,
    cotangent,
    first_gain,
    query_weight,
    key_matrix,
    value_matrix,
    output_weight,
    second_gain,
    router_weight,
    gate_up_weight,
    down_weight,
):
    seq_len, model_width = tokens.shape
    q_heads = query_weight.shape[1] // HEAD_DIM
    kv_heads = key_matrix.shape[1] // HEAD_DIM
    group_size = q_heads // kv_heads
    experts_all = router_weight.shape[1]
    local_experts = gate_up_weight.shape[1]
    inner_width = down_weight.shape[2]
    half_inner = inner_width // 2
    q_width, kv_width = query_weight.shape[1], key_matrix.shape[1]
    slot_count = 8 * max(
        seq_len // 32, (seq_len * routes.shape[1] + 8 * experts_all - 1) // (8 * experts_all)
    )
    score_factor = HEAD_DIM ** (-0.5)
    along_z = [[z * 2 + x for z in range(4)] for x in range(2)]
    expert_at, shard_at = lax.axis_index(EXPERT), lax.axis_index(SHARD)
    x_at = lax.rem(shard_at, 2)
    depth = first_gain.shape[0]

    early = 3
    up_first = gate_up_weight.transpose(1, 0, 2)
    down_first = down_weight.transpose(1, 0, 2)

    def along(halves):
        return lax.all_gather(
            halves.reshape(2 * depth, 3 * half_inner), SHARD, axis=0, tiled=True, axis_index_groups=along_z
        )

    halves = exchange_halves(up_first, down_first, 0, 1)
    expert_weights = [along(halves[0])]
    up_first, down_first, _ = lax.optimization_barrier((up_first, down_first, halves[0]))
    halves = exchange_halves(up_first, down_first, 1, early - 1)
    expert_weights += [along(h) for h in halves]

    position = jnp.arange(seq_len, dtype=jnp.int32)
    length = lengths[0]
    valid_rows = (position < length).astype(jnp.float32)
    dout_full = cotangent.astype(jnp.float32) * valid_rows[:, None]
    dout_low = dout_full.astype(jnp.bfloat16)
    mixer_block = jnp.concatenate([query_weight, key_matrix, value_matrix], axis=1)
    small_block = jnp.concatenate(
        [
            router_weight.astype(jnp.float32),
            first_gain.astype(jnp.float32)[:, None],
            second_gain.astype(jnp.float32)[:, None],
            jnp.zeros((depth, 128 - experts_all - 2), jnp.float32),
        ],
        axis=1,
    )
    mixer_block, output_block, small_block, dout_low = lax.optimization_barrier(
        (mixer_block, output_weight, small_block, dout_low) + tuple(halves)
    )[:4]
    mixer_full, output_full, small_full, dout_plane, *halves = gather_weights(
        mixer_block, output_block, small_block, dout_low, up_first, down_first, early
    )
    expert_weights += [along(h) for h in halves]
    mixer_full = mixer_full.reshape(model_width, mixer_block.shape[1])
    output_full = output_full.reshape(model_width, output_weight.shape[1])
    small_full = small_full.reshape(model_width, 128)
    dout_plane = dout_plane.reshape(8, seq_len, model_width)
    router_full = small_full[:, :experts_all].astype(jnp.bfloat16)
    gain_one, gain_two = small_full[:, experts_all], small_full[:, experts_all + 1]

    cosine, sine_table = rope_tables(seq_len, HEAD_DIM)
    source = tokens.astype(jnp.float32)
    first_scale = lax.rsqrt(jnp.mean(source * source, axis=-1, keepdims=True) + norm_eps)
    first_norm_output = (source * first_scale * gain_one).astype(jnp.bfloat16)
    mixed_in = product("za,ao->zo", first_norm_output, mixer_full)
    queries = rotate(mixed_in[:, :q_width].reshape(seq_len, q_heads, HEAD_DIM), cosine, sine_table)
    queries = queries.astype(jnp.bfloat16).reshape(seq_len, kv_heads, group_size, HEAD_DIM)
    key_row_block = rotate(
        mixed_in[:, q_width : q_width + kv_width].reshape(seq_len, kv_heads, HEAD_DIM), cosine, sine_table
    ).astype(jnp.bfloat16)
    value_row_block = (
        mixed_in[:, q_width + kv_width :].astype(jnp.bfloat16).reshape(seq_len, kv_heads, HEAD_DIM)
    )
    allowed = (position[None, :] <= position[:, None]) & (position[None, :] < length)
    scores = jnp.where(
        allowed, product("qhgd,khd->hgqk", queries, key_row_block) * score_factor, -1e30
    )
    row_max = jnp.max(scores, axis=-1, keepdims=True)
    shifted = jnp.exp(scores - row_max)
    row_total = jnp.sum(shifted, axis=-1, keepdims=True)
    log_total = row_max + jnp.log(row_total)
    probs_low = (shifted / row_total).astype(jnp.bfloat16)
    mixed_heads = (
        product("hgqk,khd->qhgd", probs_low, value_row_block)
        .reshape(seq_len, q_heads * HEAD_DIM)
        .astype(jnp.bfloat16)
    )
    hidden = source + product("sf,df->sd", mixed_heads, output_full)
    second_scale = lax.rsqrt(jnp.mean(hidden * hidden, axis=-1, keepdims=True) + norm_eps)
    second_normed = (hidden * second_scale * gain_two).astype(jnp.bfloat16)
    logits = product("sd,de->se", second_normed, router_full)
    chosen = (routes[:, :, None] == jnp.arange(experts_all, dtype=jnp.int32)).astype(jnp.float32)
    picked = jnp.sum(chosen * logits[:, None, :], axis=-1)
    gate_soft = jax.nn.softmax(picked, axis=-1)
    routed = jnp.sum(chosen, axis=1) * valid_rows[:, None]
    earlier = (position[None, :] < position[:, None]).astype(jnp.bfloat16)
    rank_rows = product("st,te->se", earlier, routed.astype(jnp.bfloat16))
    slot_of = jnp.where(routed > 0, rank_rows, -1.0)
    gate_low = gate_soft.astype(jnp.bfloat16).astype(jnp.float32)
    gate_full = jnp.sum(chosen * gate_low[:, :, None], axis=1)
    listed = -(-2 * experts_all // 16) * 16
    table = jnp.concatenate(
        [gate_full, slot_of, jnp.zeros((seq_len, listed - 2 * experts_all), jnp.float32)], axis=1
    ).T
    rows_plane, table_plane = gather_rows(second_normed, table)
    rows_plane = rows_plane.reshape(8, seq_len, model_width)
    table_plane = table_plane.reshape(8, listed, seq_len)
    first_own = (expert_at * local_experts).astype(jnp.int32).reshape(1)
    slot_rows = -(-slot_count // 16) * 16
    turn, results = first_own, []
    for e in range(local_experts):
        results.append(
            run_expert(turn, table_plane, rows_plane, dout_plane, expert_weights[e], e, experts_all, slot_rows)
        )
        turn = lax.optimization_barrier((first_own, results[-1][3]))[0]
    answers, row_grads, sums, dots = zip(*results)
    sums = lax.optimization_barrier(tuple(sums[:-1])) + (sums[-1],)
    dot_rows, grad_rows, value_rows = combine_rows(
        first_own, answers, row_grads, dots, table_plane, experts_all
    )
    dot_rows = dot_rows.T
    output = (hidden + value_rows).astype(jnp.bfloat16)
    gate_grad = jnp.sum(chosen * dot_rows[:, None, :experts_all], axis=-1)
    inner_sum = jnp.sum(gate_soft * gate_grad, axis=-1, keepdims=True)
    picked_grad = gate_soft * (gate_grad - inner_sum)
    logits_grad = jnp.sum(chosen * picked_grad[:, :, None], axis=1).astype(jnp.bfloat16)
    router_term = product("sd,se->de", second_normed, logits_grad)

    totals = [
        lax.psum_scatter(
            sums[expert], SHARD, scatter_dimension=0, tiled=True, axis_index_groups=along_z
        ).reshape(2, depth, 3 * half_inner)
        for expert in range(local_experts)
    ]

    normed_grad = grad_rows + product("se,de->sd", logits_grad, router_full)
    hidden_grad, second_gain_term = norm_back(normed_grad, hidden, second_scale, gain_two)
    hidden_grad = hidden_grad + dout_full
    attn_grad = hidden_grad.astype(jnp.bfloat16)
    output_term = product("sd,sf->df", attn_grad, mixed_heads)
    mixed_grad = (
        product("za,ao->zo", attn_grad, output_full)
        .astype(jnp.bfloat16)
        .reshape(seq_len, kv_heads, group_size, HEAD_DIM)
    )
    scores_again = jnp.where(
        allowed, product("qhgd,khd->hgqk", queries, key_row_block) * score_factor, -1e30
    )
    probs_again = jnp.exp(scores_again - log_total)
    probs_grad = product("qhgd,khd->hgqk", mixed_grad, value_row_block)
    row_inner = jnp.sum(probs_again * probs_grad, axis=-1, keepdims=True)
    scores_grad = (probs_again * (probs_grad - row_inner)).astype(jnp.bfloat16)
    query_back = product("hgqk,khd->qhgd", scores_grad, key_row_block) * score_factor
    key_back = product("hgqk,qhgd->khd", scores_grad, queries) * score_factor
    value_back = product("hgqk,qhgd->khd", probs_again.astype(jnp.bfloat16), mixed_grad)
    query_pre = (
        unrotate(query_back.reshape(seq_len, q_heads, HEAD_DIM), cosine, sine_table)
        .astype(jnp.bfloat16)
        .reshape(seq_len, q_heads * HEAD_DIM)
    )
    key_pre = (
        unrotate(key_back, cosine, sine_table)
        .astype(jnp.bfloat16)
        .reshape(seq_len, kv_heads * HEAD_DIM)
    )
    value_pre = value_back.astype(jnp.bfloat16).reshape(seq_len, kv_heads * HEAD_DIM)
    mixed_pre = jnp.concatenate([query_pre, key_pre, value_pre], axis=1)
    mixer_term = product("sd,sf->df", first_norm_output, mixed_pre).astype(jnp.bfloat16)
    normed1_grad = product("sf,df->sd", mixed_pre, mixer_full)
    tokens_grad, first_gain_term = norm_back(normed1_grad, source, first_scale, gain_one)
    tokens_grad = tokens_grad + hidden_grad
    small_terms = jnp.concatenate(
        [
            router_term,
            first_gain_term[:, None],
            second_gain_term[:, None],
            jnp.zeros((model_width, 128 - experts_all - 2), jnp.float32),
        ],
        axis=1,
    ).reshape(4, 2, depth, 128)
    swapped = 2
    small_sum, output_sum, mixer_sum, *got = sum_grads(
        small_terms,
        output_term.astype(jnp.bfloat16).reshape(4, 2, depth, output_weight.shape[1]),
        mixer_term.reshape(4, 2, depth, mixer_block.shape[1]),
        totals[:swapped],
    )
    late = lax.optimization_barrier((small_sum,) + tuple(totals[swapped:-1]))[1:]
    got += swap_totals(late, 5)
    last = lax.optimization_barrier((got[-1], totals[-1]))[1:]
    got += swap_totals(last, 7)
    both_sums, down_sums = place_sums(x_at.reshape(1), totals, got)
    return (
        output,
        tokens_grad,
        small_sum[:, experts_all],
        mixer_sum[:, :q_width],
        mixer_sum[:, q_width : q_width + kv_width],
        mixer_sum[:, q_width + kv_width :],
        output_sum,
        small_sum[:, experts_all + 1],
        small_sum[:, :experts_all],
        both_sums.transpose(1, 0, 2),
        down_sums.transpose(1, 0, 2),
    )


def solution(mesh):
    small_slice = mesh.shape[EXPERT] == 4 and mesh.shape[SHARD] == 8
    placed = (
        P((EXPERT, SHARD), None),
        P((EXPERT, SHARD)),
        P((EXPERT, SHARD), None),
        P((EXPERT, SHARD), None),
        P(SHARD),
        P(SHARD, None),
        P(SHARD, None),
        P(SHARD, None),
        P(SHARD, None),
        P(SHARD),
        P(SHARD, None),
        P(SHARD, EXPERT, None),
        P(SHARD, EXPERT, None),
    )
    return jax.shard_map(
        layer_on_device if small_slice else on_device,
        mesh=mesh,
        in_specs=placed,
        out_specs=(
            P((EXPERT, SHARD), None),
            P((EXPERT, SHARD), None),
            P(SHARD),
            P(SHARD, None),
            P(SHARD, None),
            P(SHARD, None),
            P(SHARD, None),
            P(SHARD),
            P(SHARD, None),
            P(SHARD, EXPERT, None),
            P(SHARD, EXPERT, None),
        ),
        check_vma=False,
    )
```

```python
import functools
import itertools

import jax
import jax.numpy as jnp
from jax import lax
from jax.experimental import pallas as pl
from jax.experimental.pallas import tpu as pltpu
from jax.sharding import PartitionSpec as P

HEAD_DIM = 64
EXPERT, SHARD = "expert", "shard"


norm_eps = 1e-06


def product(form, left, right):
    return jnp.einsum(form, left, right, preferred_element_type=jnp.float32)


def rope_tables(row_count, head_width):
    half_width = head_width // 2
    frequency = 10000.0 ** (-(jnp.arange(half_width, dtype=jnp.float32) * (2.0 / head_width)))
    angles = jnp.arange(row_count, dtype=jnp.float32)[:, None] * frequency[None, :]
    return (jnp.cos(angles)[:, None, :], jnp.sin(angles)[:, None, :])


def rotate(values_in, cosine, sine_table):
    half_width = values_in.shape[-1] // 2
    first_half = values_in[..., :half_width]
    second_half = values_in[..., half_width:]
    return jnp.concatenate(
        [
            first_half * cosine - second_half * sine_table,
            second_half * cosine + first_half * sine_table,
        ],
        axis=-1,
    )


def unrotate(grad_in, cosine, sine_table):
    half_width = grad_in.shape[-1] // 2
    first_half = grad_in[..., :half_width]
    second_half = grad_in[..., half_width:]
    return jnp.concatenate(
        [
            first_half * cosine + second_half * sine_table,
            second_half * cosine - first_half * sine_table,
        ],
        axis=-1,
    )


def norm_back(upstream, source, inv_scale, gain_vec):
    scaled = upstream * gain_vec
    gain_grad = jnp.sum(upstream * source * inv_scale, axis=0)
    grad_out = inv_scale * (
        scaled - source * inv_scale * inv_scale * jnp.mean(scaled * source, axis=-1, keepdims=True)
    )
    return (grad_out, gain_grad)


def on_device(
    tokens,
    lengths,
    routes,
    cotangent,
    first_gain,
    query_weight,
    key_matrix,
    value_matrix,
    output_weight,
    second_gain,
    router_weight,
    gate_up_weight,
    down_weight,
):
    seq_len, model_width = tokens.shape
    route_width = routes.shape[1]
    q_heads = query_weight.shape[1] // HEAD_DIM
    kv_heads = key_matrix.shape[1] // HEAD_DIM
    group_size = q_heads // kv_heads
    experts_all = router_weight.shape[1]
    local_experts = gate_up_weight.shape[1]
    inner_width = down_weight.shape[2]
    owners = lax.axis_size(EXPERT)
    slot_count = 8 * max(
        seq_len // 32, (seq_len * route_width + 8 * experts_all - 1) // (8 * experts_all)
    )
    score_factor = HEAD_DIM ** (-0.5)
    gain_one, query_full, key_complete, value_complete, output_full, gain_two, router_full = (
        lax.all_gather(first_gain, SHARD, axis=0, tiled=True),
        lax.all_gather(query_weight, SHARD, axis=0, tiled=True),
        lax.all_gather(key_matrix, SHARD, axis=0, tiled=True),
        lax.all_gather(value_matrix, SHARD, axis=0, tiled=True),
        lax.all_gather(output_weight, SHARD, axis=0, tiled=True),
        lax.all_gather(second_gain, SHARD, axis=0, tiled=True),
        lax.all_gather(router_weight, SHARD, axis=0, tiled=True),
    )
    gate_up_full, down_full = (
        lax.all_gather(gate_up_weight, SHARD, axis=0, tiled=True),
        lax.all_gather(down_weight, SHARD, axis=0, tiled=True),
    )
    gain_one = gain_one.astype(jnp.float32)
    gain_two = gain_two.astype(jnp.float32)
    cosine, sine_table = rope_tables(seq_len, HEAD_DIM)
    source = tokens.astype(jnp.float32)
    first_scale = lax.rsqrt(jnp.mean(source * source, axis=-1, keepdims=True) + norm_eps)
    first_norm_output = (source * first_scale * gain_one).astype(jnp.bfloat16)
    queries = rotate(
        product("za,ao->zo", first_norm_output, query_full).reshape(seq_len, q_heads, HEAD_DIM),
        cosine,
        sine_table,
    )
    queries = queries.astype(jnp.bfloat16).reshape(seq_len, kv_heads, group_size, HEAD_DIM)
    key_row_block = rotate(
        product("za,ao->zo", first_norm_output, key_complete).reshape(seq_len, kv_heads, HEAD_DIM),
        cosine,
        sine_table,
    ).astype(jnp.bfloat16)
    value_row_block = (
        product("za,ao->zo", first_norm_output, value_complete)
        .astype(jnp.bfloat16)
        .reshape(seq_len, kv_heads, HEAD_DIM)
    )
    position = jnp.arange(seq_len, dtype=jnp.int32)
    length = lengths[0]
    allowed = (position[None, :] <= position[:, None]) & (position[None, :] < length)
    scores = jnp.where(
        allowed, product("qhgd,khd->hgqk", queries, key_row_block) * score_factor, -1e30
    )
    row_max = jnp.max(scores, axis=-1, keepdims=True)
    shifted = jnp.exp(scores - row_max)
    row_total = jnp.sum(shifted, axis=-1, keepdims=True)
    log_total = row_max + jnp.log(row_total)
    probs_low = (shifted / row_total).astype(jnp.bfloat16)
    mixed_heads = (
        product("hgqk,khd->qhgd", probs_low, value_row_block)
        .reshape(seq_len, q_heads * HEAD_DIM)
        .astype(jnp.bfloat16)
    )
    hidden = source + product("sf,df->sd", mixed_heads, output_full)
    second_scale = lax.rsqrt(jnp.mean(hidden * hidden, axis=-1, keepdims=True) + norm_eps)
    second_normed = (hidden * second_scale * gain_two).astype(jnp.bfloat16)
    logits = product("sd,de->se", second_normed, router_full)
    chosen = (routes[:, :, None] == jnp.arange(experts_all, dtype=jnp.int32)).astype(jnp.float32)
    picked = jnp.sum(chosen * logits[:, None, :], axis=-1)
    gate_soft = jax.nn.softmax(picked, axis=-1)
    valid_rows = (position < length).astype(jnp.float32)
    routed = jnp.sum(chosen, axis=1) * valid_rows[:, None]
    earlier = (position[None, :] < position[:, None]).astype(jnp.bfloat16)
    rank_rows = product("st,te->se", earlier, routed.astype(jnp.bfloat16))
    slot_ids = jnp.arange(slot_count, dtype=jnp.float32)
    placing = (routed.T[:, None, :] * (rank_rows.T[:, None, :] == slot_ids[None, :, None])).astype(
        jnp.bfloat16
    )
    outgoing = (
        product("ems,sd->emd", placing, second_normed)
        .astype(jnp.bfloat16)
        .reshape(owners, local_experts, slot_count, model_width)
    )
    row_block = lax.all_to_all(outgoing, EXPERT, split_axis=0, concat_axis=0, tiled=True)
    both_pre = product("oemd,def->oemf", row_block, gate_up_full)
    active = (jax.nn.silu(both_pre[..., :inner_width]) * both_pre[..., inner_width:]).astype(
        jnp.bfloat16
    )
    answer = product("oemf,def->oemd", active, down_full).astype(jnp.bfloat16)
    returned = lax.all_to_all(answer, EXPERT, split_axis=0, concat_axis=0, tiled=True).reshape(
        experts_all, slot_count, model_width
    )
    gate_full = product("ske,sk->se", chosen.astype(jnp.bfloat16), gate_soft.astype(jnp.bfloat16))
    placing_float = placing.astype(jnp.float32)
    combine = (placing_float * gate_full.T[:, None, :]).astype(jnp.bfloat16)
    output = (hidden + product("ems,emd->sd", combine, returned)).astype(jnp.bfloat16)
    dout_full = cotangent.astype(jnp.float32) * valid_rows[:, None]
    dout_low = dout_full.astype(jnp.bfloat16)
    grad_rows = (
        product("ems,sd->emd", combine, dout_low)
        .astype(jnp.bfloat16)
        .reshape(owners, local_experts, slot_count, model_width)
    )
    incoming = lax.all_to_all(grad_rows, EXPERT, split_axis=0, concat_axis=0, tiled=True)
    answer_dot = product("emd,sd->ems", returned, dout_low)
    gate_grad_full = jnp.sum(placing_float * answer_dot, axis=1)
    gate_grad = jnp.sum(chosen * gate_grad_full.T[:, None, :], axis=-1)
    inner_sum = jnp.sum(gate_soft * gate_grad, axis=-1, keepdims=True)
    picked_grad = gate_soft * (gate_grad - inner_sum)
    logits_grad = jnp.sum(chosen * picked_grad[:, :, None], axis=1).astype(jnp.bfloat16)
    router_term = product("sd,se->de", second_normed, logits_grad)
    gate_up_full, down_full = (
        lax.all_gather(gate_up_weight, SHARD, axis=0, tiled=True),
        lax.all_gather(down_weight, SHARD, axis=0, tiled=True),
    )
    gate_part = both_pre[..., :inner_width]
    up_part = both_pre[..., inner_width:]
    sigmoid_gate = jax.nn.sigmoid(gate_part)
    silu_gate = gate_part * sigmoid_gate
    active_again = (silu_gate * up_part).astype(jnp.bfloat16)
    active_grad = product("oemd,def->oemf", incoming, down_full)
    both_grad = jnp.concatenate(
        [
            active_grad * up_part * sigmoid_gate * (1.0 + gate_part * (1.0 - sigmoid_gate)),
            active_grad * silu_gate,
        ],
        axis=-1,
    ).astype(jnp.bfloat16)
    row_grad = product("oemf,def->oemd", both_grad, gate_up_full).astype(jnp.bfloat16)
    gate_up_term = product("oemd,oemf->def", row_block, both_grad)
    down_term = product("oemd,oemf->def", incoming, active_again)
    back_rows = lax.all_to_all(row_grad, EXPERT, split_axis=0, concat_axis=0, tiled=True).reshape(
        experts_all, slot_count, model_width
    )
    gate_up_total, down_total = (
        lax.psum_scatter(
            gate_up_term.astype(jnp.bfloat16), SHARD, scatter_dimension=0, tiled=True
        ).astype(jnp.float32),
        lax.psum_scatter(
            down_term.astype(jnp.bfloat16), SHARD, scatter_dimension=0, tiled=True
        ).astype(jnp.float32),
    )
    normed_grad = product("ems,emd->sd", placing, back_rows) + product(
        "se,de->sd", logits_grad, router_full
    )
    hidden_grad, second_gain_term = norm_back(normed_grad, hidden, second_scale, gain_two)
    hidden_grad = hidden_grad + dout_full
    attn_grad = hidden_grad.astype(jnp.bfloat16)
    output_term = product("sd,sf->df", attn_grad, mixed_heads)
    mixed_grad = (
        product("za,ao->zo", attn_grad, output_full)
        .astype(jnp.bfloat16)
        .reshape(seq_len, kv_heads, group_size, HEAD_DIM)
    )
    scores_again = jnp.where(
        allowed, product("qhgd,khd->hgqk", queries, key_row_block) * score_factor, -1e30
    )
    probs_again = jnp.exp(scores_again - log_total)
    probs_grad = product("qhgd,khd->hgqk", mixed_grad, value_row_block)
    row_inner = jnp.sum(probs_again * probs_grad, axis=-1, keepdims=True)
    scores_grad = (probs_again * (probs_grad - row_inner)).astype(jnp.bfloat16)
    query_back = product("hgqk,khd->qhgd", scores_grad, key_row_block) * score_factor
    key_back = product("hgqk,qhgd->khd", scores_grad, queries) * score_factor
    value_back = product("hgqk,qhgd->khd", probs_again.astype(jnp.bfloat16), mixed_grad)
    query_pre = (
        unrotate(query_back.reshape(seq_len, q_heads, HEAD_DIM), cosine, sine_table)
        .astype(jnp.bfloat16)
        .reshape(seq_len, q_heads * HEAD_DIM)
    )
    key_pre = (
        unrotate(key_back, cosine, sine_table)
        .astype(jnp.bfloat16)
        .reshape(seq_len, kv_heads * HEAD_DIM)
    )
    value_pre = value_back.astype(jnp.bfloat16).reshape(seq_len, kv_heads * HEAD_DIM)
    query_term = product("sd,sf->df", first_norm_output, query_pre)
    key_term = product("sd,sf->df", first_norm_output, key_pre)
    value_term = product("sd,sf->df", first_norm_output, value_pre)
    normed1_grad = (
        product("sf,df->sd", query_pre, query_full)
        + product("sf,df->sd", key_pre, key_complete)
        + product("sf,df->sd", value_pre, value_complete)
    )
    tokens_grad, first_gain_term = norm_back(normed1_grad, source, first_scale, gain_one)
    tokens_grad = tokens_grad + hidden_grad
    mixer_sums = (
        lax.psum_scatter(
            first_gain_term.astype(jnp.bfloat16), SHARD, scatter_dimension=0, tiled=True
        ).astype(jnp.float32),
        lax.psum_scatter(
            query_term.astype(jnp.bfloat16), SHARD, scatter_dimension=0, tiled=True
        ).astype(jnp.float32),
        lax.psum_scatter(
            key_term.astype(jnp.bfloat16), SHARD, scatter_dimension=0, tiled=True
        ).astype(jnp.float32),
        lax.psum_scatter(
            value_term.astype(jnp.bfloat16), SHARD, scatter_dimension=0, tiled=True
        ).astype(jnp.float32),
        lax.psum_scatter(
            output_term.astype(jnp.bfloat16), SHARD, scatter_dimension=0, tiled=True
        ).astype(jnp.float32),
        lax.psum_scatter(
            second_gain_term.astype(jnp.bfloat16), SHARD, scatter_dimension=0, tiled=True
        ).astype(jnp.float32),
        lax.psum_scatter(
            router_term.astype(jnp.bfloat16), SHARD, scatter_dimension=0, tiled=True
        ).astype(jnp.float32),
    )
    mixer_sums = (
        lax.psum(mixer_sums[0].astype(jnp.bfloat16), EXPERT).astype(jnp.float32),
        lax.psum(mixer_sums[1].astype(jnp.bfloat16), EXPERT).astype(jnp.float32),
        lax.psum(mixer_sums[2].astype(jnp.bfloat16), EXPERT).astype(jnp.float32),
        lax.psum(mixer_sums[3].astype(jnp.bfloat16), EXPERT).astype(jnp.float32),
        lax.psum(mixer_sums[4].astype(jnp.bfloat16), EXPERT).astype(jnp.float32),
        lax.psum(mixer_sums[5].astype(jnp.bfloat16), EXPERT).astype(jnp.float32),
        lax.psum(mixer_sums[6].astype(jnp.bfloat16), EXPERT).astype(jnp.float32),
    )
    return (
        output,
        tokens_grad,
        mixer_sums[0],
        mixer_sums[1],
        mixer_sums[2],
        mixer_sums[3],
        mixer_sums[4],
        mixer_sums[5],
        mixer_sums[6],
        gate_up_total,
        down_total,
    )


MESH_IDS = pl.DeviceIdType.MESH


class Place:
    def __init__(self):
        e, s = lax.axis_index(EXPERT), lax.axis_index(SHARD)
        self.y, self.c = lax.div(e, 2), lax.rem(e, 2)
        self.z, self.x = lax.div(s, 2), lax.rem(s, 2)
        self.ox, self.oy, self.oc = 1 - self.x, 1 - self.y, 1 - self.c
        self.to_x = (e, s + 1 - 2 * self.x)
        self.to_y = (e + 2 - 4 * self.y, s)
        self.to_c = (e + 1 - 2 * self.c, s)
        z = self.z
        self.zs = (z, z + 1 - 2 * lax.rem(z, 2), lax.rem(z + 2, 4), 3 - z)
        self.to_z = [None] + [(e, self.zs[d] * 2 + self.x) for d in (1, 2, 3)]


class Sender:
    def __init__(self, send_sem, recv_sem):
        self.send_sem, self.recv_sem, self.started = send_sem, recv_sem, []

    def __call__(self, source, target, device):
        number = len(self.started)
        assert number < self.send_sem.shape[0]
        copy = pltpu.make_async_remote_copy(
            src_ref=source,
            dst_ref=target,
            send_sem=self.send_sem.at[number],
            recv_sem=self.recv_sem.at[number],
            device_id=device,
            device_id_type=MESH_IDS,
        )
        copy.start()
        self.started.append(copy)
        return copy

    def finish(self):
        for copy in self.started:
            copy.wait_send()


def greet(devices):
    barrier = pltpu.get_barrier_semaphore()
    for device in devices:
        pl.semaphore_signal(barrier, inc=1, device_id=device, device_id_type=MESH_IDS)
    pl.semaphore_wait(barrier, len(devices))


def gather_in_plane(place, send, items, beside=lambda: None):
    x, y, c = place.x, place.y, place.c
    ox, oy = place.ox, place.oy
    first = []
    for view, source, ready, own in items:
        for copy in ready:
            copy.wait_recv()
        block = source(y, None)
        by_x = send(block, view(x, y, c, None), place.to_x)
        by_y, back = None, None
        if own:
            back = send(source(oy, 1), view(x, oy, c, 1), place.to_x)
        else:
            by_y = send(block, view(x, y, c, None), place.to_y)
        first.append((by_x, by_y, back))
    result = beside()
    landed = []
    for (view, source, ready, own), (by_x, by_y, back) in zip(items, first):
        if not own:
            landed.append(send(source(y, None), view(x, y, c, None), place.to_c))
        by_x.wait_recv()
        over_y = send(view(ox, y, c, 0), view(ox, y, c, 0), place.to_y)
        landed.append(send(view(ox, y, c, None), view(ox, y, c, None), place.to_c))
        if not own:
            by_y.wait_recv()
            back = send(view(x, oy, c, 1), view(x, oy, c, 1), place.to_x)
            landed.append(send(view(x, oy, c, None), view(x, oy, c, None), place.to_c))
        landed.append((view, over_y, back))
    final = []
    for entry in landed:
        if isinstance(entry, tuple):
            view, over_y, back = entry
            over_y.wait_recv()
            back.wait_recv()
            final.append(send(view(ox, oy, c, None), view(ox, oy, c, None), place.to_c))
        else:
            final.append(entry)
    for copy in final:
        copy.wait_recv()
    return result


def half_rows(half, rows):
    return pl.ds(0, rows) if half is None else pl.ds(half * (rows // 2), rows // 2)


def halves_kernel(first, *refs):
    up_ref, down_ref, out, send_sem, recv_sem, copy_sem = refs
    place = Place()
    send = Sender(send_sem, recv_sem)
    greet([place.to_x])
    sent, local = start_halves(place, send, copy_sem, up_ref, down_ref, out, first)
    for copy in sent:
        copy.wait_recv()
    for copy in local:
        copy.wait()
    send.finish()


def start_halves(place, send, copy_sem, up_ref, down_ref, out_ref, first):
    x, ox = place.x, place.ox
    half = down_ref.shape[2] // 2
    sent, local = [], []
    for number in range(out_ref.shape[0]):
        out, expert = out_ref.at[number], first + number

        def pieces(xx):
            at = pl.ds(pl.multiple_of(xx * half, half), half)
            later = pl.ds(pl.multiple_of((xx + 2) * half, half), half)
            return (up_ref.at[expert, :, at], up_ref.at[expert, :, later], down_ref.at[expert, :, at])

        for index, piece in enumerate(pieces(ox)):
            sent.append(send(piece, out.at[x, :, index * half : (index + 1) * half], place.to_x))
        for index, piece in enumerate(pieces(x)):
            copy = pltpu.make_async_copy(
                piece, out.at[x, :, index * half : (index + 1) * half], copy_sem.at[3 * number + index]
            )
            copy.start()
            local.append(copy)
    return sent, local


def exchange_halves(up, down, first, count):
    depth, inner = down.shape[1:]
    return pl.pallas_call(
        functools.partial(halves_kernel, first),
        out_shape=jax.ShapeDtypeStruct((count, 2, depth, 3 * inner // 2), up.dtype),
        in_specs=[pl.BlockSpec(memory_space=pltpu.VMEM)] * 2,
        out_specs=pl.BlockSpec(memory_space=pl.ANY),
        scratch_shapes=[pltpu.SemaphoreType.DMA((3 * count,))] * 3,
        compiler_params=pltpu.CompilerParams(collective_id=4 if first == 0 else 6, has_side_effects=True),
        cost_estimate=pl.CostEstimate(flops=0, bytes_accessed=40_000_000, transcendentals=0),
        name="exchange_halves",
    )(up, down)


def weights_kernel(
    first, up_ref, down_ref, w_ref, o_ref, small_ref, rows_ref, w_out, o_out, small_out, rows_out, halves_out,
    send_sem, recv_sem, copy_sem, half_sem,
):
    place = Place()
    send = Sender(send_sem, recv_sem)
    x, y, c, z = place.x, place.y, place.c, place.z
    depth = w_ref.shape[0]
    piece = depth // 4
    blocks = rows_ref.shape[0]
    greet([place.to_x, place.to_y, place.to_c] + place.to_z[1:])

    def columns(ref, yy, cc):
        part = ref.shape[1] // 4
        return pl.ds(pl.multiple_of((yy * 2 + cc) * part, part), part)

    def pieces(yy, cc, half):
        start = (yy * 2 + cc) * piece
        if half is None:
            return pl.ds(pl.multiple_of(start, piece), piece)
        return pl.ds(pl.multiple_of(start + half * (piece // 2), piece // 2), piece // 2)

    wide = [(w_ref, w_out), (o_ref, o_out)]
    from_z = {}
    for d in (1, 2, 3):
        from_z[d] = [
            send(ref.at[:, columns(ref, y, c)], out.at[z, x, :, columns(ref, y, c)], place.to_z[d])
            for ref, out in wide
        ] + [send(small_ref.at[pieces(y, c, None)], small_out.at[z, x, pieces(y, c, None)], place.to_z[d])]
    local = [
        pltpu.make_async_copy(w_ref, w_out.at[z, x], copy_sem.at[0]),
        pltpu.make_async_copy(o_ref, o_out.at[z, x], copy_sem.at[1]),
        pltpu.make_async_copy(small_ref, small_out.at[z, x], copy_sem.at[2]),
        pltpu.make_async_copy(rows_ref, rows_out.at[c, x, y], copy_sem.at[3]),
    ]
    for copy in local:
        copy.start()

    def wide_view(ref, out, zz):
        return lambda xx, yy, cc, half: out.at[zz, xx, half_rows(half, depth), columns(ref, yy, cc)]

    def small_view(zz):
        return lambda xx, yy, cc, half: small_out.at[zz, xx, pieces(yy, cc, half)]

    def rows_view(xx, yy, cc, half):
        return rows_out.at[cc, xx, yy, half_rows(half, blocks)]

    items = [
        (
            wide_view(ref, out, z),
            lambda yy, half, ref=ref: ref.at[half_rows(half, depth), columns(ref, yy, c)],
            [],
            True,
        )
        for ref, out in wide
    ]
    items.append((small_view(z), lambda yy, half: small_ref.at[pieces(yy, c, half)], [], True))
    for d in (1, 2, 3):
        zz = place.zs[d]
        views = [wide_view(ref, out, zz) for ref, out in wide] + [small_view(zz)]
        for view, copy in zip(views, from_z[d]):
            items.append((view, lambda yy, half, view=view: view(x, yy, c, half), [copy], False))
    items.append((rows_view, lambda yy, half: rows_ref.at[half_rows(half, blocks)], [], False))
    sent, kept = gather_in_plane(
        place, send, items, lambda: start_halves(place, send, half_sem, up_ref, down_ref, halves_out, first)
    )
    for copy in sent:
        copy.wait_recv()
    for copy in local + kept:
        copy.wait()
    send.finish()


def gather_weights(w, o, small, rows, up, down, first):
    depth, inner = down.shape[1:]
    count = up.shape[0] - first
    copies = 128
    arrays = (w, o, small)
    return pl.pallas_call(
        functools.partial(weights_kernel, first),
        out_shape=tuple(jax.ShapeDtypeStruct((4, 2) + a.shape, a.dtype) for a in arrays)
        + (jax.ShapeDtypeStruct((2, 2, 2) + rows.shape, rows.dtype),)
        + (jax.ShapeDtypeStruct((count, 2, depth, 3 * inner // 2), up.dtype),),
        in_specs=[pl.BlockSpec(memory_space=pltpu.VMEM)] * 6,
        out_specs=(pl.BlockSpec(memory_space=pl.ANY),) * 5,
        scratch_shapes=[
            pltpu.SemaphoreType.DMA((copies,)),
            pltpu.SemaphoreType.DMA((copies,)),
            pltpu.SemaphoreType.DMA((4,)),
            pltpu.SemaphoreType.DMA((3 * count,)),
        ],
        compiler_params=pltpu.CompilerParams(collective_id=0, has_side_effects=True),
        cost_estimate=pl.CostEstimate(flops=0, bytes_accessed=200_000_000, transcendentals=0),
        name="gather_weights",
    )(up, down, w, o, small, rows)


def rows_kernel(a_ref, b_ref, a_out, b_out, send_sem, recv_sem, copy_sem):
    place = Place()
    send = Sender(send_sem, recv_sem)
    x, y, c = place.x, place.y, place.c
    greet([place.to_x, place.to_y, place.to_c])
    local = [
        pltpu.make_async_copy(a_ref, a_out.at[c, x, y], copy_sem.at[0]),
        pltpu.make_async_copy(b_ref, b_out.at[c, x, y], copy_sem.at[1]),
    ]
    for copy in local:
        copy.start()

    def item(source, out):
        rows = source.shape[0]
        return (
            lambda xx, yy, cc, half: out.at[cc, xx, yy, half_rows(half, rows)],
            lambda yy, half: source.at[half_rows(half, rows)],
            [],
            False,
        )

    gather_in_plane(place, send, [item(b_ref, b_out), item(a_ref, a_out)])
    for copy in local:
        copy.wait()
    send.finish()


def gather_rows(a, b):
    return pl.pallas_call(
        rows_kernel,
        out_shape=(
            jax.ShapeDtypeStruct((2, 2, 2) + a.shape, a.dtype),
            jax.ShapeDtypeStruct((2, 2, 2) + b.shape, b.dtype),
        ),
        in_specs=[pl.BlockSpec(memory_space=pltpu.VMEM)] * 2,
        out_specs=(pl.BlockSpec(memory_space=pl.ANY),) * 2,
        scratch_shapes=[
            pltpu.SemaphoreType.DMA((16,)),
            pltpu.SemaphoreType.DMA((16,)),
            pltpu.SemaphoreType.DMA((2,)),
        ],
        compiler_params=pltpu.CompilerParams(collective_id=1, has_side_effects=True),
        cost_estimate=pl.CostEstimate(flops=0, bytes_accessed=90_000_000, transcendentals=0),
        name="gather_rows",
    )(a, b)


def add_into(target, left, right):
    lead = target.shape[:-2]
    rows = target.shape[-2]
    step = 16 if rows % 16 == 0 else 8
    count = rows // step

    def body(i, carry):
        at = pl.ds(pl.multiple_of(i * step, step), step)
        for index in itertools.product(*(range(n) for n in lead)):
            at_all = index + (at,)
            total = left[at_all].astype(jnp.float32) + right[at_all].astype(jnp.float32)
            target[at_all] = total.astype(target.dtype)
        return carry

    lax.fori_loop(0, count, body, 0)


def combine_kernel(experts, experts_all, first_ref, *refs):
    answer_refs, row_refs, dots_refs = (refs[i * experts : (i + 1) * experts] for i in range(3))
    table_ref, outs, refs = refs[3 * experts], refs[3 * experts + 1 : 3 * experts + 4], refs[3 * experts + 4 :]
    away, held, from_c, from_first, from_second = (refs[3 * i : 3 * i + 3] for i in range(5))
    answer_buf, row_buf, fetch_sem, send_sem, recv_sem = refs[15:]
    place = Place()
    send = Sender(send_sem, recv_sem)
    x, y, c = place.x, place.y, place.c
    ox, oy, oc = place.ox, place.oy, place.oc
    slot_rows = answer_refs[0].shape[1]
    seq_len, width = outs[1].shape
    dot_rows = outs[0].shape[0]
    first = first_ref[0]
    order = []
    for dx, dy in ((1, 1), (1, 0), (0, 1), (0, 0)):
        xx, yy = (ox if dx else x), (oy if dy else y)
        order += [(xx, yy, oc), (xx, yy, c)]

    def fetch(number):
        xx, yy, cc = order[number]
        seq = cc * 4 + xx * 2 + yy
        slot = number % 2
        copies = []
        for expert in range(experts):
            at = slice(expert * slot_rows, (expert + 1) * slot_rows)
            for which, (source, buf) in enumerate(((row_refs, row_buf), (answer_refs, answer_buf))):
                copies.append(
                    pltpu.make_async_copy(
                        source[expert].at[seq], buf.at[slot, at], fetch_sem.at[slot, 2 * expert + which]
                    )
                )
        for copy in copies:
            copy.start()
        return copies

    def compute(number, targets):
        xx, yy, cc = order[number]
        seq = cc * 4 + xx * 2 + yy
        slot = number % 2
        slot_ids = lax.broadcasted_iota(jnp.int32, (slot_rows, seq_len), 0).astype(jnp.float32)
        dot_ids = lax.broadcasted_iota(jnp.int32, (dot_rows, seq_len), 0)
        placings, combines = [], []
        dots = jnp.zeros((dot_rows, seq_len), jnp.float32)
        for expert in range(experts):
            placing = (slot_ids == table_ref[seq, pl.ds(experts_all + first + expert, 1), :]).astype(jnp.float32)
            placings.append(placing)
            combines.append(placing * table_ref[seq, pl.ds(first + expert, 1), :])
            dots = jnp.where(dot_ids == first + expert, dots_refs[expert][seq], dots)
        placing = jnp.concatenate(placings, axis=0).astype(jnp.bfloat16)
        combine = jnp.concatenate(combines, axis=0).astype(jnp.bfloat16)
        targets[0][...] = dots
        down = (((0,), (0,)), ((), ()))
        for left, buf, target in ((placing, row_buf, targets[1]), (combine, answer_buf, targets[2])):
            total = lax.dot_general(left, buf[slot], down, preferred_element_type=jnp.float32)
            target[...] = total.astype(target.dtype)

    heights = [out.shape[0] for out in outs]

    def half(part, xx, yy, which):
        return held[part].at[xx, yy, half_rows(which, heights[part])]

    fetched = {0: fetch(0)}
    greet([place.to_x, place.to_y, place.to_c])
    over = [[] for _ in outs]
    for step in range(4):
        for number in (2 * step, 2 * step + 1):
            xx, yy, cc = order[number]
            if number + 1 < len(order):
                fetched[number + 1] = fetch(number + 1)
            for copy in fetched.pop(number):
                copy.wait()
            if number % 2 == 0:
                compute(number, [ref.at[xx, yy] for ref in away])
                crossed = [
                    send(away[part].at[xx, yy], from_c[part].at[xx, yy], place.to_c) for part in range(3)
                ]
            else:
                compute(number, [ref.at[xx, yy] for ref in held])
        for part in range(3):
            crossed[part].wait_recv()
            add_into(held[part].at[xx, yy], held[part].at[xx, yy], from_c[part].at[xx, yy])
            first_got = from_first[part]
            if step == 0:
                over[part].append(send(half(part, xx, yy, 0), first_got.at[0, 1], place.to_y))
                over[part].append(send(half(part, xx, yy, 1), first_got.at[1, 1], place.to_x))
            elif step == 1:
                over[part].append(send(half(part, xx, yy, 1), first_got.at[1, 0], place.to_x))
            elif step == 2:
                over[part].append(send(half(part, xx, yy, 0), first_got.at[0, 0], place.to_y))
    second = []
    for part in range(3):
        a0, b0, b1, a1 = over[part]
        a0.wait_recv()
        add_into(half(part, ox, y, 0), half(part, ox, y, 0), from_first[part].at[0, 1])
        a2 = send(half(part, ox, y, 0), from_second[part].at[0], place.to_x)
        b0.wait_recv()
        add_into(half(part, x, oy, 1), half(part, x, oy, 1), from_first[part].at[1, 1])
        b2 = send(half(part, x, oy, 1), from_second[part].at[1], place.to_y)
        second.append((a2, b2))
    for part in range(3):
        a0, b0, b1, a1 = over[part]
        a1.wait_recv()
        add_into(half(part, x, y, 0), half(part, x, y, 0), from_first[part].at[0, 0])
        b1.wait_recv()
        add_into(half(part, x, y, 1), half(part, x, y, 1), from_first[part].at[1, 0])
    for part, (a2, b2) in enumerate(second):
        for which, copy in enumerate((a2, b2)):
            copy.wait_recv()
            at = half_rows(which, heights[part])
            add_into(outs[part].at[at], half(part, x, y, which), from_second[part].at[which])
    send.finish()


def combine_rows(first_own, answers, row_grads, dots, table, experts_all):
    experts = len(answers)
    seq_len = table.shape[2]
    _, slot_rows, width = answers[0].shape
    kinds = [
        ((-(-experts_all // 32) * 32, seq_len), jnp.float32),
        ((seq_len, width), jnp.bfloat16),
        ((seq_len, width), jnp.bfloat16),
    ]

    def scratch(lead, cut=1):
        return [pltpu.VMEM(lead + (shape[0] // cut, shape[1]), kind) for shape, kind in kinds]

    return pl.pallas_call(
        functools.partial(combine_kernel, experts, experts_all),
        out_shape=tuple(jax.ShapeDtypeStruct(shape, jnp.float32) for shape, _ in kinds),
        in_specs=[pl.BlockSpec(memory_space=pltpu.SMEM)]
        + [pl.BlockSpec(memory_space=pl.ANY)] * (2 * experts)
        + [pl.BlockSpec(memory_space=pltpu.VMEM)] * (experts + 1),
        out_specs=(pl.BlockSpec(memory_space=pltpu.VMEM),) * 3,
        scratch_shapes=scratch((2, 2))
        + scratch((2, 2))
        + scratch((2, 2))
        + scratch((2, 2), 2)
        + scratch((2,), 2)
        + [pltpu.VMEM((2, experts * slot_rows, width), jnp.bfloat16)] * 2
        + [
            pltpu.SemaphoreType.DMA((2, 2 * experts)),
            pltpu.SemaphoreType.DMA((32,)),
            pltpu.SemaphoreType.DMA((32,)),
        ],
        compiler_params=pltpu.CompilerParams(
            collective_id=2, has_side_effects=True, vmem_limit_bytes=60 * 2**20
        ),
        cost_estimate=pl.CostEstimate(
            flops=32 * seq_len * width * experts * slot_rows, bytes_accessed=150_000_000, transcendentals=0
        ),
        name="combine_rows",
    )(first_own, *answers, *row_grads, *dots, table)


def grads_kernel(count, cuts, *refs):
    total_refs, refs = refs[:count], refs[count:]
    ins, refs = refs[:3], refs[3:]
    outs, got_refs, refs = refs[:3], refs[3 : 3 + count], refs[3 + count :]
    many = len(cuts)
    held, from_c, from_first, from_second, own, from_z, alls = (refs[many * i : many * (i + 1)] for i in range(7))
    send_sem, recv_sem = refs[7 * many :]
    place = Place()
    send = Sender(send_sem, recv_sem)
    x, y, c, z = place.x, place.y, place.c, place.z
    ox, oy, oc = place.ox, place.oy, place.oc
    greet([place.to_x, place.to_y, place.to_c] + place.to_z[1:])
    depth = ins[1].shape[2]
    piece = depth // 4
    order = [(ox, oy), (ox, y), (x, oy), (x, y)]

    def take(part, xx, yy, cc):
        number, start, wide = cuts[part]
        ref, quarter = ins[number], yy * 2 + cc
        if number == 0:
            return ref.at[:, xx, pl.ds(pl.multiple_of(quarter * piece, piece), piece)]
        at = pl.multiple_of(quarter * (ref.shape[3] // 4) + start, 128)
        return ref.at[:, xx, :, pl.ds(at, wide)]

    def half(part, xx, yy, which):
        return held[part].at[xx, yy, :, half_rows(which, own[part].shape[1])]

    crossed = [
        [send(take(part, xx, yy, oc), from_c[part].at[xx, yy], place.to_c) for xx, yy in order]
        for part in range(many)
    ]
    over, second, arriving, spread, last = {}, {}, {}, {}, {}

    def over_links(part):
        for step, (xx, yy) in enumerate(order):
            crossed[part][step].wait_recv()
            add_into(held[part].at[xx, yy], take(part, xx, yy, c), from_c[part].at[xx, yy])
            got = from_first[part]
            if step == 0:
                a0 = send(half(part, xx, yy, 0), got.at[0, 1], place.to_y)
                b0 = send(half(part, xx, yy, 1), got.at[1, 1], place.to_x)
            elif step == 1:
                b1 = send(half(part, xx, yy, 1), got.at[1, 0], place.to_x)
            elif step == 2:
                a1 = send(half(part, xx, yy, 0), got.at[0, 0], place.to_y)
        over[part] = (a0, b0, a1, b1)

    def over_again(part):
        a0, b0, a1, b1 = over[part]
        got = from_first[part]
        a0.wait_recv()
        add_into(half(part, ox, y, 0), half(part, ox, y, 0), got.at[0, 1])
        a2 = send(half(part, ox, y, 0), from_second[part].at[0], place.to_x)
        b0.wait_recv()
        add_into(half(part, x, oy, 1), half(part, x, oy, 1), got.at[1, 1])
        b2 = send(half(part, x, oy, 1), from_second[part].at[1], place.to_y)
        a1.wait_recv()
        add_into(half(part, x, y, 0), half(part, x, y, 0), got.at[0, 0])
        b1.wait_recv()
        add_into(half(part, x, y, 1), half(part, x, y, 1), got.at[1, 0])
        second[part] = (a2, b2)

    def over_z(part):
        for which, copy in enumerate(second[part]):
            copy.wait_recv()
            at = half_rows(which, own[part].shape[1])
            add_into(own[part].at[:, at], half(part, x, y, which), from_second[part].at[which])
        arriving[part] = [
            send(own[part].at[place.zs[d]], from_z[part].at[d - 1], place.to_z[d]) for d in (1, 2, 3)
        ]

    def back_over_y(part):
        mine, arrived = alls[part].at[y, c], from_z[part]
        for copy in arriving[part]:
            copy.wait_recv()
        add_into(arrived.at[0], arrived.at[0], arrived.at[1])
        add_into(arrived.at[2], arrived.at[2], own[part].at[z])
        add_into(mine, arrived.at[0], arrived.at[2])
        over_y = send(mine, mine, place.to_y)
        spread[part] = (over_y, send(mine, mine, place.to_c))

    def back_over_c(part):
        over_y, over_c = spread[part]
        over_y.wait_recv()
        other = alls[part].at[oy, c]
        last[part] = (over_c, send(other, other, place.to_c))

    def lay_out(part):
        for copy in last[part]:
            copy.wait_recv()
        number, start, wide = cuts[part]
        for yy, cc in itertools.product((0, 1), (0, 1)):
            if number == 0:
                at = (yy * 2 + cc) * piece
                outs[0][at : at + piece, :] = alls[part][yy, cc]
                continue
            at = (yy * 2 + cc) * (ins[number].shape[3] // 4) + start

            def body(i, carry, number=number, at=at, yy=yy, cc=cc, wide=wide):
                rows = pl.ds(pl.multiple_of(i * 16, 16), 16)
                outs[number][rows, at : at + wide] = alls[part][yy, cc, rows, :].astype(jnp.float32)
                return carry

            lax.fori_loop(0, depth // 16, body, 0)

    steps = [(over_links, 0), (over_again, 1), (over_z, 2), (back_over_y, 4), (back_over_c, 5), (lay_out, 6)]
    swapped = []
    for turn in range(many + 6):
        for step, delay in steps:
            if 0 <= turn - delay < many:
                step(turn - delay)
        if turn == many:
            swapped = [send(total.at[:, ox], got, place.to_x) for total, got in zip(total_refs, got_refs)]
    for copy in swapped:
        copy.wait_recv()
    send.finish()


def sum_grads(small, output, mixer, totals):
    depth = output.shape[2]
    arrays = (small, output, mixer)
    wide = mixer.shape[3] // 4
    split = wide * 3 // 5 // 128 * 128
    cuts = [(0, 0, small.shape[3]), (1, 0, output.shape[3] // 4), (2, 0, split), (2, split, wide - split)]
    shapes = [((depth // 4 if number == 0 else depth, width), arrays[number].dtype) for number, _, width in cuts]
    count = len(totals)

    def scratch(lead, cut=1):
        return [pltpu.VMEM(lead + (height // cut, wide), kind) for (height, wide), kind in shapes]

    return pl.pallas_call(
        functools.partial(grads_kernel, count, cuts),
        out_shape=tuple(jax.ShapeDtypeStruct(a.shape[2:], jnp.float32) for a in arrays)
        + tuple(jax.ShapeDtypeStruct(t.shape[:1] + t.shape[2:], t.dtype) for t in totals),
        in_specs=[pl.BlockSpec(memory_space=pl.ANY)] * count + [pl.BlockSpec(memory_space=pltpu.VMEM)] * 3,
        out_specs=(pl.BlockSpec(memory_space=pltpu.VMEM),) * 3 + (pl.BlockSpec(memory_space=pl.ANY),) * count,
        scratch_shapes=scratch((2, 2, 4))
        + scratch((2, 2, 4))
        + scratch((2, 2, 4), 2)
        + scratch((2, 4), 2)
        + scratch((4,))
        + scratch((3,))
        + scratch((2, 2))
        + [pltpu.SemaphoreType.DMA((72,)), pltpu.SemaphoreType.DMA((72,))],
        compiler_params=pltpu.CompilerParams(
            collective_id=3, has_side_effects=True, vmem_limit_bytes=60 * 2**20
        ),
        cost_estimate=pl.CostEstimate(flops=0, bytes_accessed=300_000_000, transcendentals=0),
        name="sum_grads",
    )(*totals, *arrays)


def swap_kernel(count, *refs):
    total_refs, got_refs, (send_sem, recv_sem) = refs[:count], refs[count : 2 * count], refs[2 * count :]
    place = Place()
    send = Sender(send_sem, recv_sem)
    greet([place.to_x])
    for total, got in zip(total_refs, got_refs):
        send(total.at[:, place.ox], got, place.to_x)
    for copy in send.started:
        copy.wait_recv()
    send.finish()


def swap_totals(totals, collective):
    count = len(totals)
    return pl.pallas_call(
        functools.partial(swap_kernel, count),
        out_shape=tuple(jax.ShapeDtypeStruct(t.shape[:1] + t.shape[2:], t.dtype) for t in totals),
        in_specs=[pl.BlockSpec(memory_space=pl.ANY)] * count,
        out_specs=(pl.BlockSpec(memory_space=pl.ANY),) * count,
        scratch_shapes=[pltpu.SemaphoreType.DMA((count,))] * 2,
        compiler_params=pltpu.CompilerParams(collective_id=collective, has_side_effects=True),
        cost_estimate=pl.CostEstimate(flops=0, bytes_accessed=40_000_000, transcendentals=0),
        name="swap_totals",
    )(*totals)


def place_kernel(groups, side_ref, *refs):
    kept_refs, got_refs = refs[:groups], refs[groups : 2 * groups]
    up_out, down_out = refs[2 * groups :]
    half = down_out.shape[2] // 2
    first = side_ref[0] == 0
    experts = [(g, k) for g in range(groups) for k in range(kept_refs[g].shape[0])]
    for expert, (g, k) in enumerate(experts):
        kept = kept_refs[g][k, 0].astype(jnp.float32)
        got = got_refs[g][k].astype(jnp.float32)
        low, high = jnp.where(first, kept, got), jnp.where(first, got, kept)
        for index, part in enumerate((low, high)):
            for group in (0, 1):
                at = (2 * group + index) * half
                up_out[expert, :, at : at + half] = part[:, group * half : (group + 1) * half]
            down_out[expert, :, index * half : (index + 1) * half] = part[:, 2 * half :]


def place_sums(side, totals, got):
    count = sum(g.shape[0] for g in got)
    _, depth, width = got[0].shape
    step = depth // 4
    half = width // 3
    return pl.pallas_call(
        functools.partial(place_kernel, len(got)),
        out_shape=(
            jax.ShapeDtypeStruct((count, depth, 4 * half), jnp.float32),
            jax.ShapeDtypeStruct((count, depth, 2 * half), jnp.float32),
        ),
        grid_spec=pltpu.PrefetchScalarGridSpec(
            num_scalar_prefetch=1,
            grid=(4,),
            in_specs=[
                pl.BlockSpec((t.shape[0], 1, step, width), lambda i, side: (0, side[0], i, 0)) for t in totals
            ]
            + [pl.BlockSpec((g.shape[0], step, width), lambda i, side: (0, i, 0)) for g in got],
            out_specs=(
                pl.BlockSpec((count, step, 4 * half), lambda i, side: (0, i, 0)),
                pl.BlockSpec((count, step, 2 * half), lambda i, side: (0, i, 0)),
            ),
        ),
        cost_estimate=pl.CostEstimate(flops=0, bytes_accessed=9_000_000, transcendentals=0),
        name="place_sums",
    )(side, *totals, *got)


def expert_kernel(
    expert, experts_all, first_ref, table_ref, rows_ref, dout_ref, w_ref, *refs
):
    answer_ref, row_ref, w_out, dots_ref, total, picked, picked_dout = refs[-7:]
    group, slot_rows, width = answer_ref.shape
    half = w_ref.shape[3] // 3

    def weight(columns):
        return w_ref[:, 0, :, columns].reshape(width, -1)

    both_columns, down_columns = slice(0, 2 * half), slice(2 * half, 3 * half)
    seq_len = rows_ref.shape[1]
    step = pl.program_id(0)
    slot_ids = lax.broadcasted_iota(jnp.int32, (slot_rows, seq_len), 0).astype(jnp.float32)
    gate_parts = []

    def own_row(q, at):
        return table_ref[q, pl.ds(at + first_ref[0] + expert, 1), :]

    for q in range(group):
        placing = (slot_ids == own_row(q, experts_all)).astype(jnp.float32)
        gate_parts.append(jnp.sum(placing * own_row(q, 0), axis=1, keepdims=True))
        low = placing.astype(jnp.bfloat16)
        at = slice(q * slot_rows, (q + 1) * slot_rows)
        picked[at, :] = jnp.dot(low, rows_ref[q], preferred_element_type=jnp.float32).astype(jnp.bfloat16)
        picked_dout[at, :] = jnp.dot(low, dout_ref[q], preferred_element_type=jnp.float32).astype(jnp.bfloat16)
    gate = jnp.concatenate(gate_parts, axis=0)
    both = jnp.dot(picked[...], weight(both_columns), preferred_element_type=jnp.float32)
    gate_part, up_part = both[:, :half], both[:, half:]
    sigmoid = 1.0 / (1.0 + jnp.exp(-gate_part))
    silu = gate_part * sigmoid
    active = (silu * up_part).astype(jnp.bfloat16)
    across = (((1,), (1,)), ((), ()))
    down = (((0,), (0,)), ((), ()))
    answer = lax.dot_general(active, weight(down_columns), across, preferred_element_type=jnp.float32)
    answer = answer.astype(jnp.bfloat16)
    dots = jnp.sum(picked_dout[...].astype(jnp.float32) * answer.astype(jnp.float32), axis=1, keepdims=True)
    for q in range(group):
        at = slice(q * slot_rows, (q + 1) * slot_rows)
        answer_ref[q] = answer[at, :]
        placing = (slot_ids == own_row(q, experts_all)).astype(jnp.float32)
        dots_ref[q] = jnp.sum(placing * dots[at, :], axis=0, keepdims=True)
    picked_dout[...] = (picked_dout[...].astype(jnp.float32) * gate).astype(jnp.bfloat16)
    active_grad = jnp.dot(picked_dout[...], weight(down_columns), preferred_element_type=jnp.float32)
    both_grad = jnp.concatenate(
        [
            active_grad * up_part * sigmoid * (1.0 + gate_part * (1.0 - sigmoid)),
            active_grad * silu,
        ],
        axis=1,
    ).astype(jnp.bfloat16)
    row = lax.dot_general(both_grad, weight(both_columns), across, preferred_element_type=jnp.float32)
    row = row.astype(jnp.bfloat16)
    for q in range(group):
        row_ref[q] = row[q * slot_rows : (q + 1) * slot_rows, :]
    up_term = lax.dot_general(picked[...], both_grad, down, preferred_element_type=jnp.float32)
    down_term = lax.dot_general(picked_dout[...], active, down, preferred_element_type=jnp.float32)

    @pl.when(step == 0)
    def _():
        total[:, : 2 * half] = up_term
        total[:, 2 * half :] = down_term

    @pl.when(step > 0)
    def _():
        total[:, : 2 * half] += up_term
        total[:, 2 * half :] += down_term

    @pl.when(step == pl.num_programs(0) - 1)
    def _():
        w_out[...] = total[...].astype(w_out.dtype).reshape(w_out.shape)


def run_expert(first_own, table, rows, dout, weights, expert, experts_all, slot_rows, sums, number, sum_count):
    count, seq_len, width = rows.shape
    group = count // 2
    weights, at = weights
    parts, _, deep, wide = weights.shape
    one = pl.BlockSpec((group, 1, seq_len), lambda i: (i, 0, 0))
    listed = pl.BlockSpec((group,) + table.shape[1:], lambda i: (i, 0, 0))
    tall = pl.BlockSpec((group, seq_len, width), lambda i: (i, 0, 0))
    slot = pl.BlockSpec((group, slot_rows, width), lambda i: (i, 0, 0))
    taken = pl.BlockSpec((parts, 1, deep, wide), lambda i: (0, at, 0, 0))
    given = pl.BlockSpec((parts, 1, deep, wide), lambda i: (0, number, 0, 0))
    flops = 2 * count * slot_rows * width * (2 * seq_len + 3 * wide)
    held = [] if sums is None else [sums]
    return pl.pallas_call(
        functools.partial(expert_kernel, expert, experts_all),
        grid=(2,),
        out_shape=(
            jax.ShapeDtypeStruct((count, slot_rows, width), jnp.bfloat16),
            jax.ShapeDtypeStruct((count, slot_rows, width), jnp.bfloat16),
            jax.ShapeDtypeStruct((parts, sum_count, deep, wide), jnp.bfloat16),
            jax.ShapeDtypeStruct((count, 1, seq_len), jnp.float32),
        ),
        in_specs=[pl.BlockSpec(memory_space=pltpu.SMEM), listed, tall, tall, taken]
        + [pl.BlockSpec(memory_space=pl.ANY)] * len(held),
        out_specs=(slot, slot, given, one),
        scratch_shapes=[
            pltpu.VMEM((parts * deep, wide), jnp.float32),
            pltpu.VMEM((group * slot_rows, width), jnp.bfloat16),
            pltpu.VMEM((group * slot_rows, width), jnp.bfloat16),
        ],
        input_output_aliases={5: 2} if held else {},
        compiler_params=pltpu.CompilerParams(vmem_limit_bytes=60 * 2**20),
        cost_estimate=pl.CostEstimate(flops=flops, bytes_accessed=25_000_000, transcendentals=0),
        name="run_expert",
    )(first_own, table, rows, dout, weights, *held)


def layer_on_device(
    tokens,
    lengths,
    routes,
    cotangent,
    first_gain,
    query_weight,
    key_matrix,
    value_matrix,
    output_weight,
    second_gain,
    router_weight,
    gate_up_weight,
    down_weight,
):
    seq_len, model_width = tokens.shape
    q_heads = query_weight.shape[1] // HEAD_DIM
    kv_heads = key_matrix.shape[1] // HEAD_DIM
    group_size = q_heads // kv_heads
    experts_all = router_weight.shape[1]
    local_experts = gate_up_weight.shape[1]
    inner_width = down_weight.shape[2]
    half_inner = inner_width // 2
    q_width, kv_width = query_weight.shape[1], key_matrix.shape[1]
    slot_count = 8 * max(
        seq_len // 32, (seq_len * routes.shape[1] + 8 * experts_all - 1) // (8 * experts_all)
    )
    score_factor = HEAD_DIM ** (-0.5)
    along_z = [[z * 2 + x for z in range(4)] for x in range(2)]
    expert_at, shard_at = lax.axis_index(EXPERT), lax.axis_index(SHARD)
    x_at = lax.rem(shard_at, 2)
    depth = first_gain.shape[0]

    early = 3
    up_first = gate_up_weight.transpose(1, 0, 2)
    down_first = down_weight.transpose(1, 0, 2)

    def along(halves):
        block = halves.reshape(1, halves.shape[0], 2 * depth, 3 * half_inner)
        return lax.all_gather(block, SHARD, axis=0, tiled=True, axis_index_groups=along_z)

    halves = exchange_halves(up_first, down_first, 0, 1)
    expert_weights = [(along(halves), 0)]
    up_first, down_first, _ = lax.optimization_barrier((up_first, down_first, halves))
    halves = exchange_halves(up_first, down_first, 1, early - 1)
    gathered = along(halves)
    expert_weights += [(gathered, number) for number in range(early - 1)]

    position = jnp.arange(seq_len, dtype=jnp.int32)
    length = lengths[0]
    valid_rows = (position < length).astype(jnp.float32)
    dout_full = cotangent.astype(jnp.float32) * valid_rows[:, None]
    dout_low = dout_full.astype(jnp.bfloat16)
    mixer_block = jnp.concatenate([query_weight, key_matrix, value_matrix], axis=1)
    small_block = jnp.concatenate(
        [
            router_weight.astype(jnp.float32),
            first_gain.astype(jnp.float32)[:, None],
            second_gain.astype(jnp.float32)[:, None],
            jnp.zeros((depth, 128 - experts_all - 2), jnp.float32),
        ],
        axis=1,
    )
    mixer_block, output_block, small_block, dout_low = lax.optimization_barrier(
        (mixer_block, output_weight, small_block, dout_low, halves)
    )[:4]
    mixer_full, output_full, small_full, dout_plane, halves = gather_weights(
        mixer_block, output_block, small_block, dout_low, up_first, down_first, early
    )
    gathered = along(halves)
    expert_weights += [(gathered, number) for number in range(local_experts - early)]
    mixer_full = mixer_full.reshape(model_width, mixer_block.shape[1])
    output_full = output_full.reshape(model_width, output_weight.shape[1])
    small_full = small_full.reshape(model_width, 128)
    dout_plane = dout_plane.reshape(8, seq_len, model_width)
    router_full = small_full[:, :experts_all].astype(jnp.bfloat16)
    gain_one, gain_two = small_full[:, experts_all], small_full[:, experts_all + 1]

    cosine, sine_table = rope_tables(seq_len, HEAD_DIM)
    source = tokens.astype(jnp.float32)
    first_scale = lax.rsqrt(jnp.mean(source * source, axis=-1, keepdims=True) + norm_eps)
    first_norm_output = (source * first_scale * gain_one).astype(jnp.bfloat16)
    mixed_in = product("za,ao->zo", first_norm_output, mixer_full)
    queries = rotate(mixed_in[:, :q_width].reshape(seq_len, q_heads, HEAD_DIM), cosine, sine_table)
    queries = queries.astype(jnp.bfloat16).reshape(seq_len, kv_heads, group_size, HEAD_DIM)
    key_row_block = rotate(
        mixed_in[:, q_width : q_width + kv_width].reshape(seq_len, kv_heads, HEAD_DIM), cosine, sine_table
    ).astype(jnp.bfloat16)
    value_row_block = (
        mixed_in[:, q_width + kv_width :].astype(jnp.bfloat16).reshape(seq_len, kv_heads, HEAD_DIM)
    )
    allowed = (position[None, :] <= position[:, None]) & (position[None, :] < length)
    scores = jnp.where(
        allowed, product("qhgd,khd->hgqk", queries, key_row_block) * score_factor, -1e30
    )
    row_max = jnp.max(scores, axis=-1, keepdims=True)
    shifted = jnp.exp(scores - row_max)
    row_total = jnp.sum(shifted, axis=-1, keepdims=True)
    log_total = row_max + jnp.log(row_total)
    probs_low = (shifted / row_total).astype(jnp.bfloat16)
    mixed_heads = (
        product("hgqk,khd->qhgd", probs_low, value_row_block)
        .reshape(seq_len, q_heads * HEAD_DIM)
        .astype(jnp.bfloat16)
    )
    hidden = source + product("sf,df->sd", mixed_heads, output_full)
    second_scale = lax.rsqrt(jnp.mean(hidden * hidden, axis=-1, keepdims=True) + norm_eps)
    second_normed = (hidden * second_scale * gain_two).astype(jnp.bfloat16)
    logits = product("sd,de->se", second_normed, router_full)
    chosen = (routes[:, :, None] == jnp.arange(experts_all, dtype=jnp.int32)).astype(jnp.float32)
    picked = jnp.sum(chosen * logits[:, None, :], axis=-1)
    gate_soft = jax.nn.softmax(picked, axis=-1)
    routed = jnp.sum(chosen, axis=1) * valid_rows[:, None]
    earlier = (position[None, :] < position[:, None]).astype(jnp.bfloat16)
    rank_rows = product("st,te->se", earlier, routed.astype(jnp.bfloat16))
    slot_of = jnp.where(routed > 0, rank_rows, -1.0)
    gate_low = gate_soft.astype(jnp.bfloat16).astype(jnp.float32)
    gate_full = jnp.sum(chosen * gate_low[:, :, None], axis=1)
    listed = -(-2 * experts_all // 16) * 16
    table = jnp.concatenate(
        [gate_full, slot_of, jnp.zeros((seq_len, listed - 2 * experts_all), jnp.float32)], axis=1
    ).T
    rows_plane, table_plane = gather_rows(second_normed, table)
    rows_plane = rows_plane.reshape(8, seq_len, model_width)
    table_plane = table_plane.reshape(8, listed, seq_len)
    first_own = (expert_at * local_experts).astype(jnp.int32).reshape(1)
    slot_rows = -(-slot_count // 16) * 16
    turn, results, sums = first_own, [], []
    for first, count in ((0, early), (early, local_experts - early)):
        held = None
        for number in range(count):
            e = first + number
            answer, row_grad, held, dot = run_expert(
                turn, table_plane, rows_plane, dout_plane, expert_weights[e], e, experts_all, slot_rows,
                held, number, count,
            )
            results.append((answer, row_grad, dot))
            turn = lax.optimization_barrier((first_own, dot))[0]
        sums.append(held)
    answers, row_grads, dots = zip(*results)
    dot_rows, grad_rows, value_rows = combine_rows(
        first_own, answers, row_grads, dots, table_plane, experts_all
    )
    dot_rows = dot_rows.T
    output = (hidden + value_rows).astype(jnp.bfloat16)
    gate_grad = jnp.sum(chosen * dot_rows[:, None, :experts_all], axis=-1)
    inner_sum = jnp.sum(gate_soft * gate_grad, axis=-1, keepdims=True)
    picked_grad = gate_soft * (gate_grad - inner_sum)
    logits_grad = jnp.sum(chosen * picked_grad[:, :, None], axis=1).astype(jnp.bfloat16)
    router_term = product("sd,se->de", second_normed, logits_grad)

    totals = [
        lax.psum_scatter(
            held, SHARD, scatter_dimension=0, tiled=True, axis_index_groups=along_z
        ).reshape(held.shape[1], 2, depth, 3 * half_inner)
        for held in sums
    ]

    normed_grad = grad_rows + product("se,de->sd", logits_grad, router_full)
    hidden_grad, second_gain_term = norm_back(normed_grad, hidden, second_scale, gain_two)
    hidden_grad = hidden_grad + dout_full
    attn_grad = hidden_grad.astype(jnp.bfloat16)
    output_term = product("sd,sf->df", attn_grad, mixed_heads)
    mixed_grad = (
        product("za,ao->zo", attn_grad, output_full)
        .astype(jnp.bfloat16)
        .reshape(seq_len, kv_heads, group_size, HEAD_DIM)
    )
    scores_again = jnp.where(
        allowed, product("qhgd,khd->hgqk", queries, key_row_block) * score_factor, -1e30
    )
    probs_again = jnp.exp(scores_again - log_total)
    probs_grad = product("qhgd,khd->hgqk", mixed_grad, value_row_block)
    row_inner = jnp.sum(probs_again * probs_grad, axis=-1, keepdims=True)
    scores_grad = (probs_again * (probs_grad - row_inner)).astype(jnp.bfloat16)
    query_back = product("hgqk,khd->qhgd", scores_grad, key_row_block) * score_factor
    key_back = product("hgqk,qhgd->khd", scores_grad, queries) * score_factor
    value_back = product("hgqk,qhgd->khd", probs_again.astype(jnp.bfloat16), mixed_grad)
    query_pre = (
        unrotate(query_back.reshape(seq_len, q_heads, HEAD_DIM), cosine, sine_table)
        .astype(jnp.bfloat16)
        .reshape(seq_len, q_heads * HEAD_DIM)
    )
    key_pre = (
        unrotate(key_back, cosine, sine_table)
        .astype(jnp.bfloat16)
        .reshape(seq_len, kv_heads * HEAD_DIM)
    )
    value_pre = value_back.astype(jnp.bfloat16).reshape(seq_len, kv_heads * HEAD_DIM)
    mixed_pre = jnp.concatenate([query_pre, key_pre, value_pre], axis=1)
    mixer_term = product("sd,sf->df", first_norm_output, mixed_pre).astype(jnp.bfloat16)
    normed1_grad = product("sf,df->sd", mixed_pre, mixer_full)
    tokens_grad, first_gain_term = norm_back(normed1_grad, source, first_scale, gain_one)
    tokens_grad = tokens_grad + hidden_grad
    small_terms = jnp.concatenate(
        [
            router_term,
            first_gain_term[:, None],
            second_gain_term[:, None],
            jnp.zeros((model_width, 128 - experts_all - 2), jnp.float32),
        ],
        axis=1,
    ).reshape(4, 2, depth, 128)
    small_sum, output_sum, mixer_sum, *got = sum_grads(
        small_terms,
        output_term.astype(jnp.bfloat16).reshape(4, 2, depth, output_weight.shape[1]),
        mixer_term.reshape(4, 2, depth, mixer_block.shape[1]),
        totals[:1],
    )
    late = lax.optimization_barrier((small_sum, totals[-1]))[1:]
    got += swap_totals(late, 5)
    both_sums, down_sums = place_sums(x_at.reshape(1), totals, got)
    return (
        output,
        tokens_grad,
        small_sum[:, experts_all],
        mixer_sum[:, :q_width],
        mixer_sum[:, q_width : q_width + kv_width],
        mixer_sum[:, q_width + kv_width :],
        output_sum,
        small_sum[:, experts_all + 1],
        small_sum[:, :experts_all],
        both_sums.transpose(1, 0, 2),
        down_sums.transpose(1, 0, 2),
    )


def solution(mesh):
    small_slice = mesh.shape[EXPERT] == 4 and mesh.shape[SHARD] == 8
    placed = (
        P((EXPERT, SHARD), None),
        P((EXPERT, SHARD)),
        P((EXPERT, SHARD), None),
        P((EXPERT, SHARD), None),
        P(SHARD),
        P(SHARD, None),
        P(SHARD, None),
        P(SHARD, None),
        P(SHARD, None),
        P(SHARD),
        P(SHARD, None),
        P(SHARD, EXPERT, None),
        P(SHARD, EXPERT, None),
    )
    return jax.shard_map(
        layer_on_device if small_slice else on_device,
        mesh=mesh,
        in_specs=placed,
        out_specs=(
            P((EXPERT, SHARD), None),
            P((EXPERT, SHARD), None),
            P(SHARD),
            P(SHARD, None),
            P(SHARD, None),
            P(SHARD, None),
            P(SHARD, None),
            P(SHARD),
            P(SHARD, None),
            P(SHARD, EXPERT, None),
            P(SHARD, EXPERT, None),
        ),
        check_vma=False,
    )
```

```python
import functools
import itertools

import jax
import jax.numpy as jnp
from jax import lax
from jax.experimental import pallas as pl
from jax.experimental.pallas import tpu as pltpu
from jax.sharding import PartitionSpec as P

HEAD_DIM = 64
EXPERT, SHARD = "expert", "shard"


norm_eps = 1e-06


def product(form, left, right):
    return jnp.einsum(form, left, right, preferred_element_type=jnp.float32)


def rope_tables(row_count, head_width):
    half_width = head_width // 2
    frequency = 10000.0 ** (-(jnp.arange(half_width, dtype=jnp.float32) * (2.0 / head_width)))
    angles = jnp.arange(row_count, dtype=jnp.float32)[:, None] * frequency[None, :]
    return (jnp.cos(angles)[:, None, :], jnp.sin(angles)[:, None, :])


def rotate(values_in, cosine, sine_table):
    half_width = values_in.shape[-1] // 2
    first_half = values_in[..., :half_width]
    second_half = values_in[..., half_width:]
    return jnp.concatenate(
        [
            first_half * cosine - second_half * sine_table,
            second_half * cosine + first_half * sine_table,
        ],
        axis=-1,
    )


def unrotate(grad_in, cosine, sine_table):
    half_width = grad_in.shape[-1] // 2
    first_half = grad_in[..., :half_width]
    second_half = grad_in[..., half_width:]
    return jnp.concatenate(
        [
            first_half * cosine + second_half * sine_table,
            second_half * cosine - first_half * sine_table,
        ],
        axis=-1,
    )


def norm_back(upstream, source, inv_scale, gain_vec):
    scaled = upstream * gain_vec
    gain_grad = jnp.sum(upstream * source * inv_scale, axis=0)
    grad_out = inv_scale * (
        scaled - source * inv_scale * inv_scale * jnp.mean(scaled * source, axis=-1, keepdims=True)
    )
    return (grad_out, gain_grad)


def on_device(
    tokens,
    lengths,
    routes,
    cotangent,
    first_gain,
    query_weight,
    key_matrix,
    value_matrix,
    output_weight,
    second_gain,
    router_weight,
    gate_up_weight,
    down_weight,
):
    seq_len, model_width = tokens.shape
    route_width = routes.shape[1]
    q_heads = query_weight.shape[1] // HEAD_DIM
    kv_heads = key_matrix.shape[1] // HEAD_DIM
    group_size = q_heads // kv_heads
    experts_all = router_weight.shape[1]
    local_experts = gate_up_weight.shape[1]
    inner_width = down_weight.shape[2]
    owners = lax.axis_size(EXPERT)
    slot_count = 8 * max(
        seq_len // 32, (seq_len * route_width + 8 * experts_all - 1) // (8 * experts_all)
    )
    score_factor = HEAD_DIM ** (-0.5)
    gain_one, query_full, key_complete, value_complete, output_full, gain_two, router_full = (
        lax.all_gather(first_gain, SHARD, axis=0, tiled=True),
        lax.all_gather(query_weight, SHARD, axis=0, tiled=True),
        lax.all_gather(key_matrix, SHARD, axis=0, tiled=True),
        lax.all_gather(value_matrix, SHARD, axis=0, tiled=True),
        lax.all_gather(output_weight, SHARD, axis=0, tiled=True),
        lax.all_gather(second_gain, SHARD, axis=0, tiled=True),
        lax.all_gather(router_weight, SHARD, axis=0, tiled=True),
    )
    gate_up_full, down_full = (
        lax.all_gather(gate_up_weight, SHARD, axis=0, tiled=True),
        lax.all_gather(down_weight, SHARD, axis=0, tiled=True),
    )
    gain_one = gain_one.astype(jnp.float32)
    gain_two = gain_two.astype(jnp.float32)
    cosine, sine_table = rope_tables(seq_len, HEAD_DIM)
    source = tokens.astype(jnp.float32)
    first_scale = lax.rsqrt(jnp.mean(source * source, axis=-1, keepdims=True) + norm_eps)
    first_norm_output = (source * first_scale * gain_one).astype(jnp.bfloat16)
    queries = rotate(
        product("za,ao->zo", first_norm_output, query_full).reshape(seq_len, q_heads, HEAD_DIM),
        cosine,
        sine_table,
    )
    queries = queries.astype(jnp.bfloat16).reshape(seq_len, kv_heads, group_size, HEAD_DIM)
    key_row_block = rotate(
        product("za,ao->zo", first_norm_output, key_complete).reshape(seq_len, kv_heads, HEAD_DIM),
        cosine,
        sine_table,
    ).astype(jnp.bfloat16)
    value_row_block = (
        product("za,ao->zo", first_norm_output, value_complete)
        .astype(jnp.bfloat16)
        .reshape(seq_len, kv_heads, HEAD_DIM)
    )
    position = jnp.arange(seq_len, dtype=jnp.int32)
    length = lengths[0]
    allowed = (position[None, :] <= position[:, None]) & (position[None, :] < length)
    scores = jnp.where(
        allowed, product("qhgd,khd->hgqk", queries, key_row_block) * score_factor, -1e30
    )
    row_max = jnp.max(scores, axis=-1, keepdims=True)
    shifted = jnp.exp(scores - row_max)
    row_total = jnp.sum(shifted, axis=-1, keepdims=True)
    log_total = row_max + jnp.log(row_total)
    probs_low = (shifted / row_total).astype(jnp.bfloat16)
    mixed_heads = (
        product("hgqk,khd->qhgd", probs_low, value_row_block)
        .reshape(seq_len, q_heads * HEAD_DIM)
        .astype(jnp.bfloat16)
    )
    hidden = source + product("sf,df->sd", mixed_heads, output_full)
    second_scale = lax.rsqrt(jnp.mean(hidden * hidden, axis=-1, keepdims=True) + norm_eps)
    second_normed = (hidden * second_scale * gain_two).astype(jnp.bfloat16)
    logits = product("sd,de->se", second_normed, router_full)
    chosen = (routes[:, :, None] == jnp.arange(experts_all, dtype=jnp.int32)).astype(jnp.float32)
    picked = jnp.sum(chosen * logits[:, None, :], axis=-1)
    gate_soft = jax.nn.softmax(picked, axis=-1)
    valid_rows = (position < length).astype(jnp.float32)
    routed = jnp.sum(chosen, axis=1) * valid_rows[:, None]
    earlier = (position[None, :] < position[:, None]).astype(jnp.bfloat16)
    rank_rows = product("st,te->se", earlier, routed.astype(jnp.bfloat16))
    slot_ids = jnp.arange(slot_count, dtype=jnp.float32)
    placing = (routed.T[:, None, :] * (rank_rows.T[:, None, :] == slot_ids[None, :, None])).astype(
        jnp.bfloat16
    )
    outgoing = (
        product("ems,sd->emd", placing, second_normed)
        .astype(jnp.bfloat16)
        .reshape(owners, local_experts, slot_count, model_width)
    )
    row_block = lax.all_to_all(outgoing, EXPERT, split_axis=0, concat_axis=0, tiled=True)
    both_pre = product("oemd,def->oemf", row_block, gate_up_full)
    active = (jax.nn.silu(both_pre[..., :inner_width]) * both_pre[..., inner_width:]).astype(
        jnp.bfloat16
    )
    answer = product("oemf,def->oemd", active, down_full).astype(jnp.bfloat16)
    returned = lax.all_to_all(answer, EXPERT, split_axis=0, concat_axis=0, tiled=True).reshape(
        experts_all, slot_count, model_width
    )
    gate_full = product("ske,sk->se", chosen.astype(jnp.bfloat16), gate_soft.astype(jnp.bfloat16))
    placing_float = placing.astype(jnp.float32)
    combine = (placing_float * gate_full.T[:, None, :]).astype(jnp.bfloat16)
    output = (hidden + product("ems,emd->sd", combine, returned)).astype(jnp.bfloat16)
    dout_full = cotangent.astype(jnp.float32) * valid_rows[:, None]
    dout_low = dout_full.astype(jnp.bfloat16)
    grad_rows = (
        product("ems,sd->emd", combine, dout_low)
        .astype(jnp.bfloat16)
        .reshape(owners, local_experts, slot_count, model_width)
    )
    incoming = lax.all_to_all(grad_rows, EXPERT, split_axis=0, concat_axis=0, tiled=True)
    answer_dot = product("emd,sd->ems", returned, dout_low)
    gate_grad_full = jnp.sum(placing_float * answer_dot, axis=1)
    gate_grad = jnp.sum(chosen * gate_grad_full.T[:, None, :], axis=-1)
    inner_sum = jnp.sum(gate_soft * gate_grad, axis=-1, keepdims=True)
    picked_grad = gate_soft * (gate_grad - inner_sum)
    logits_grad = jnp.sum(chosen * picked_grad[:, :, None], axis=1).astype(jnp.bfloat16)
    router_term = product("sd,se->de", second_normed, logits_grad)
    gate_up_full, down_full = (
        lax.all_gather(gate_up_weight, SHARD, axis=0, tiled=True),
        lax.all_gather(down_weight, SHARD, axis=0, tiled=True),
    )
    gate_part = both_pre[..., :inner_width]
    up_part = both_pre[..., inner_width:]
    sigmoid_gate = jax.nn.sigmoid(gate_part)
    silu_gate = gate_part * sigmoid_gate
    active_again = (silu_gate * up_part).astype(jnp.bfloat16)
    active_grad = product("oemd,def->oemf", incoming, down_full)
    both_grad = jnp.concatenate(
        [
            active_grad * up_part * sigmoid_gate * (1.0 + gate_part * (1.0 - sigmoid_gate)),
            active_grad * silu_gate,
        ],
        axis=-1,
    ).astype(jnp.bfloat16)
    row_grad = product("oemf,def->oemd", both_grad, gate_up_full).astype(jnp.bfloat16)
    gate_up_term = product("oemd,oemf->def", row_block, both_grad)
    down_term = product("oemd,oemf->def", incoming, active_again)
    back_rows = lax.all_to_all(row_grad, EXPERT, split_axis=0, concat_axis=0, tiled=True).reshape(
        experts_all, slot_count, model_width
    )
    gate_up_total, down_total = (
        lax.psum_scatter(
            gate_up_term.astype(jnp.bfloat16), SHARD, scatter_dimension=0, tiled=True
        ).astype(jnp.float32),
        lax.psum_scatter(
            down_term.astype(jnp.bfloat16), SHARD, scatter_dimension=0, tiled=True
        ).astype(jnp.float32),
    )
    normed_grad = product("ems,emd->sd", placing, back_rows) + product(
        "se,de->sd", logits_grad, router_full
    )
    hidden_grad, second_gain_term = norm_back(normed_grad, hidden, second_scale, gain_two)
    hidden_grad = hidden_grad + dout_full
    attn_grad = hidden_grad.astype(jnp.bfloat16)
    output_term = product("sd,sf->df", attn_grad, mixed_heads)
    mixed_grad = (
        product("za,ao->zo", attn_grad, output_full)
        .astype(jnp.bfloat16)
        .reshape(seq_len, kv_heads, group_size, HEAD_DIM)
    )
    scores_again = jnp.where(
        allowed, product("qhgd,khd->hgqk", queries, key_row_block) * score_factor, -1e30
    )
    probs_again = jnp.exp(scores_again - log_total)
    probs_grad = product("qhgd,khd->hgqk", mixed_grad, value_row_block)
    row_inner = jnp.sum(probs_again * probs_grad, axis=-1, keepdims=True)
    scores_grad = (probs_again * (probs_grad - row_inner)).astype(jnp.bfloat16)
    query_back = product("hgqk,khd->qhgd", scores_grad, key_row_block) * score_factor
    key_back = product("hgqk,qhgd->khd", scores_grad, queries) * score_factor
    value_back = product("hgqk,qhgd->khd", probs_again.astype(jnp.bfloat16), mixed_grad)
    query_pre = (
        unrotate(query_back.reshape(seq_len, q_heads, HEAD_DIM), cosine, sine_table)
        .astype(jnp.bfloat16)
        .reshape(seq_len, q_heads * HEAD_DIM)
    )
    key_pre = (
        unrotate(key_back, cosine, sine_table)
        .astype(jnp.bfloat16)
        .reshape(seq_len, kv_heads * HEAD_DIM)
    )
    value_pre = value_back.astype(jnp.bfloat16).reshape(seq_len, kv_heads * HEAD_DIM)
    query_term = product("sd,sf->df", first_norm_output, query_pre)
    key_term = product("sd,sf->df", first_norm_output, key_pre)
    value_term = product("sd,sf->df", first_norm_output, value_pre)
    normed1_grad = (
        product("sf,df->sd", query_pre, query_full)
        + product("sf,df->sd", key_pre, key_complete)
        + product("sf,df->sd", value_pre, value_complete)
    )
    tokens_grad, first_gain_term = norm_back(normed1_grad, source, first_scale, gain_one)
    tokens_grad = tokens_grad + hidden_grad
    mixer_sums = (
        lax.psum_scatter(
            first_gain_term.astype(jnp.bfloat16), SHARD, scatter_dimension=0, tiled=True
        ).astype(jnp.float32),
        lax.psum_scatter(
            query_term.astype(jnp.bfloat16), SHARD, scatter_dimension=0, tiled=True
        ).astype(jnp.float32),
        lax.psum_scatter(
            key_term.astype(jnp.bfloat16), SHARD, scatter_dimension=0, tiled=True
        ).astype(jnp.float32),
        lax.psum_scatter(
            value_term.astype(jnp.bfloat16), SHARD, scatter_dimension=0, tiled=True
        ).astype(jnp.float32),
        lax.psum_scatter(
            output_term.astype(jnp.bfloat16), SHARD, scatter_dimension=0, tiled=True
        ).astype(jnp.float32),
        lax.psum_scatter(
            second_gain_term.astype(jnp.bfloat16), SHARD, scatter_dimension=0, tiled=True
        ).astype(jnp.float32),
        lax.psum_scatter(
            router_term.astype(jnp.bfloat16), SHARD, scatter_dimension=0, tiled=True
        ).astype(jnp.float32),
    )
    mixer_sums = (
        lax.psum(mixer_sums[0].astype(jnp.bfloat16), EXPERT).astype(jnp.float32),
        lax.psum(mixer_sums[1].astype(jnp.bfloat16), EXPERT).astype(jnp.float32),
        lax.psum(mixer_sums[2].astype(jnp.bfloat16), EXPERT).astype(jnp.float32),
        lax.psum(mixer_sums[3].astype(jnp.bfloat16), EXPERT).astype(jnp.float32),
        lax.psum(mixer_sums[4].astype(jnp.bfloat16), EXPERT).astype(jnp.float32),
        lax.psum(mixer_sums[5].astype(jnp.bfloat16), EXPERT).astype(jnp.float32),
        lax.psum(mixer_sums[6].astype(jnp.bfloat16), EXPERT).astype(jnp.float32),
    )
    return (
        output,
        tokens_grad,
        mixer_sums[0],
        mixer_sums[1],
        mixer_sums[2],
        mixer_sums[3],
        mixer_sums[4],
        mixer_sums[5],
        mixer_sums[6],
        gate_up_total,
        down_total,
    )


MESH_IDS = pl.DeviceIdType.MESH


class Place:
    def __init__(self):
        e, s = lax.axis_index(EXPERT), lax.axis_index(SHARD)
        self.y, self.c = lax.div(e, 2), lax.rem(e, 2)
        self.z, self.x = lax.div(s, 2), lax.rem(s, 2)
        self.ox, self.oy, self.oc = 1 - self.x, 1 - self.y, 1 - self.c
        self.to_x = (e, s + 1 - 2 * self.x)
        self.to_y = (e + 2 - 4 * self.y, s)
        self.to_c = (e + 1 - 2 * self.c, s)
        z = self.z
        self.zs = (z, z + 1 - 2 * lax.rem(z, 2), lax.rem(z + 2, 4), 3 - z)
        self.to_z = [None] + [(e, self.zs[d] * 2 + self.x) for d in (1, 2, 3)]


class Sender:
    def __init__(self, send_sem, recv_sem):
        self.send_sem, self.recv_sem, self.started = send_sem, recv_sem, []

    def __call__(self, source, target, device):
        number = len(self.started)
        assert number < self.send_sem.shape[0]
        copy = pltpu.make_async_remote_copy(
            src_ref=source,
            dst_ref=target,
            send_sem=self.send_sem.at[number],
            recv_sem=self.recv_sem.at[number],
            device_id=device,
            device_id_type=MESH_IDS,
        )
        copy.start()
        self.started.append(copy)
        return copy

    def finish(self):
        for copy in self.started:
            copy.wait_send()


def greet(devices):
    barrier = pltpu.get_barrier_semaphore()
    for device in devices:
        pl.semaphore_signal(barrier, inc=1, device_id=device, device_id_type=MESH_IDS)
    pl.semaphore_wait(barrier, len(devices))


def gather_in_plane(place, send, groups, beside=lambda: None):
    x, y, c = place.x, place.y, place.c
    ox, oy, oc = place.ox, place.oy, place.oc
    first, landed, final = {}, {}, []

    def over_links(number):
        first[number] = []
        for view, source, ready, own in groups[number]:
            ready()
            block = source(y, None)
            by_x = send(block, view(x, y, c, None), place.to_x)
            by_y, back = None, None
            if own:
                back = send(source(oy, 1), view(x, oy, c, 1), place.to_x)
            else:
                by_y = send(block, view(x, y, c, None), place.to_y)
            first[number].append((by_x, by_y, back))

    def over_again(number):
        landed[number] = []
        for (view, source, ready, own), (by_x, by_y, back) in zip(groups[number], first[number]):
            if not own:
                final.append(send(source(y, None), view(x, y, c, None), place.to_c))
            by_x.wait_recv()
            over_y = send(view(ox, y, c, 0), view(ox, y, c, 0), place.to_y)
            final.append(send(view(ox, y, c, None), view(ox, y, c, None), place.to_c))
            if not own:
                by_y.wait_recv()
                back = send(view(x, oy, c, 1), view(x, oy, c, 1), place.to_x)
                final.append(send(view(x, oy, c, None), view(x, oy, c, None), place.to_c))
            landed[number].append((view, over_y, back))

    def over_core(number):
        for view, over_y, back in landed[number]:
            over_y.wait_recv()
            back.wait_recv()
            final.append(send(view(ox, oy, c, None), view(ox, oy, c, None), place.to_c))

    result = None
    for turn in range(len(groups) + 2):
        for delay, step in enumerate((over_links, over_again, over_core)):
            if 0 <= turn - delay < len(groups):
                step(turn - delay)
        if turn == min(1, len(groups) - 1):
            result = beside()
    for copy in final:
        copy.wait_recv()
    return result


def cut_rows(half, rows):
    more = rows * 3 // 4 // 16 * 16
    return pl.ds(0, rows) if half is None else pl.ds(more, rows - more) if half else pl.ds(0, more)


def half_rows(half, rows):
    return pl.ds(0, rows) if half is None else pl.ds(half * (rows // 2), rows // 2)


def halves_kernel(first, *refs):
    up_ref, down_ref, out, send_sem, recv_sem, copy_sem = refs
    place = Place()
    send = Sender(send_sem, recv_sem)
    greet([place.to_x])
    sent, local = start_halves(place, send, copy_sem, up_ref, down_ref, out, first)
    for copy in sent:
        copy.wait_recv()
    for copy in local:
        copy.wait()
    send.finish()


def start_halves(place, send, copy_sem, up_ref, down_ref, out_ref, first, base=0):
    x, ox = place.x, place.ox
    half = down_ref.shape[2] // 2
    sent, local = [], []
    for number in range(out_ref.shape[0]):
        out, expert = out_ref.at[number], first + number

        def pieces(xx):
            at = pl.ds(pl.multiple_of(xx * half, half), half)
            later = pl.ds(pl.multiple_of((xx + 2) * half, half), half)
            return (up_ref.at[expert, :, at], up_ref.at[expert, :, later], down_ref.at[expert, :, at])

        for index, piece in enumerate(pieces(ox)):
            sent.append(send(piece, out.at[x, :, index * half : (index + 1) * half], place.to_x))
        for index, piece in enumerate(pieces(x)):
            copy = pltpu.make_async_copy(
                piece, out.at[x, :, index * half : (index + 1) * half], copy_sem.at[base + 3 * number + index]
            )
            copy.start()
            local.append(copy)
    return sent, local


def exchange_halves(up, down, first, count):
    depth, inner = down.shape[1:]
    return pl.pallas_call(
        functools.partial(halves_kernel, first),
        out_shape=jax.ShapeDtypeStruct((count, 2, depth, 3 * inner // 2), up.dtype),
        in_specs=[pl.BlockSpec(memory_space=pltpu.VMEM)] * 2,
        out_specs=pl.BlockSpec(memory_space=pl.ANY),
        scratch_shapes=[pltpu.SemaphoreType.DMA((3 * count,))] * 3,
        compiler_params=pltpu.CompilerParams(collective_id=4 if first == 0 else 6, has_side_effects=True),
        cost_estimate=pl.CostEstimate(flops=0, bytes_accessed=40_000_000, transcendentals=0),
        name="exchange_halves",
    )(up, down)


def weights_kernel(
    first, up_ref, down_ref, w_ref, o_ref, small_ref, rows_ref, w_out, o_out, small_out, rows_out,
    *refs,
):
    halves_outs, (send_sem, recv_sem, copy_sem, half_sem) = refs[:-4], refs[-4:]
    place = Place()
    send = Sender(send_sem, recv_sem)
    x, y, c, z = place.x, place.y, place.c, place.z
    depth = w_ref.shape[0]
    piece = depth // 4
    blocks = rows_ref.shape[0]
    greet([place.to_x, place.to_y, place.to_c] + place.to_z[1:])

    def columns(ref, yy, cc):
        part = ref.shape[1] // 4
        return pl.ds(pl.multiple_of((yy * 2 + cc) * part, part), part)

    def pieces(yy, cc, half):
        start = (yy * 2 + cc) * piece
        if half is None:
            return pl.ds(pl.multiple_of(start, piece), piece)
        return pl.ds(pl.multiple_of(start + half * (piece // 2), piece // 2), piece // 2)

    wide = [(w_ref, w_out), (o_ref, o_out)]
    from_z = {}
    for d in (2, 1):
        from_z[d] = [
            send(ref.at[:, columns(ref, y, c)], out.at[z, x, :, columns(ref, y, c)], place.to_z[d])
            for ref, out in wide
        ] + [send(small_ref.at[pieces(y, c, None)], small_out.at[z, x, pieces(y, c, None)], place.to_z[d])]
    local = [
        pltpu.make_async_copy(w_ref, w_out.at[z, x], copy_sem.at[0]),
        pltpu.make_async_copy(o_ref, o_out.at[z, x], copy_sem.at[1]),
        pltpu.make_async_copy(small_ref, small_out.at[z, x], copy_sem.at[2]),
        pltpu.make_async_copy(rows_ref, rows_out.at[c, x, y], copy_sem.at[3]),
    ]
    for copy in local:
        copy.start()

    def wide_view(ref, out, zz):
        return lambda xx, yy, cc, half: out.at[zz, xx, cut_rows(half, depth), columns(ref, yy, cc)]

    def small_view(zz):
        return lambda xx, yy, cc, half: small_out.at[zz, xx, pieces(yy, cc, half)]

    def rows_view(xx, yy, cc, half):
        return rows_out.at[cc, xx, yy, cut_rows(half, blocks)]

    items = [
        (
            wide_view(ref, out, z),
            lambda yy, half, ref=ref: ref.at[cut_rows(half, depth), columns(ref, yy, c)],
            lambda: None,
            True,
        )
        for ref, out in wide
    ]
    items.append((small_view(z), lambda yy, half: small_ref.at[pieces(yy, c, half)], lambda: None, True))
    items.append((rows_view, lambda yy, half: rows_ref.at[cut_rows(half, blocks)], lambda: None, False))
    from_z[3] = []

    def arrive(d, number, view):
        from_z[d][number].wait_recv()
        if d == 2:
            block = view(x, y, c, None)
            from_z[3].append(send(block, block, place.to_z[1]))

    groups = [items]
    for d in (1, 2, 3):
        zz = place.zs[d]
        views = [wide_view(ref, out, zz) for ref, out in wide] + [small_view(zz)]
        groups.append(
            [
                (
                    view,
                    lambda yy, half, view=view: view(x, yy, c, half),
                    functools.partial(arrive, d, number, view),
                    False,
                )
                for number, view in enumerate(views)
            ]
        )

    def beside():
        sent, kept, expert = [], [], first
        for out in halves_outs:
            more_sent, more_kept = start_halves(
                place, send, half_sem, up_ref, down_ref, out, expert, 3 * (expert - first)
            )
            sent, kept, expert = sent + more_sent, kept + more_kept, expert + out.shape[0]
        return sent, kept

    sent, kept = gather_in_plane(place, send, groups, beside)
    for copy in sent:
        copy.wait_recv()
    for copy in local + kept:
        copy.wait()
    send.finish()


def gather_weights(w, o, small, rows, up, down, first, counts):
    depth, inner = down.shape[1:]
    count = sum(counts)
    copies = 128
    arrays = (w, o, small)
    return pl.pallas_call(
        functools.partial(weights_kernel, first),
        out_shape=tuple(jax.ShapeDtypeStruct((4, 2) + a.shape, a.dtype) for a in arrays)
        + (jax.ShapeDtypeStruct((2, 2, 2) + rows.shape, rows.dtype),)
        + tuple(jax.ShapeDtypeStruct((n, 2, depth, 3 * inner // 2), up.dtype) for n in counts),
        in_specs=[pl.BlockSpec(memory_space=pltpu.VMEM)] * 6,
        out_specs=(pl.BlockSpec(memory_space=pl.ANY),) * (4 + len(counts)),
        scratch_shapes=[
            pltpu.SemaphoreType.DMA((copies,)),
            pltpu.SemaphoreType.DMA((copies,)),
            pltpu.SemaphoreType.DMA((4,)),
            pltpu.SemaphoreType.DMA((3 * count,)),
        ],
        compiler_params=pltpu.CompilerParams(collective_id=0, has_side_effects=True),
        cost_estimate=pl.CostEstimate(flops=0, bytes_accessed=200_000_000, transcendentals=0),
        name="gather_weights",
    )(up, down, w, o, small, rows)


def rows_kernel(a_ref, b_ref, a_out, b_out, send_sem, recv_sem, copy_sem):
    place = Place()
    send = Sender(send_sem, recv_sem)
    x, y, c = place.x, place.y, place.c
    greet([place.to_x, place.to_y, place.to_c])
    local = [
        pltpu.make_async_copy(a_ref, a_out.at[c, x, y], copy_sem.at[0]),
        pltpu.make_async_copy(b_ref, b_out.at[c, x, y], copy_sem.at[1]),
    ]
    for copy in local:
        copy.start()

    def item(source, out):
        rows = source.shape[0]
        return (
            lambda xx, yy, cc, half: out.at[cc, xx, yy, half_rows(half, rows)],
            lambda yy, half: source.at[half_rows(half, rows)],
            lambda: None,
            False,
        )

    gather_in_plane(place, send, [[item(b_ref, b_out), item(a_ref, a_out)]])
    for copy in local:
        copy.wait()
    send.finish()


def gather_rows(a, b):
    return pl.pallas_call(
        rows_kernel,
        out_shape=(
            jax.ShapeDtypeStruct((2, 2, 2) + a.shape, a.dtype),
            jax.ShapeDtypeStruct((2, 2, 2) + b.shape, b.dtype),
        ),
        in_specs=[pl.BlockSpec(memory_space=pltpu.VMEM)] * 2,
        out_specs=(pl.BlockSpec(memory_space=pl.ANY),) * 2,
        scratch_shapes=[
            pltpu.SemaphoreType.DMA((16,)),
            pltpu.SemaphoreType.DMA((16,)),
            pltpu.SemaphoreType.DMA((2,)),
        ],
        compiler_params=pltpu.CompilerParams(collective_id=1, has_side_effects=True),
        cost_estimate=pl.CostEstimate(flops=0, bytes_accessed=90_000_000, transcendentals=0),
        name="gather_rows",
    )(a, b)


def add_into(target, left, right):
    lead = target.shape[:-2]
    rows = target.shape[-2]
    step = 16 if rows % 16 == 0 else 8
    count = rows // step

    def body(i, carry):
        at = pl.ds(pl.multiple_of(i * step, step), step)
        for index in itertools.product(*(range(n) for n in lead)):
            at_all = index + (at,)
            total = left[at_all].astype(jnp.float32) + right[at_all].astype(jnp.float32)
            target[at_all] = total.astype(target.dtype)
        return carry

    lax.fori_loop(0, count, body, 0)


def combine_kernel(experts, experts_all, first_ref, *refs):
    answer_refs, row_refs, dots_refs = (refs[i * experts : (i + 1) * experts] for i in range(3))
    table_ref, outs, refs = refs[3 * experts], refs[3 * experts + 1 : 3 * experts + 4], refs[3 * experts + 4 :]
    away, held, from_c, from_first, from_second = (refs[3 * i : 3 * i + 3] for i in range(5))
    answer_buf, row_buf, fetch_sem, send_sem, recv_sem = refs[15:]
    place = Place()
    send = Sender(send_sem, recv_sem)
    x, y, c = place.x, place.y, place.c
    ox, oy, oc = place.ox, place.oy, place.oc
    slot_rows = answer_refs[0].shape[1]
    seq_len, width = outs[1].shape
    dot_rows = outs[0].shape[0]
    first = first_ref[0]
    order = []
    for dx, dy in ((1, 1), (1, 0), (0, 1), (0, 0)):
        xx, yy = (ox if dx else x), (oy if dy else y)
        order += [(xx, yy, oc), (xx, yy, c)]

    def fetch(number):
        xx, yy, cc = order[number]
        seq = cc * 4 + xx * 2 + yy
        slot = number % 2
        copies = []
        for expert in range(experts):
            at = slice(expert * slot_rows, (expert + 1) * slot_rows)
            for which, (source, buf) in enumerate(((row_refs, row_buf), (answer_refs, answer_buf))):
                copies.append(
                    pltpu.make_async_copy(
                        source[expert].at[seq], buf.at[slot, at], fetch_sem.at[slot, 2 * expert + which]
                    )
                )
        for copy in copies:
            copy.start()
        return copies

    def compute(number, targets):
        xx, yy, cc = order[number]
        seq = cc * 4 + xx * 2 + yy
        slot = number % 2
        slot_ids = lax.broadcasted_iota(jnp.int32, (slot_rows, seq_len), 0).astype(jnp.float32)
        dot_ids = lax.broadcasted_iota(jnp.int32, (dot_rows, seq_len), 0)
        placings, combines = [], []
        dots = jnp.zeros((dot_rows, seq_len), jnp.float32)
        for expert in range(experts):
            placing = (slot_ids == table_ref[seq, pl.ds(experts_all + first + expert, 1), :]).astype(jnp.float32)
            placings.append(placing)
            combines.append(placing * table_ref[seq, pl.ds(first + expert, 1), :])
            dots = jnp.where(dot_ids == first + expert, dots_refs[expert][seq], dots)
        placing = jnp.concatenate(placings, axis=0).astype(jnp.bfloat16)
        combine = jnp.concatenate(combines, axis=0).astype(jnp.bfloat16)
        targets[0][...] = dots
        down = (((0,), (0,)), ((), ()))
        for left, buf, target in ((placing, row_buf, targets[1]), (combine, answer_buf, targets[2])):
            total = lax.dot_general(left, buf[slot], down, preferred_element_type=jnp.float32)
            target[...] = total.astype(target.dtype)

    heights = [out.shape[0] for out in outs]

    def half(part, xx, yy, which):
        return held[part].at[xx, yy, half_rows(which, heights[part])]

    fetched = {0: fetch(0)}
    greet([place.to_x, place.to_y, place.to_c])
    over = [[] for _ in outs]
    for step in range(4):
        for number in (2 * step, 2 * step + 1):
            xx, yy, cc = order[number]
            if number + 1 < len(order):
                fetched[number + 1] = fetch(number + 1)
            for copy in fetched.pop(number):
                copy.wait()
            if number % 2 == 0:
                compute(number, [ref.at[xx, yy] for ref in away])
                crossed = [
                    send(away[part].at[xx, yy], from_c[part].at[xx, yy], place.to_c) for part in range(3)
                ]
            else:
                compute(number, [ref.at[xx, yy] for ref in held])
        for part in range(3):
            crossed[part].wait_recv()
            add_into(held[part].at[xx, yy], held[part].at[xx, yy], from_c[part].at[xx, yy])
            first_got = from_first[part]
            if step == 0:
                over[part].append(send(half(part, xx, yy, 0), first_got.at[0, 1], place.to_y))
                over[part].append(send(half(part, xx, yy, 1), first_got.at[1, 1], place.to_x))
            elif step == 1:
                over[part].append(send(half(part, xx, yy, 1), first_got.at[1, 0], place.to_x))
            elif step == 2:
                over[part].append(send(half(part, xx, yy, 0), first_got.at[0, 0], place.to_y))
    second = []
    for part in range(3):
        a0, b0, b1, a1 = over[part]
        a0.wait_recv()
        add_into(half(part, ox, y, 0), half(part, ox, y, 0), from_first[part].at[0, 1])
        a2 = send(half(part, ox, y, 0), from_second[part].at[0], place.to_x)
        b0.wait_recv()
        add_into(half(part, x, oy, 1), half(part, x, oy, 1), from_first[part].at[1, 1])
        b2 = send(half(part, x, oy, 1), from_second[part].at[1], place.to_y)
        second.append((a2, b2))
    for part in range(3):
        a0, b0, b1, a1 = over[part]
        a1.wait_recv()
        add_into(half(part, x, y, 0), half(part, x, y, 0), from_first[part].at[0, 0])
        b1.wait_recv()
        add_into(half(part, x, y, 1), half(part, x, y, 1), from_first[part].at[1, 0])
    for part, (a2, b2) in enumerate(second):
        for which, copy in enumerate((a2, b2)):
            copy.wait_recv()
            at = half_rows(which, heights[part])
            add_into(outs[part].at[at], half(part, x, y, which), from_second[part].at[which])
    send.finish()


def combine_rows(first_own, answers, row_grads, dots, table, experts_all):
    experts = len(answers)
    seq_len = table.shape[2]
    _, slot_rows, width = answers[0].shape
    kinds = [
        ((-(-experts_all // 32) * 32, seq_len), jnp.float32),
        ((seq_len, width), jnp.bfloat16),
        ((seq_len, width), jnp.bfloat16),
    ]

    def scratch(lead, cut=1):
        return [pltpu.VMEM(lead + (shape[0] // cut, shape[1]), kind) for shape, kind in kinds]

    return pl.pallas_call(
        functools.partial(combine_kernel, experts, experts_all),
        out_shape=tuple(jax.ShapeDtypeStruct(shape, jnp.float32) for shape, _ in kinds),
        in_specs=[pl.BlockSpec(memory_space=pltpu.SMEM)]
        + [pl.BlockSpec(memory_space=pl.ANY)] * (2 * experts)
        + [pl.BlockSpec(memory_space=pltpu.VMEM)] * (experts + 1),
        out_specs=(pl.BlockSpec(memory_space=pltpu.VMEM),) * 3,
        scratch_shapes=scratch((2, 2))
        + scratch((2, 2))
        + scratch((2, 2))
        + scratch((2, 2), 2)
        + scratch((2,), 2)
        + [pltpu.VMEM((2, experts * slot_rows, width), jnp.bfloat16)] * 2
        + [
            pltpu.SemaphoreType.DMA((2, 2 * experts)),
            pltpu.SemaphoreType.DMA((32,)),
            pltpu.SemaphoreType.DMA((32,)),
        ],
        compiler_params=pltpu.CompilerParams(
            collective_id=2, has_side_effects=True, vmem_limit_bytes=60 * 2**20
        ),
        cost_estimate=pl.CostEstimate(
            flops=32 * seq_len * width * experts * slot_rows, bytes_accessed=150_000_000, transcendentals=0
        ),
        name="combine_rows",
    )(first_own, *answers, *row_grads, *dots, table)


def grads_kernel(count, cuts, spans, *refs):
    total_refs, refs = refs[:count], refs[count:]
    ins, refs = refs[:3], refs[3:]
    outs, refs = refs[: len(spans)], refs[len(spans) :]
    got_refs, refs = refs[:count], refs[count:]
    many = len(cuts)
    held, from_c, from_first, from_second, own, from_z, alls = (refs[many * i : many * (i + 1)] for i in range(7))
    send_sem, recv_sem = refs[7 * many :]
    place = Place()
    send = Sender(send_sem, recv_sem)
    x, y, c, z = place.x, place.y, place.c, place.z
    ox, oy, oc = place.ox, place.oy, place.oc
    greet([place.to_x, place.to_y, place.to_c] + place.to_z[1:])
    depth = ins[1].shape[2]
    piece = depth // 4
    order = [(ox, oy), (ox, y), (x, oy), (x, y)]

    def take(part, xx, yy, cc):
        number, start, wide = cuts[part]
        ref, quarter = ins[number], yy * 2 + cc
        if number == 0:
            return ref.at[:, xx, pl.ds(pl.multiple_of(quarter * piece, piece), piece)]
        at = pl.multiple_of(quarter * (ref.shape[3] // 4) + start, 128)
        return ref.at[:, xx, :, pl.ds(at, wide)]

    def half(part, xx, yy, which):
        return held[part].at[xx, yy, :, half_rows(which, own[part].shape[1])]

    crossed = [
        [send(take(part, xx, yy, oc), from_c[part].at[xx, yy], place.to_c) for xx, yy in order]
        for part in range(many)
    ]
    over, second, arriving, spread, last = {}, {}, {}, {}, {}

    def over_links(part):
        for step, (xx, yy) in enumerate(order):
            crossed[part][step].wait_recv()
            add_into(held[part].at[xx, yy], take(part, xx, yy, c), from_c[part].at[xx, yy])
            got = from_first[part]
            if step == 0:
                a0 = send(half(part, xx, yy, 0), got.at[0, 1], place.to_y)
                b0 = send(half(part, xx, yy, 1), got.at[1, 1], place.to_x)
            elif step == 1:
                b1 = send(half(part, xx, yy, 1), got.at[1, 0], place.to_x)
            elif step == 2:
                a1 = send(half(part, xx, yy, 0), got.at[0, 0], place.to_y)
        over[part] = (a0, b0, a1, b1)

    def over_again(part):
        a0, b0, a1, b1 = over[part]
        got = from_first[part]
        a0.wait_recv()
        add_into(half(part, ox, y, 0), half(part, ox, y, 0), got.at[0, 1])
        a2 = send(half(part, ox, y, 0), from_second[part].at[0], place.to_x)
        b0.wait_recv()
        add_into(half(part, x, oy, 1), half(part, x, oy, 1), got.at[1, 1])
        b2 = send(half(part, x, oy, 1), from_second[part].at[1], place.to_y)
        a1.wait_recv()
        add_into(half(part, x, y, 0), half(part, x, y, 0), got.at[0, 0])
        b1.wait_recv()
        add_into(half(part, x, y, 1), half(part, x, y, 1), got.at[1, 0])
        second[part] = (a2, b2)

    def over_z(part):
        for which, copy in enumerate(second[part]):
            copy.wait_recv()
            at = half_rows(which, own[part].shape[1])
            add_into(own[part].at[:, at], half(part, x, y, which), from_second[part].at[which])
        arriving[part] = [
            send(own[part].at[place.zs[d]], from_z[part].at[slot], place.to_z[1]) for slot, d in ((1, 3), (0, 1))
        ]

    def over_z_again(part):
        arrived = from_z[part]
        for copy in arriving[part]:
            copy.wait_recv()
        add_into(arrived.at[1], arrived.at[1], own[part].at[place.zs[2]])
        arriving[part] = send(arrived.at[1], arrived.at[2], place.to_z[2])
        add_into(arrived.at[0], arrived.at[0], own[part].at[z])

    def back_over_y(part):
        mine, arrived = alls[part].at[y, c], from_z[part]
        arriving[part].wait_recv()
        add_into(mine, arrived.at[0], arrived.at[2])
        over_y = send(mine, mine, place.to_y)
        spread[part] = (over_y, send(mine, mine, place.to_c))

    def back_over_c(part):
        over_y, over_c = spread[part]
        over_y.wait_recv()
        other = alls[part].at[oy, c]
        last[part] = (over_c, send(other, other, place.to_c))

    def lay_out(part):
        for copy in last[part]:
            copy.wait_recv()
        number, start, wide = cuts[part]
        for yy, cc in itertools.product((0, 1), (0, 1)):
            if number == 0:
                at = (yy * 2 + cc) * piece
                outs[0][at : at + piece, :] = alls[part][yy, cc]
                continue
            at = (yy * 2 + cc) * (ins[number].shape[3] // 4) + start
            for out, (owner, low, high) in zip(outs, spans):
                left, right = max(low, at), min(high, at + wide)
                if owner != number or left >= right:
                    continue

                def body(i, carry, out=out, low=low, left=left, right=right, at=at, yy=yy, cc=cc):
                    rows = pl.ds(pl.multiple_of(i * 16, 16), 16)
                    block = alls[part][yy, cc, rows, left - at : right - at]
                    out[rows, left - low : right - low] = block.astype(jnp.float32)
                    return carry

                lax.fori_loop(0, depth // 16, body, 0)

    steps = [(over_links, 0), (over_again, 1), (over_z, 2), (over_z_again, 3)]
    steps += [(back_over_y, 5), (back_over_c, 6), (lay_out, 7)]
    swapped = []
    for turn in range(many + 7):
        for step, delay in steps:
            if 0 <= turn - delay < many:
                step(turn - delay)
        if turn == many:
            swapped = [send(total.at[:, ox], got, place.to_x) for total, got in zip(total_refs, got_refs)]
    for copy in swapped:
        copy.wait_recv()
    send.finish()


def sum_grads(small, output, mixer, totals, q_width):
    depth = output.shape[2]
    arrays = (small, output, mixer)
    wide = mixer.shape[3] // 4
    split = wide * 3 // 5 // 128 * 128
    cuts = [(0, 0, small.shape[3]), (1, 0, output.shape[3] // 4), (2, 0, split), (2, split, wide - split)]
    shapes = [((depth // 4 if number == 0 else depth, width), arrays[number].dtype) for number, _, width in cuts]
    count = len(totals)
    last = (q_width + mixer.shape[3]) // 2
    spans = [(0, 0, small.shape[3]), (1, 0, output.shape[3])]
    spans += [(2, 0, q_width), (2, q_width, last), (2, last, mixer.shape[3])]

    def scratch(lead, cut=1):
        return [pltpu.VMEM(lead + (height // cut, wide), kind) for (height, wide), kind in shapes]

    return pl.pallas_call(
        functools.partial(grads_kernel, count, cuts, spans),
        out_shape=tuple(jax.ShapeDtypeStruct((depth, high - low), jnp.float32) for _, low, high in spans)
        + tuple(jax.ShapeDtypeStruct(t.shape[:1] + t.shape[2:], t.dtype) for t in totals),
        in_specs=[pl.BlockSpec(memory_space=pl.ANY)] * count + [pl.BlockSpec(memory_space=pltpu.VMEM)] * 3,
        out_specs=(pl.BlockSpec(memory_space=pltpu.VMEM),) * len(spans)
        + (pl.BlockSpec(memory_space=pl.ANY),) * count,
        scratch_shapes=scratch((2, 2, 4))
        + scratch((2, 2, 4))
        + scratch((2, 2, 4), 2)
        + scratch((2, 4), 2)
        + scratch((4,))
        + scratch((3,))
        + scratch((2, 2))
        + [pltpu.SemaphoreType.DMA((72,)), pltpu.SemaphoreType.DMA((72,))],
        compiler_params=pltpu.CompilerParams(
            collective_id=3, has_side_effects=True, vmem_limit_bytes=60 * 2**20
        ),
        cost_estimate=pl.CostEstimate(flops=0, bytes_accessed=300_000_000, transcendentals=0),
        name="sum_grads",
    )(*totals, *arrays)


def swap_kernel(count, *refs):
    total_refs, got_refs, (send_sem, recv_sem) = refs[:count], refs[count : 2 * count], refs[2 * count :]
    place = Place()
    send = Sender(send_sem, recv_sem)
    greet([place.to_x])
    for total, got in zip(total_refs, got_refs):
        send(total.at[:, place.ox], got, place.to_x)
    for copy in send.started:
        copy.wait_recv()
    send.finish()


def swap_totals(totals, collective):
    count = len(totals)
    return pl.pallas_call(
        functools.partial(swap_kernel, count),
        out_shape=tuple(jax.ShapeDtypeStruct(t.shape[:1] + t.shape[2:], t.dtype) for t in totals),
        in_specs=[pl.BlockSpec(memory_space=pl.ANY)] * count,
        out_specs=(pl.BlockSpec(memory_space=pl.ANY),) * count,
        scratch_shapes=[pltpu.SemaphoreType.DMA((count,))] * 2,
        compiler_params=pltpu.CompilerParams(collective_id=collective, has_side_effects=True),
        cost_estimate=pl.CostEstimate(flops=0, bytes_accessed=40_000_000, transcendentals=0),
        name="swap_totals",
    )(*totals)


def place_kernel(groups, side_ref, *refs):
    kept_refs, got_refs = refs[:groups], refs[groups : 2 * groups]
    up_out, down_out = refs[2 * groups :]
    half = down_out.shape[2] // 2
    first = side_ref[0] == 0
    experts = [(g, k) for g in range(groups) for k in range(kept_refs[g].shape[0])]
    for expert, (g, k) in enumerate(experts):
        kept = kept_refs[g][k, 0].astype(jnp.float32)
        got = got_refs[g][k].astype(jnp.float32)
        low, high = jnp.where(first, kept, got), jnp.where(first, got, kept)
        for index, part in enumerate((low, high)):
            for group in (0, 1):
                at = (2 * group + index) * half
                up_out[expert, :, at : at + half] = part[:, group * half : (group + 1) * half]
            down_out[expert, :, index * half : (index + 1) * half] = part[:, 2 * half :]


def place_sums(side, totals, got):
    count = sum(g.shape[0] for g in got)
    _, depth, width = got[0].shape
    step = depth // 4
    half = width // 3
    return pl.pallas_call(
        functools.partial(place_kernel, len(got)),
        out_shape=(
            jax.ShapeDtypeStruct((count, depth, 4 * half), jnp.float32),
            jax.ShapeDtypeStruct((count, depth, 2 * half), jnp.float32),
        ),
        grid_spec=pltpu.PrefetchScalarGridSpec(
            num_scalar_prefetch=1,
            grid=(4,),
            in_specs=[
                pl.BlockSpec((t.shape[0], 1, step, width), lambda i, side: (0, side[0], i, 0)) for t in totals
            ]
            + [pl.BlockSpec((g.shape[0], step, width), lambda i, side: (0, i, 0)) for g in got],
            out_specs=(
                pl.BlockSpec((count, step, 4 * half), lambda i, side: (0, i, 0)),
                pl.BlockSpec((count, step, 2 * half), lambda i, side: (0, i, 0)),
            ),
        ),
        cost_estimate=pl.CostEstimate(flops=0, bytes_accessed=9_000_000, transcendentals=0),
        name="place_sums",
    )(side, *totals, *got)


def expert_kernel(
    expert, experts_all, first_ref, table_ref, rows_ref, dout_ref, w_ref, *refs
):
    answer_ref, row_ref, w_out, dots_ref, total, picked, picked_dout = refs[-7:]
    group, slot_rows, width = answer_ref.shape
    half = w_ref.shape[3] // 3

    def weight(columns):
        return w_ref[:, 0, :, columns].reshape(width, -1)

    both_columns, down_columns = slice(0, 2 * half), slice(2 * half, 3 * half)
    seq_len = rows_ref.shape[1]
    step = pl.program_id(0)
    slot_ids = lax.broadcasted_iota(jnp.int32, (slot_rows, seq_len), 0).astype(jnp.float32)
    gate_parts = []

    def own_row(q, at):
        return table_ref[q, pl.ds(at + first_ref[0] + expert, 1), :]

    for q in range(group):
        placing = (slot_ids == own_row(q, experts_all)).astype(jnp.float32)
        gate_parts.append(jnp.sum(placing * own_row(q, 0), axis=1, keepdims=True))
        low = placing.astype(jnp.bfloat16)
        at = slice(q * slot_rows, (q + 1) * slot_rows)
        picked[at, :] = jnp.dot(low, rows_ref[q], preferred_element_type=jnp.float32).astype(jnp.bfloat16)
        picked_dout[at, :] = jnp.dot(low, dout_ref[q], preferred_element_type=jnp.float32).astype(jnp.bfloat16)
    gate = jnp.concatenate(gate_parts, axis=0)
    both = jnp.dot(picked[...], weight(both_columns), preferred_element_type=jnp.float32)
    gate_part, up_part = both[:, :half], both[:, half:]
    sigmoid = 1.0 / (1.0 + jnp.exp(-gate_part))
    silu = gate_part * sigmoid
    active = (silu * up_part).astype(jnp.bfloat16)
    across = (((1,), (1,)), ((), ()))
    down = (((0,), (0,)), ((), ()))
    answer = lax.dot_general(active, weight(down_columns), across, preferred_element_type=jnp.float32)
    answer = answer.astype(jnp.bfloat16)
    dots = jnp.sum(picked_dout[...].astype(jnp.float32) * answer.astype(jnp.float32), axis=1, keepdims=True)
    for q in range(group):
        at = slice(q * slot_rows, (q + 1) * slot_rows)
        answer_ref[q] = answer[at, :]
        placing = (slot_ids == own_row(q, experts_all)).astype(jnp.float32)
        dots_ref[q] = jnp.sum(placing * dots[at, :], axis=0, keepdims=True)
    picked_dout[...] = (picked_dout[...].astype(jnp.float32) * gate).astype(jnp.bfloat16)
    active_grad = jnp.dot(picked_dout[...], weight(down_columns), preferred_element_type=jnp.float32)
    both_grad = jnp.concatenate(
        [
            active_grad * up_part * sigmoid * (1.0 + gate_part * (1.0 - sigmoid)),
            active_grad * silu,
        ],
        axis=1,
    ).astype(jnp.bfloat16)
    row = lax.dot_general(both_grad, weight(both_columns), across, preferred_element_type=jnp.float32)
    row = row.astype(jnp.bfloat16)
    for q in range(group):
        row_ref[q] = row[q * slot_rows : (q + 1) * slot_rows, :]
    up_term = lax.dot_general(picked[...], both_grad, down, preferred_element_type=jnp.float32)
    down_term = lax.dot_general(picked_dout[...], active, down, preferred_element_type=jnp.float32)

    @pl.when(step == 0)
    def _():
        total[:, : 2 * half] = up_term
        total[:, 2 * half :] = down_term

    @pl.when(step > 0)
    def _():
        total[:, : 2 * half] += up_term
        total[:, 2 * half :] += down_term

    @pl.when(step == pl.num_programs(0) - 1)
    def _():
        w_out[...] = total[...].astype(w_out.dtype).reshape(w_out.shape)


def run_expert(first_own, table, rows, dout, weights, expert, experts_all, slot_rows, sums, number, sum_count):
    count, seq_len, width = rows.shape
    group = count // 2
    weights, at = weights
    parts, _, deep, wide = weights.shape
    one = pl.BlockSpec((group, 1, seq_len), lambda i: (i, 0, 0))
    listed = pl.BlockSpec((group,) + table.shape[1:], lambda i: (i, 0, 0))
    tall = pl.BlockSpec((group, seq_len, width), lambda i: (i, 0, 0))
    slot = pl.BlockSpec((group, slot_rows, width), lambda i: (i, 0, 0))
    taken = pl.BlockSpec((parts, 1, deep, wide), lambda i: (0, at, 0, 0))
    given = pl.BlockSpec((parts, 1, deep, wide), lambda i: (0, number, 0, 0))
    flops = 2 * count * slot_rows * width * (2 * seq_len + 3 * wide)
    held = [] if sums is None else [sums]
    return pl.pallas_call(
        functools.partial(expert_kernel, expert, experts_all),
        grid=(2,),
        out_shape=(
            jax.ShapeDtypeStruct((count, slot_rows, width), jnp.bfloat16),
            jax.ShapeDtypeStruct((count, slot_rows, width), jnp.bfloat16),
            jax.ShapeDtypeStruct((parts, sum_count, deep, wide), jnp.bfloat16),
            jax.ShapeDtypeStruct((count, 1, seq_len), jnp.float32),
        ),
        in_specs=[pl.BlockSpec(memory_space=pltpu.SMEM), listed, tall, tall, taken]
        + [pl.BlockSpec(memory_space=pl.ANY)] * len(held),
        out_specs=(slot, slot, given, one),
        scratch_shapes=[
            pltpu.VMEM((parts * deep, wide), jnp.float32),
            pltpu.VMEM((group * slot_rows, width), jnp.bfloat16),
            pltpu.VMEM((group * slot_rows, width), jnp.bfloat16),
        ],
        input_output_aliases={5: 2} if held else {},
        compiler_params=pltpu.CompilerParams(vmem_limit_bytes=60 * 2**20),
        cost_estimate=pl.CostEstimate(flops=flops, bytes_accessed=25_000_000, transcendentals=0),
        name="run_expert",
    )(first_own, table, rows, dout, weights, *held)


def layer_on_device(
    tokens,
    lengths,
    routes,
    cotangent,
    first_gain,
    query_weight,
    key_matrix,
    value_matrix,
    output_weight,
    second_gain,
    router_weight,
    gate_up_weight,
    down_weight,
):
    seq_len, model_width = tokens.shape
    q_heads = query_weight.shape[1] // HEAD_DIM
    kv_heads = key_matrix.shape[1] // HEAD_DIM
    group_size = q_heads // kv_heads
    experts_all = router_weight.shape[1]
    local_experts = gate_up_weight.shape[1]
    inner_width = down_weight.shape[2]
    half_inner = inner_width // 2
    q_width, kv_width = query_weight.shape[1], key_matrix.shape[1]
    slot_count = 8 * max(
        seq_len // 32, (seq_len * routes.shape[1] + 8 * experts_all - 1) // (8 * experts_all)
    )
    score_factor = HEAD_DIM ** (-0.5)
    along_z = [[z * 2 + x for z in range(4)] for x in range(2)]
    expert_at, shard_at = lax.axis_index(EXPERT), lax.axis_index(SHARD)
    x_at = lax.rem(shard_at, 2)
    depth = first_gain.shape[0]

    early = 4
    up_first = gate_up_weight.transpose(1, 0, 2)
    down_first = down_weight.transpose(1, 0, 2)

    def along(halves):
        block = halves.reshape(1, halves.shape[0], 2 * depth, 3 * half_inner)
        return lax.all_gather(block, SHARD, axis=0, tiled=True, axis_index_groups=along_z)

    halves = exchange_halves(up_first, down_first, 0, 1)
    expert_weights = [(along(halves), 0)]
    up_first, down_first, _ = lax.optimization_barrier((up_first, down_first, halves))
    halves = exchange_halves(up_first, down_first, 1, early - 1)
    gathered = along(halves)
    expert_weights += [(gathered, number) for number in range(early - 1)]

    position = jnp.arange(seq_len, dtype=jnp.int32)
    length = lengths[0]
    valid_rows = (position < length).astype(jnp.float32)
    dout_full = cotangent.astype(jnp.float32) * valid_rows[:, None]
    dout_low = dout_full.astype(jnp.bfloat16)
    mixer_block = jnp.concatenate([query_weight, key_matrix, value_matrix], axis=1)
    small_block = jnp.concatenate(
        [
            router_weight.astype(jnp.float32),
            first_gain.astype(jnp.float32)[:, None],
            second_gain.astype(jnp.float32)[:, None],
            jnp.zeros((depth, 128 - experts_all - 2), jnp.float32),
        ],
        axis=1,
    )
    mixer_block, output_block, small_block, dout_low = lax.optimization_barrier(
        (mixer_block, output_weight, small_block, dout_low, halves)
    )[:4]
    mixer_full, output_full, small_full, dout_plane, *halves = gather_weights(
        mixer_block, output_block, small_block, dout_low, up_first, down_first, early, (local_experts - early,)
    )
    for some in halves:
        gathered = along(some)
        expert_weights += [(gathered, number) for number in range(some.shape[0])]
    mixer_full = mixer_full.reshape(model_width, mixer_block.shape[1])
    output_full = output_full.reshape(model_width, output_weight.shape[1])
    small_full = small_full.reshape(model_width, 128)
    dout_plane = dout_plane.reshape(8, seq_len, model_width)
    router_full = small_full[:, :experts_all].astype(jnp.bfloat16)
    gain_one, gain_two = small_full[:, experts_all], small_full[:, experts_all + 1]

    cosine, sine_table = rope_tables(seq_len, HEAD_DIM)
    source = tokens.astype(jnp.float32)
    first_scale = lax.rsqrt(jnp.mean(source * source, axis=-1, keepdims=True) + norm_eps)
    first_norm_output = (source * first_scale * gain_one).astype(jnp.bfloat16)
    mixed_in = product("za,ao->zo", first_norm_output, mixer_full)
    queries = rotate(mixed_in[:, :q_width].reshape(seq_len, q_heads, HEAD_DIM), cosine, sine_table)
    queries = queries.astype(jnp.bfloat16).reshape(seq_len, kv_heads, group_size, HEAD_DIM)
    key_row_block = rotate(
        mixed_in[:, q_width : q_width + kv_width].reshape(seq_len, kv_heads, HEAD_DIM), cosine, sine_table
    ).astype(jnp.bfloat16)
    value_row_block = (
        mixed_in[:, q_width + kv_width :].astype(jnp.bfloat16).reshape(seq_len, kv_heads, HEAD_DIM)
    )
    allowed = (position[None, :] <= position[:, None]) & (position[None, :] < length)
    scores = jnp.where(
        allowed, product("qhgd,khd->hgqk", queries, key_row_block) * score_factor, -1e30
    )
    row_max = jnp.max(scores, axis=-1, keepdims=True)
    shifted = jnp.exp(scores - row_max)
    row_total = jnp.sum(shifted, axis=-1, keepdims=True)
    log_total = row_max + jnp.log(row_total)
    probs_low = (shifted / row_total).astype(jnp.bfloat16)
    mixed_heads = (
        product("hgqk,khd->qhgd", probs_low, value_row_block)
        .reshape(seq_len, q_heads * HEAD_DIM)
        .astype(jnp.bfloat16)
    )
    hidden = source + product("sf,df->sd", mixed_heads, output_full)
    second_scale = lax.rsqrt(jnp.mean(hidden * hidden, axis=-1, keepdims=True) + norm_eps)
    second_normed = (hidden * second_scale * gain_two).astype(jnp.bfloat16)
    logits = product("sd,de->se", second_normed, router_full)
    chosen = (routes[:, :, None] == jnp.arange(experts_all, dtype=jnp.int32)).astype(jnp.float32)
    picked = jnp.sum(chosen * logits[:, None, :], axis=-1)
    gate_soft = jax.nn.softmax(picked, axis=-1)
    routed = jnp.sum(chosen, axis=1) * valid_rows[:, None]
    earlier = (position[None, :] < position[:, None]).astype(jnp.bfloat16)
    rank_rows = product("st,te->se", earlier, routed.astype(jnp.bfloat16))
    slot_of = jnp.where(routed > 0, rank_rows, -1.0)
    gate_low = gate_soft.astype(jnp.bfloat16).astype(jnp.float32)
    gate_full = jnp.sum(chosen * gate_low[:, :, None], axis=1)
    listed = -(-2 * experts_all // 16) * 16
    table = jnp.concatenate(
        [gate_full, slot_of, jnp.zeros((seq_len, listed - 2 * experts_all), jnp.float32)], axis=1
    ).T
    rows_plane, table_plane = gather_rows(second_normed, table)
    rows_plane = rows_plane.reshape(8, seq_len, model_width)
    table_plane = table_plane.reshape(8, listed, seq_len)
    first_own = (expert_at * local_experts).astype(jnp.int32).reshape(1)
    slot_rows = -(-slot_count // 16) * 16
    turn, results, sums = first_own, [], []
    for first, count in ((0, 3), (3, local_experts - 3)):
        held = None
        for number in range(count):
            e = first + number
            answer, row_grad, held, dot = run_expert(
                turn, table_plane, rows_plane, dout_plane, expert_weights[e], e, experts_all, slot_rows,
                held, number, count,
            )
            results.append((answer, row_grad, dot))
            turn = lax.optimization_barrier((first_own, dot))[0]
        sums.append(held)
    answers, row_grads, dots = zip(*results)
    dot_rows, grad_rows, value_rows = combine_rows(
        first_own, answers, row_grads, dots, table_plane, experts_all
    )
    dot_rows = dot_rows.T
    output = (hidden + value_rows).astype(jnp.bfloat16)
    gate_grad = jnp.sum(chosen * dot_rows[:, None, :experts_all], axis=-1)
    inner_sum = jnp.sum(gate_soft * gate_grad, axis=-1, keepdims=True)
    picked_grad = gate_soft * (gate_grad - inner_sum)
    logits_grad = jnp.sum(chosen * picked_grad[:, :, None], axis=1).astype(jnp.bfloat16)
    router_term = product("sd,se->de", second_normed, logits_grad)

    totals = [
        lax.psum_scatter(
            held, SHARD, scatter_dimension=0, tiled=True, axis_index_groups=along_z
        ).reshape(held.shape[1], 2, depth, 3 * half_inner)
        for held in sums
    ]

    normed_grad = grad_rows + product("se,de->sd", logits_grad, router_full)
    hidden_grad, second_gain_term = norm_back(normed_grad, hidden, second_scale, gain_two)
    hidden_grad = hidden_grad + dout_full
    attn_grad = hidden_grad.astype(jnp.bfloat16)
    output_term = product("sd,sf->df", attn_grad, mixed_heads)
    mixed_grad = (
        product("za,ao->zo", attn_grad, output_full)
        .astype(jnp.bfloat16)
        .reshape(seq_len, kv_heads, group_size, HEAD_DIM)
    )
    scores_again = jnp.where(
        allowed, product("qhgd,khd->hgqk", queries, key_row_block) * score_factor, -1e30
    )
    probs_again = jnp.exp(scores_again - log_total)
    probs_grad = product("qhgd,khd->hgqk", mixed_grad, value_row_block)
    row_inner = jnp.sum(probs_again * probs_grad, axis=-1, keepdims=True)
    scores_grad = (probs_again * (probs_grad - row_inner)).astype(jnp.bfloat16)
    query_back = product("hgqk,khd->qhgd", scores_grad, key_row_block) * score_factor
    key_back = product("hgqk,qhgd->khd", scores_grad, queries) * score_factor
    value_back = product("hgqk,qhgd->khd", probs_again.astype(jnp.bfloat16), mixed_grad)
    query_pre = (
        unrotate(query_back.reshape(seq_len, q_heads, HEAD_DIM), cosine, sine_table)
        .astype(jnp.bfloat16)
        .reshape(seq_len, q_heads * HEAD_DIM)
    )
    key_pre = (
        unrotate(key_back, cosine, sine_table)
        .astype(jnp.bfloat16)
        .reshape(seq_len, kv_heads * HEAD_DIM)
    )
    value_pre = value_back.astype(jnp.bfloat16).reshape(seq_len, kv_heads * HEAD_DIM)
    mixed_pre = jnp.concatenate([query_pre, key_pre, value_pre], axis=1)
    mixer_term = product("sd,sf->df", first_norm_output, mixed_pre).astype(jnp.bfloat16)
    normed1_grad = product("sf,df->sd", mixed_pre, mixer_full)
    tokens_grad, first_gain_term = norm_back(normed1_grad, source, first_scale, gain_one)
    tokens_grad = tokens_grad + hidden_grad
    small_terms = jnp.concatenate(
        [
            router_term,
            first_gain_term[:, None],
            second_gain_term[:, None],
            jnp.zeros((model_width, 128 - experts_all - 2), jnp.float32),
        ],
        axis=1,
    ).reshape(4, 2, depth, 128)
    small_sum, output_sum, query_sum, key_sum, value_sum, *got = sum_grads(
        small_terms,
        output_term.astype(jnp.bfloat16).reshape(4, 2, depth, output_weight.shape[1]),
        mixer_term.reshape(4, 2, depth, mixer_block.shape[1]),
        totals[:1],
        q_width,
    )
    late = lax.optimization_barrier((small_sum, totals[-1]))[1:]
    got += swap_totals(late, 5)
    both_sums, down_sums = place_sums(x_at.reshape(1), totals, got)
    return (
        output,
        tokens_grad,
        small_sum[:, experts_all],
        query_sum,
        key_sum,
        value_sum,
        output_sum,
        small_sum[:, experts_all + 1],
        small_sum[:, :experts_all],
        both_sums.transpose(1, 0, 2),
        down_sums.transpose(1, 0, 2),
    )


def solution(mesh):
    small_slice = mesh.shape[EXPERT] == 4 and mesh.shape[SHARD] == 8
    placed = (
        P((EXPERT, SHARD), None),
        P((EXPERT, SHARD)),
        P((EXPERT, SHARD), None),
        P((EXPERT, SHARD), None),
        P(SHARD),
        P(SHARD, None),
        P(SHARD, None),
        P(SHARD, None),
        P(SHARD, None),
        P(SHARD),
        P(SHARD, None),
        P(SHARD, EXPERT, None),
        P(SHARD, EXPERT, None),
    )
    return jax.shard_map(
        layer_on_device if small_slice else on_device,
        mesh=mesh,
        in_specs=placed,
        out_specs=(
            P((EXPERT, SHARD), None),
            P((EXPERT, SHARD), None),
            P(SHARD),
            P(SHARD, None),
            P(SHARD, None),
            P(SHARD, None),
            P(SHARD, None),
            P(SHARD),
            P(SHARD, None),
            P(SHARD, EXPERT, None),
            P(SHARD, EXPERT, None),
        ),
        check_vma=False,
    )
```

```python
import functools
import itertools

import jax
import jax.numpy as jnp
from jax import lax
from jax.experimental import pallas as pl
from jax.experimental.pallas import tpu as pltpu
from jax.sharding import PartitionSpec as P

HEAD_DIM = 64
EXPERT, SHARD = "expert", "shard"


norm_eps = 1e-06


def product(form, left, right):
    return jnp.einsum(form, left, right, preferred_element_type=jnp.float32)


def rope_tables(row_count, head_width):
    half_width = head_width // 2
    frequency = 10000.0 ** (-(jnp.arange(half_width, dtype=jnp.float32) * (2.0 / head_width)))
    angles = jnp.arange(row_count, dtype=jnp.float32)[:, None] * frequency[None, :]
    return (jnp.cos(angles)[:, None, :], jnp.sin(angles)[:, None, :])


def rotate(values_in, cosine, sine_table):
    half_width = values_in.shape[-1] // 2
    first_half = values_in[..., :half_width]
    second_half = values_in[..., half_width:]
    return jnp.concatenate(
        [
            first_half * cosine - second_half * sine_table,
            second_half * cosine + first_half * sine_table,
        ],
        axis=-1,
    )


def unrotate(grad_in, cosine, sine_table):
    half_width = grad_in.shape[-1] // 2
    first_half = grad_in[..., :half_width]
    second_half = grad_in[..., half_width:]
    return jnp.concatenate(
        [
            first_half * cosine + second_half * sine_table,
            second_half * cosine - first_half * sine_table,
        ],
        axis=-1,
    )


def norm_back(upstream, source, inv_scale, gain_vec):
    scaled = upstream * gain_vec
    gain_grad = jnp.sum(upstream * source * inv_scale, axis=0)
    grad_out = inv_scale * (
        scaled - source * inv_scale * inv_scale * jnp.mean(scaled * source, axis=-1, keepdims=True)
    )
    return (grad_out, gain_grad)


def on_device(
    tokens,
    lengths,
    routes,
    cotangent,
    first_gain,
    query_weight,
    key_matrix,
    value_matrix,
    output_weight,
    second_gain,
    router_weight,
    gate_up_weight,
    down_weight,
):
    seq_len, model_width = tokens.shape
    route_width = routes.shape[1]
    q_heads = query_weight.shape[1] // HEAD_DIM
    kv_heads = key_matrix.shape[1] // HEAD_DIM
    group_size = q_heads // kv_heads
    experts_all = router_weight.shape[1]
    local_experts = gate_up_weight.shape[1]
    inner_width = down_weight.shape[2]
    owners = lax.axis_size(EXPERT)
    slot_count = 8 * max(
        seq_len // 32, (seq_len * route_width + 8 * experts_all - 1) // (8 * experts_all)
    )
    score_factor = HEAD_DIM ** (-0.5)
    gain_one, query_full, key_complete, value_complete, output_full, gain_two, router_full = (
        lax.all_gather(first_gain, SHARD, axis=0, tiled=True),
        lax.all_gather(query_weight, SHARD, axis=0, tiled=True),
        lax.all_gather(key_matrix, SHARD, axis=0, tiled=True),
        lax.all_gather(value_matrix, SHARD, axis=0, tiled=True),
        lax.all_gather(output_weight, SHARD, axis=0, tiled=True),
        lax.all_gather(second_gain, SHARD, axis=0, tiled=True),
        lax.all_gather(router_weight, SHARD, axis=0, tiled=True),
    )
    gate_up_full, down_full = (
        lax.all_gather(gate_up_weight, SHARD, axis=0, tiled=True),
        lax.all_gather(down_weight, SHARD, axis=0, tiled=True),
    )
    gain_one = gain_one.astype(jnp.float32)
    gain_two = gain_two.astype(jnp.float32)
    cosine, sine_table = rope_tables(seq_len, HEAD_DIM)
    source = tokens.astype(jnp.float32)
    first_scale = lax.rsqrt(jnp.mean(source * source, axis=-1, keepdims=True) + norm_eps)
    first_norm_output = (source * first_scale * gain_one).astype(jnp.bfloat16)
    queries = rotate(
        product("za,ao->zo", first_norm_output, query_full).reshape(seq_len, q_heads, HEAD_DIM),
        cosine,
        sine_table,
    )
    queries = queries.astype(jnp.bfloat16).reshape(seq_len, kv_heads, group_size, HEAD_DIM)
    key_row_block = rotate(
        product("za,ao->zo", first_norm_output, key_complete).reshape(seq_len, kv_heads, HEAD_DIM),
        cosine,
        sine_table,
    ).astype(jnp.bfloat16)
    value_row_block = (
        product("za,ao->zo", first_norm_output, value_complete)
        .astype(jnp.bfloat16)
        .reshape(seq_len, kv_heads, HEAD_DIM)
    )
    position = jnp.arange(seq_len, dtype=jnp.int32)
    length = lengths[0]
    allowed = (position[None, :] <= position[:, None]) & (position[None, :] < length)
    scores = jnp.where(
        allowed, product("qhgd,khd->hgqk", queries, key_row_block) * score_factor, -1e30
    )
    row_max = jnp.max(scores, axis=-1, keepdims=True)
    shifted = jnp.exp(scores - row_max)
    row_total = jnp.sum(shifted, axis=-1, keepdims=True)
    log_total = row_max + jnp.log(row_total)
    probs_low = (shifted / row_total).astype(jnp.bfloat16)
    mixed_heads = (
        product("hgqk,khd->qhgd", probs_low, value_row_block)
        .reshape(seq_len, q_heads * HEAD_DIM)
        .astype(jnp.bfloat16)
    )
    hidden = source + product("sf,df->sd", mixed_heads, output_full)
    second_scale = lax.rsqrt(jnp.mean(hidden * hidden, axis=-1, keepdims=True) + norm_eps)
    second_normed = (hidden * second_scale * gain_two).astype(jnp.bfloat16)
    logits = product("sd,de->se", second_normed, router_full)
    chosen = (routes[:, :, None] == jnp.arange(experts_all, dtype=jnp.int32)).astype(jnp.float32)
    picked = jnp.sum(chosen * logits[:, None, :], axis=-1)
    gate_soft = jax.nn.softmax(picked, axis=-1)
    valid_rows = (position < length).astype(jnp.float32)
    routed = jnp.sum(chosen, axis=1) * valid_rows[:, None]
    earlier = (position[None, :] < position[:, None]).astype(jnp.bfloat16)
    rank_rows = product("st,te->se", earlier, routed.astype(jnp.bfloat16))
    slot_ids = jnp.arange(slot_count, dtype=jnp.float32)
    placing = (routed.T[:, None, :] * (rank_rows.T[:, None, :] == slot_ids[None, :, None])).astype(
        jnp.bfloat16
    )
    outgoing = (
        product("ems,sd->emd", placing, second_normed)
        .astype(jnp.bfloat16)
        .reshape(owners, local_experts, slot_count, model_width)
    )
    row_block = lax.all_to_all(outgoing, EXPERT, split_axis=0, concat_axis=0, tiled=True)
    both_pre = product("oemd,def->oemf", row_block, gate_up_full)
    active = (jax.nn.silu(both_pre[..., :inner_width]) * both_pre[..., inner_width:]).astype(
        jnp.bfloat16
    )
    answer = product("oemf,def->oemd", active, down_full).astype(jnp.bfloat16)
    returned = lax.all_to_all(answer, EXPERT, split_axis=0, concat_axis=0, tiled=True).reshape(
        experts_all, slot_count, model_width
    )
    gate_full = product("ske,sk->se", chosen.astype(jnp.bfloat16), gate_soft.astype(jnp.bfloat16))
    placing_float = placing.astype(jnp.float32)
    combine = (placing_float * gate_full.T[:, None, :]).astype(jnp.bfloat16)
    output = (hidden + product("ems,emd->sd", combine, returned)).astype(jnp.bfloat16)
    dout_full = cotangent.astype(jnp.float32) * valid_rows[:, None]
    dout_low = dout_full.astype(jnp.bfloat16)
    grad_rows = (
        product("ems,sd->emd", combine, dout_low)
        .astype(jnp.bfloat16)
        .reshape(owners, local_experts, slot_count, model_width)
    )
    incoming = lax.all_to_all(grad_rows, EXPERT, split_axis=0, concat_axis=0, tiled=True)
    answer_dot = product("emd,sd->ems", returned, dout_low)
    gate_grad_full = jnp.sum(placing_float * answer_dot, axis=1)
    gate_grad = jnp.sum(chosen * gate_grad_full.T[:, None, :], axis=-1)
    inner_sum = jnp.sum(gate_soft * gate_grad, axis=-1, keepdims=True)
    picked_grad = gate_soft * (gate_grad - inner_sum)
    logits_grad = jnp.sum(chosen * picked_grad[:, :, None], axis=1).astype(jnp.bfloat16)
    router_term = product("sd,se->de", second_normed, logits_grad)
    gate_up_full, down_full = (
        lax.all_gather(gate_up_weight, SHARD, axis=0, tiled=True),
        lax.all_gather(down_weight, SHARD, axis=0, tiled=True),
    )
    gate_part = both_pre[..., :inner_width]
    up_part = both_pre[..., inner_width:]
    sigmoid_gate = jax.nn.sigmoid(gate_part)
    silu_gate = gate_part * sigmoid_gate
    active_again = (silu_gate * up_part).astype(jnp.bfloat16)
    active_grad = product("oemd,def->oemf", incoming, down_full)
    both_grad = jnp.concatenate(
        [
            active_grad * up_part * sigmoid_gate * (1.0 + gate_part * (1.0 - sigmoid_gate)),
            active_grad * silu_gate,
        ],
        axis=-1,
    ).astype(jnp.bfloat16)
    row_grad = product("oemf,def->oemd", both_grad, gate_up_full).astype(jnp.bfloat16)
    gate_up_term = product("oemd,oemf->def", row_block, both_grad)
    down_term = product("oemd,oemf->def", incoming, active_again)
    back_rows = lax.all_to_all(row_grad, EXPERT, split_axis=0, concat_axis=0, tiled=True).reshape(
        experts_all, slot_count, model_width
    )
    gate_up_total, down_total = (
        lax.psum_scatter(
            gate_up_term.astype(jnp.bfloat16), SHARD, scatter_dimension=0, tiled=True
        ).astype(jnp.float32),
        lax.psum_scatter(
            down_term.astype(jnp.bfloat16), SHARD, scatter_dimension=0, tiled=True
        ).astype(jnp.float32),
    )
    normed_grad = product("ems,emd->sd", placing, back_rows) + product(
        "se,de->sd", logits_grad, router_full
    )
    hidden_grad, second_gain_term = norm_back(normed_grad, hidden, second_scale, gain_two)
    hidden_grad = hidden_grad + dout_full
    attn_grad = hidden_grad.astype(jnp.bfloat16)
    output_term = product("sd,sf->df", attn_grad, mixed_heads)
    mixed_grad = (
        product("za,ao->zo", attn_grad, output_full)
        .astype(jnp.bfloat16)
        .reshape(seq_len, kv_heads, group_size, HEAD_DIM)
    )
    scores_again = jnp.where(
        allowed, product("qhgd,khd->hgqk", queries, key_row_block) * score_factor, -1e30
    )
    probs_again = jnp.exp(scores_again - log_total)
    probs_grad = product("qhgd,khd->hgqk", mixed_grad, value_row_block)
    row_inner = jnp.sum(probs_again * probs_grad, axis=-1, keepdims=True)
    scores_grad = (probs_again * (probs_grad - row_inner)).astype(jnp.bfloat16)
    query_back = product("hgqk,khd->qhgd", scores_grad, key_row_block) * score_factor
    key_back = product("hgqk,qhgd->khd", scores_grad, queries) * score_factor
    value_back = product("hgqk,qhgd->khd", probs_again.astype(jnp.bfloat16), mixed_grad)
    query_pre = (
        unrotate(query_back.reshape(seq_len, q_heads, HEAD_DIM), cosine, sine_table)
        .astype(jnp.bfloat16)
        .reshape(seq_len, q_heads * HEAD_DIM)
    )
    key_pre = (
        unrotate(key_back, cosine, sine_table)
        .astype(jnp.bfloat16)
        .reshape(seq_len, kv_heads * HEAD_DIM)
    )
    value_pre = value_back.astype(jnp.bfloat16).reshape(seq_len, kv_heads * HEAD_DIM)
    query_term = product("sd,sf->df", first_norm_output, query_pre)
    key_term = product("sd,sf->df", first_norm_output, key_pre)
    value_term = product("sd,sf->df", first_norm_output, value_pre)
    normed1_grad = (
        product("sf,df->sd", query_pre, query_full)
        + product("sf,df->sd", key_pre, key_complete)
        + product("sf,df->sd", value_pre, value_complete)
    )
    tokens_grad, first_gain_term = norm_back(normed1_grad, source, first_scale, gain_one)
    tokens_grad = tokens_grad + hidden_grad
    mixer_sums = (
        lax.psum_scatter(
            first_gain_term.astype(jnp.bfloat16), SHARD, scatter_dimension=0, tiled=True
        ).astype(jnp.float32),
        lax.psum_scatter(
            query_term.astype(jnp.bfloat16), SHARD, scatter_dimension=0, tiled=True
        ).astype(jnp.float32),
        lax.psum_scatter(
            key_term.astype(jnp.bfloat16), SHARD, scatter_dimension=0, tiled=True
        ).astype(jnp.float32),
        lax.psum_scatter(
            value_term.astype(jnp.bfloat16), SHARD, scatter_dimension=0, tiled=True
        ).astype(jnp.float32),
        lax.psum_scatter(
            output_term.astype(jnp.bfloat16), SHARD, scatter_dimension=0, tiled=True
        ).astype(jnp.float32),
        lax.psum_scatter(
            second_gain_term.astype(jnp.bfloat16), SHARD, scatter_dimension=0, tiled=True
        ).astype(jnp.float32),
        lax.psum_scatter(
            router_term.astype(jnp.bfloat16), SHARD, scatter_dimension=0, tiled=True
        ).astype(jnp.float32),
    )
    mixer_sums = (
        lax.psum(mixer_sums[0].astype(jnp.bfloat16), EXPERT).astype(jnp.float32),
        lax.psum(mixer_sums[1].astype(jnp.bfloat16), EXPERT).astype(jnp.float32),
        lax.psum(mixer_sums[2].astype(jnp.bfloat16), EXPERT).astype(jnp.float32),
        lax.psum(mixer_sums[3].astype(jnp.bfloat16), EXPERT).astype(jnp.float32),
        lax.psum(mixer_sums[4].astype(jnp.bfloat16), EXPERT).astype(jnp.float32),
        lax.psum(mixer_sums[5].astype(jnp.bfloat16), EXPERT).astype(jnp.float32),
        lax.psum(mixer_sums[6].astype(jnp.bfloat16), EXPERT).astype(jnp.float32),
    )
    return (
        output,
        tokens_grad,
        mixer_sums[0],
        mixer_sums[1],
        mixer_sums[2],
        mixer_sums[3],
        mixer_sums[4],
        mixer_sums[5],
        mixer_sums[6],
        gate_up_total,
        down_total,
    )


MESH_IDS = pl.DeviceIdType.MESH


class Place:
    def __init__(self):
        e, s = lax.axis_index(EXPERT), lax.axis_index(SHARD)
        self.y, self.c = lax.div(e, 2), lax.rem(e, 2)
        self.z, self.x = lax.div(s, 2), lax.rem(s, 2)
        self.ox, self.oy, self.oc = 1 - self.x, 1 - self.y, 1 - self.c
        self.to_x = (e, s + 1 - 2 * self.x)
        self.to_y = (e + 2 - 4 * self.y, s)
        self.to_c = (e + 1 - 2 * self.c, s)
        z = self.z
        self.zs = (z, z + 1 - 2 * lax.rem(z, 2), lax.rem(z + 2, 4), 3 - z)
        self.to_z = [None] + [(e, self.zs[d] * 2 + self.x) for d in (1, 2, 3)]


class Sender:
    def __init__(self, send_sem, recv_sem):
        self.send_sem, self.recv_sem, self.started = send_sem, recv_sem, []

    def __call__(self, source, target, device):
        number = len(self.started)
        assert number < self.send_sem.shape[0]
        copy = pltpu.make_async_remote_copy(
            src_ref=source,
            dst_ref=target,
            send_sem=self.send_sem.at[number],
            recv_sem=self.recv_sem.at[number],
            device_id=device,
            device_id_type=MESH_IDS,
        )
        copy.start()
        self.started.append(copy)
        return copy

    def finish(self):
        for copy in self.started:
            copy.wait_send()


def greet(devices):
    barrier = pltpu.get_barrier_semaphore()
    for device in devices:
        pl.semaphore_signal(barrier, inc=1, device_id=device, device_id_type=MESH_IDS)
    pl.semaphore_wait(barrier, len(devices))


def gather_in_plane(place, send, groups, beside=lambda: None):
    x, y, c = place.x, place.y, place.c
    ox, oy, oc = place.ox, place.oy, place.oc
    first, landed, final = {}, {}, []

    def over_links(number):
        first[number] = []
        for view, source, ready, own in groups[number]:
            ready()
            block = source(y, None)
            by_x = send(block, view(x, y, c, None), place.to_x)
            by_y, back = None, None
            if own:
                back = send(source(oy, 1), view(x, oy, c, 1), place.to_x)
            else:
                by_y = send(block, view(x, y, c, None), place.to_y)
            first[number].append((by_x, by_y, back))

    def over_again(number):
        landed[number] = []
        for (view, source, ready, own), (by_x, by_y, back) in zip(groups[number], first[number]):
            if not own:
                final.append(send(source(y, None), view(x, y, c, None), place.to_c))
            by_x.wait_recv()
            over_y = send(view(ox, y, c, 0), view(ox, y, c, 0), place.to_y)
            final.append(send(view(ox, y, c, None), view(ox, y, c, None), place.to_c))
            if not own:
                by_y.wait_recv()
                back = send(view(x, oy, c, 1), view(x, oy, c, 1), place.to_x)
                final.append(send(view(x, oy, c, None), view(x, oy, c, None), place.to_c))
            landed[number].append((view, over_y, back))

    def over_core(number):
        for view, over_y, back in landed[number]:
            over_y.wait_recv()
            back.wait_recv()
            final.append(send(view(ox, oy, c, None), view(ox, oy, c, None), place.to_c))

    result = None
    for turn in range(len(groups) + 2):
        for delay, step in enumerate((over_links, over_again, over_core)):
            if 0 <= turn - delay < len(groups):
                step(turn - delay)
        if turn == min(1, len(groups) - 1):
            result = beside()
    for copy in final:
        copy.wait_recv()
    return result


def cut_rows(half, rows):
    more = rows * 2 // 3 // 16 * 16
    return pl.ds(0, rows) if half is None else pl.ds(more, rows - more) if half else pl.ds(0, more)


def half_rows(half, rows):
    return pl.ds(0, rows) if half is None else pl.ds(half * (rows // 2), rows // 2)


def halves_kernel(first, *refs):
    up_ref, down_ref, out, send_sem, recv_sem, copy_sem = refs
    place = Place()
    send = Sender(send_sem, recv_sem)
    greet([place.to_x])
    sent, local = start_halves(place, send, copy_sem, up_ref, down_ref, out, first)
    for copy in sent:
        copy.wait_recv()
    for copy in local:
        copy.wait()
    send.finish()


def start_halves(place, send, copy_sem, up_ref, down_ref, out_ref, first, base=0):
    x, ox = place.x, place.ox
    half = down_ref.shape[2] // 2
    sent, local = [], []
    for number in range(out_ref.shape[0]):
        out, expert = out_ref.at[number], first + number

        def pieces(xx):
            at = pl.ds(pl.multiple_of(xx * half, half), half)
            later = pl.ds(pl.multiple_of((xx + 2) * half, half), half)
            return (up_ref.at[expert, :, at], up_ref.at[expert, :, later], down_ref.at[expert, :, at])

        for index, piece in enumerate(pieces(ox)):
            sent.append(send(piece, out.at[x, :, index * half : (index + 1) * half], place.to_x))
        for index, piece in enumerate(pieces(x)):
            copy = pltpu.make_async_copy(
                piece, out.at[x, :, index * half : (index + 1) * half], copy_sem.at[base + 3 * number + index]
            )
            copy.start()
            local.append(copy)
    return sent, local


def exchange_halves(up, down, first, count):
    depth, inner = down.shape[1:]
    return pl.pallas_call(
        functools.partial(halves_kernel, first),
        out_shape=jax.ShapeDtypeStruct((count, 2, depth, 3 * inner // 2), up.dtype),
        in_specs=[pl.BlockSpec(memory_space=pltpu.VMEM)] * 2,
        out_specs=pl.BlockSpec(memory_space=pl.ANY),
        scratch_shapes=[pltpu.SemaphoreType.DMA((3 * count,))] * 3,
        compiler_params=pltpu.CompilerParams(collective_id=4 if first == 0 else 6, has_side_effects=True),
        cost_estimate=pl.CostEstimate(flops=0, bytes_accessed=40_000_000, transcendentals=0),
        name="exchange_halves",
    )(up, down)


def weights_kernel(
    first, up_ref, down_ref, w_ref, o_ref, small_ref, rows_ref, w_out, o_out, small_out, rows_out,
    *refs,
):
    halves_outs, (send_sem, recv_sem, copy_sem, half_sem) = refs[:-4], refs[-4:]
    place = Place()
    send = Sender(send_sem, recv_sem)
    x, y, c, z = place.x, place.y, place.c, place.z
    depth = w_ref.shape[0]
    piece = depth // 4
    blocks = rows_ref.shape[0]
    greet([place.to_x, place.to_y, place.to_c] + place.to_z[1:])

    def columns(ref, yy, cc):
        part = ref.shape[1] // 4
        return pl.ds(pl.multiple_of((yy * 2 + cc) * part, part), part)

    def pieces(yy, cc, half):
        start = (yy * 2 + cc) * piece
        if half is None:
            return pl.ds(pl.multiple_of(start, piece), piece)
        return pl.ds(pl.multiple_of(start + half * (piece // 2), piece // 2), piece // 2)

    wide = [(w_ref, w_out), (o_ref, o_out)]
    from_z = {}
    for d in (2, 1):
        from_z[d] = [
            send(ref.at[:, columns(ref, y, c)], out.at[z, x, :, columns(ref, y, c)], place.to_z[d])
            for ref, out in wide
        ] + [send(small_ref.at[pieces(y, c, None)], small_out.at[z, x, pieces(y, c, None)], place.to_z[d])]
    local = [
        pltpu.make_async_copy(w_ref, w_out.at[z, x], copy_sem.at[0]),
        pltpu.make_async_copy(o_ref, o_out.at[z, x], copy_sem.at[1]),
        pltpu.make_async_copy(small_ref, small_out.at[z, x], copy_sem.at[2]),
        pltpu.make_async_copy(rows_ref, rows_out.at[c, x, y], copy_sem.at[3]),
    ]
    for copy in local:
        copy.start()

    def wide_view(ref, out, zz):
        return lambda xx, yy, cc, half: out.at[zz, xx, cut_rows(half, depth), columns(ref, yy, cc)]

    def small_view(zz):
        return lambda xx, yy, cc, half: small_out.at[zz, xx, pieces(yy, cc, half)]

    def rows_view(xx, yy, cc, half):
        return rows_out.at[cc, xx, yy, cut_rows(half, blocks)]

    items = [
        (
            wide_view(ref, out, z),
            lambda yy, half, ref=ref: ref.at[cut_rows(half, depth), columns(ref, yy, c)],
            lambda: None,
            True,
        )
        for ref, out in wide
    ]
    items.append((small_view(z), lambda yy, half: small_ref.at[pieces(yy, c, half)], lambda: None, True))
    items.append((rows_view, lambda yy, half: rows_ref.at[cut_rows(half, blocks)], lambda: None, False))
    from_z[3] = []

    def arrive(d, number, view):
        from_z[d][number].wait_recv()
        if d == 2:
            block = view(x, y, c, None)
            from_z[3].append(send(block, block, place.to_z[1]))

    groups = [items]
    for d in (1, 2, 3):
        zz = place.zs[d]
        views = [wide_view(ref, out, zz) for ref, out in wide] + [small_view(zz)]
        groups.append(
            [
                (
                    view,
                    lambda yy, half, view=view: view(x, yy, c, half),
                    functools.partial(arrive, d, number, view),
                    False,
                )
                for number, view in enumerate(views)
            ]
        )

    def beside():
        sent, kept, expert = [], [], first
        for out in halves_outs:
            more_sent, more_kept = start_halves(
                place, send, half_sem, up_ref, down_ref, out, expert, 3 * (expert - first)
            )
            sent, kept, expert = sent + more_sent, kept + more_kept, expert + out.shape[0]
        return sent, kept

    sent, kept = gather_in_plane(place, send, groups, beside)
    for copy in sent:
        copy.wait_recv()
    for copy in local + kept:
        copy.wait()
    send.finish()


def gather_weights(w, o, small, rows, up, down, first, counts):
    depth, inner = down.shape[1:]
    count = sum(counts)
    copies = 128
    arrays = (w, o, small)
    return pl.pallas_call(
        functools.partial(weights_kernel, first),
        out_shape=tuple(jax.ShapeDtypeStruct((4, 2) + a.shape, a.dtype) for a in arrays)
        + (jax.ShapeDtypeStruct((2, 2, 2) + rows.shape, rows.dtype),)
        + tuple(jax.ShapeDtypeStruct((n, 2, depth, 3 * inner // 2), up.dtype) for n in counts),
        in_specs=[pl.BlockSpec(memory_space=pltpu.VMEM)] * 6,
        out_specs=(pl.BlockSpec(memory_space=pl.ANY),) * (4 + len(counts)),
        scratch_shapes=[
            pltpu.SemaphoreType.DMA((copies,)),
            pltpu.SemaphoreType.DMA((copies,)),
            pltpu.SemaphoreType.DMA((4,)),
            pltpu.SemaphoreType.DMA((3 * count,)),
        ],
        compiler_params=pltpu.CompilerParams(collective_id=0, has_side_effects=True),
        cost_estimate=pl.CostEstimate(flops=0, bytes_accessed=200_000_000, transcendentals=0),
        name="gather_weights",
    )(up, down, w, o, small, rows)


def rows_kernel(a_ref, b_ref, a_out, b_out, send_sem, recv_sem, copy_sem):
    place = Place()
    send = Sender(send_sem, recv_sem)
    x, y, c = place.x, place.y, place.c
    greet([place.to_x, place.to_y, place.to_c])
    local = [
        pltpu.make_async_copy(a_ref, a_out.at[c, x, y], copy_sem.at[0]),
        pltpu.make_async_copy(b_ref, b_out.at[c, x, y], copy_sem.at[1]),
    ]
    for copy in local:
        copy.start()

    def item(source, out):
        rows = source.shape[0]
        return (
            lambda xx, yy, cc, half: out.at[cc, xx, yy, half_rows(half, rows)],
            lambda yy, half: source.at[half_rows(half, rows)],
            lambda: None,
            False,
        )

    gather_in_plane(place, send, [[item(b_ref, b_out), item(a_ref, a_out)]])
    for copy in local:
        copy.wait()
    send.finish()


def gather_rows(a, b):
    return pl.pallas_call(
        rows_kernel,
        out_shape=(
            jax.ShapeDtypeStruct((2, 2, 2) + a.shape, a.dtype),
            jax.ShapeDtypeStruct((2, 2, 2) + b.shape, b.dtype),
        ),
        in_specs=[pl.BlockSpec(memory_space=pltpu.VMEM)] * 2,
        out_specs=(pl.BlockSpec(memory_space=pl.ANY),) * 2,
        scratch_shapes=[
            pltpu.SemaphoreType.DMA((16,)),
            pltpu.SemaphoreType.DMA((16,)),
            pltpu.SemaphoreType.DMA((2,)),
        ],
        compiler_params=pltpu.CompilerParams(collective_id=1, has_side_effects=True),
        cost_estimate=pl.CostEstimate(flops=0, bytes_accessed=90_000_000, transcendentals=0),
        name="gather_rows",
    )(a, b)


def add_into(target, left, right):
    lead = target.shape[:-2]
    rows = target.shape[-2]
    step = 16 if rows % 16 == 0 else 8
    count = rows // step

    def body(i, carry):
        at = pl.ds(pl.multiple_of(i * step, step), step)
        for index in itertools.product(*(range(n) for n in lead)):
            at_all = index + (at,)
            total = left[at_all].astype(jnp.float32) + right[at_all].astype(jnp.float32)
            target[at_all] = total.astype(target.dtype)
        return carry

    lax.fori_loop(0, count, body, 0)


def combine_kernel(experts, experts_all, first_ref, *refs):
    answer_refs, row_refs, dots_refs = (refs[i * experts : (i + 1) * experts] for i in range(3))
    table_ref, outs, refs = refs[3 * experts], refs[3 * experts + 1 : 3 * experts + 4], refs[3 * experts + 4 :]
    away, held, from_c, from_first, from_second = (refs[3 * i : 3 * i + 3] for i in range(5))
    answer_buf, row_buf, fetch_sem, send_sem, recv_sem = refs[15:]
    place = Place()
    send = Sender(send_sem, recv_sem)
    x, y, c = place.x, place.y, place.c
    ox, oy, oc = place.ox, place.oy, place.oc
    slot_rows = answer_refs[0].shape[1]
    seq_len, width = outs[1].shape
    dot_rows = outs[0].shape[0]
    first = first_ref[0]
    order = []
    for dx, dy in ((1, 1), (1, 0), (0, 1), (0, 0)):
        xx, yy = (ox if dx else x), (oy if dy else y)
        order += [(xx, yy, oc), (xx, yy, c)]

    def fetch(number):
        xx, yy, cc = order[number]
        seq = cc * 4 + xx * 2 + yy
        slot = number % 2
        copies = []
        for expert in range(experts):
            at = slice(expert * slot_rows, (expert + 1) * slot_rows)
            for which, (source, buf) in enumerate(((row_refs, row_buf), (answer_refs, answer_buf))):
                copies.append(
                    pltpu.make_async_copy(
                        source[expert].at[seq], buf.at[slot, at], fetch_sem.at[slot, 2 * expert + which]
                    )
                )
        for copy in copies:
            copy.start()
        return copies

    def compute(number, targets):
        xx, yy, cc = order[number]
        seq = cc * 4 + xx * 2 + yy
        slot = number % 2
        slot_ids = lax.broadcasted_iota(jnp.int32, (slot_rows, seq_len), 0).astype(jnp.float32)
        dot_ids = lax.broadcasted_iota(jnp.int32, (dot_rows, seq_len), 0)
        placings, combines = [], []
        dots = jnp.zeros((dot_rows, seq_len), jnp.float32)
        for expert in range(experts):
            placing = (slot_ids == table_ref[seq, pl.ds(experts_all + first + expert, 1), :]).astype(jnp.float32)
            placings.append(placing)
            combines.append(placing * table_ref[seq, pl.ds(first + expert, 1), :])
            dots = jnp.where(dot_ids == first + expert, dots_refs[expert][seq], dots)
        placing = jnp.concatenate(placings, axis=0).astype(jnp.bfloat16)
        combine = jnp.concatenate(combines, axis=0).astype(jnp.bfloat16)
        targets[0][...] = dots
        down = (((0,), (0,)), ((), ()))
        for left, buf, target in ((placing, row_buf, targets[1]), (combine, answer_buf, targets[2])):
            total = lax.dot_general(left, buf[slot], down, preferred_element_type=jnp.float32)
            target[...] = total.astype(target.dtype)

    heights = [out.shape[0] for out in outs]

    def half(part, xx, yy, which):
        return held[part].at[xx, yy, half_rows(which, heights[part])]

    fetched = {0: fetch(0)}
    greet([place.to_x, place.to_y, place.to_c])
    over = [[] for _ in outs]
    for step in range(4):
        for number in (2 * step, 2 * step + 1):
            xx, yy, cc = order[number]
            if number + 1 < len(order):
                fetched[number + 1] = fetch(number + 1)
            for copy in fetched.pop(number):
                copy.wait()
            if number % 2 == 0:
                compute(number, [ref.at[xx, yy] for ref in away])
                crossed = [
                    send(away[part].at[xx, yy], from_c[part].at[xx, yy], place.to_c) for part in range(3)
                ]
            else:
                compute(number, [ref.at[xx, yy] for ref in held])
        for part in range(3):
            crossed[part].wait_recv()
            add_into(held[part].at[xx, yy], held[part].at[xx, yy], from_c[part].at[xx, yy])
            first_got = from_first[part]
            if step == 0:
                over[part].append(send(half(part, xx, yy, 0), first_got.at[0, 1], place.to_y))
                over[part].append(send(half(part, xx, yy, 1), first_got.at[1, 1], place.to_x))
            elif step == 1:
                over[part].append(send(half(part, xx, yy, 1), first_got.at[1, 0], place.to_x))
            elif step == 2:
                over[part].append(send(half(part, xx, yy, 0), first_got.at[0, 0], place.to_y))
    second = []
    for part in range(3):
        a0, b0, b1, a1 = over[part]
        a0.wait_recv()
        add_into(half(part, ox, y, 0), half(part, ox, y, 0), from_first[part].at[0, 1])
        a2 = send(half(part, ox, y, 0), from_second[part].at[0], place.to_x)
        b0.wait_recv()
        add_into(half(part, x, oy, 1), half(part, x, oy, 1), from_first[part].at[1, 1])
        b2 = send(half(part, x, oy, 1), from_second[part].at[1], place.to_y)
        second.append((a2, b2))
    for part in range(3):
        a0, b0, b1, a1 = over[part]
        a1.wait_recv()
        add_into(half(part, x, y, 0), half(part, x, y, 0), from_first[part].at[0, 0])
        b1.wait_recv()
        add_into(half(part, x, y, 1), half(part, x, y, 1), from_first[part].at[1, 0])
    for part, (a2, b2) in enumerate(second):
        for which, copy in enumerate((a2, b2)):
            copy.wait_recv()
            at = half_rows(which, heights[part])
            add_into(outs[part].at[at], half(part, x, y, which), from_second[part].at[which])
    send.finish()


def combine_rows(first_own, answers, row_grads, dots, table, experts_all):
    experts = len(answers)
    seq_len = table.shape[2]
    _, slot_rows, width = answers[0].shape
    kinds = [
        ((-(-experts_all // 32) * 32, seq_len), jnp.float32),
        ((seq_len, width), jnp.bfloat16),
        ((seq_len, width), jnp.bfloat16),
    ]

    def scratch(lead, cut=1):
        return [pltpu.VMEM(lead + (shape[0] // cut, shape[1]), kind) for shape, kind in kinds]

    return pl.pallas_call(
        functools.partial(combine_kernel, experts, experts_all),
        out_shape=tuple(jax.ShapeDtypeStruct(shape, jnp.float32) for shape, _ in kinds),
        in_specs=[pl.BlockSpec(memory_space=pltpu.SMEM)]
        + [pl.BlockSpec(memory_space=pl.ANY)] * (2 * experts)
        + [pl.BlockSpec(memory_space=pltpu.VMEM)] * (experts + 1),
        out_specs=(pl.BlockSpec(memory_space=pltpu.VMEM),) * 3,
        scratch_shapes=scratch((2, 2))
        + scratch((2, 2))
        + scratch((2, 2))
        + scratch((2, 2), 2)
        + scratch((2,), 2)
        + [pltpu.VMEM((2, experts * slot_rows, width), jnp.bfloat16)] * 2
        + [
            pltpu.SemaphoreType.DMA((2, 2 * experts)),
            pltpu.SemaphoreType.DMA((32,)),
            pltpu.SemaphoreType.DMA((32,)),
        ],
        compiler_params=pltpu.CompilerParams(
            collective_id=2, has_side_effects=True, vmem_limit_bytes=60 * 2**20
        ),
        cost_estimate=pl.CostEstimate(
            flops=32 * seq_len * width * experts * slot_rows, bytes_accessed=150_000_000, transcendentals=0
        ),
        name="combine_rows",
    )(first_own, *answers, *row_grads, *dots, table)


def grads_kernel(count, cuts, spans, *refs):
    total_refs, refs = refs[:count], refs[count:]
    ins, refs = refs[:3], refs[3:]
    outs, refs = refs[: len(spans)], refs[len(spans) :]
    got_refs, refs = refs[:count], refs[count:]
    many = len(cuts)
    held, from_c, from_first, from_second, own, from_z, alls = (refs[many * i : many * (i + 1)] for i in range(7))
    send_sem, recv_sem = refs[7 * many :]
    place = Place()
    send = Sender(send_sem, recv_sem)
    x, y, c, z = place.x, place.y, place.c, place.z
    ox, oy, oc = place.ox, place.oy, place.oc
    greet([place.to_x, place.to_y, place.to_c] + place.to_z[1:])
    depth = ins[1].shape[2]
    piece = depth // 4
    order = [(ox, oy), (ox, y), (x, oy), (x, y)]

    def take(part, xx, yy, cc):
        number, start, wide = cuts[part]
        ref, quarter = ins[number], yy * 2 + cc
        if number == 0:
            return ref.at[:, xx, pl.ds(pl.multiple_of(quarter * piece, piece), piece)]
        at = pl.multiple_of(quarter * (ref.shape[3] // 4) + start, 128)
        return ref.at[:, xx, :, pl.ds(at, wide)]

    def half(part, xx, yy, which):
        return held[part].at[xx, yy, :, half_rows(which, own[part].shape[1])]

    crossed = [
        [send(take(part, xx, yy, oc), from_c[part].at[xx, yy], place.to_c) for xx, yy in order]
        for part in range(many)
    ]
    over, second, arriving, spread, last = {}, {}, {}, {}, {}

    def over_links(part):
        for step, (xx, yy) in enumerate(order):
            crossed[part][step].wait_recv()
            add_into(held[part].at[xx, yy], take(part, xx, yy, c), from_c[part].at[xx, yy])
            got = from_first[part]
            if step == 0:
                a0 = send(half(part, xx, yy, 0), got.at[0, 1], place.to_y)
                b0 = send(half(part, xx, yy, 1), got.at[1, 1], place.to_x)
            elif step == 1:
                b1 = send(half(part, xx, yy, 1), got.at[1, 0], place.to_x)
            elif step == 2:
                a1 = send(half(part, xx, yy, 0), got.at[0, 0], place.to_y)
        over[part] = (a0, b0, a1, b1)

    def over_again(part):
        a0, b0, a1, b1 = over[part]
        got = from_first[part]
        a0.wait_recv()
        add_into(half(part, ox, y, 0), half(part, ox, y, 0), got.at[0, 1])
        a2 = send(half(part, ox, y, 0), from_second[part].at[0], place.to_x)
        b0.wait_recv()
        add_into(half(part, x, oy, 1), half(part, x, oy, 1), got.at[1, 1])
        b2 = send(half(part, x, oy, 1), from_second[part].at[1], place.to_y)
        a1.wait_recv()
        add_into(half(part, x, y, 0), half(part, x, y, 0), got.at[0, 0])
        b1.wait_recv()
        add_into(half(part, x, y, 1), half(part, x, y, 1), got.at[1, 0])
        second[part] = (a2, b2)

    def over_z(part):
        for which, copy in enumerate(second[part]):
            copy.wait_recv()
            at = half_rows(which, own[part].shape[1])
            add_into(own[part].at[:, at], half(part, x, y, which), from_second[part].at[which])
        arriving[part] = [
            send(own[part].at[place.zs[d]], from_z[part].at[slot], place.to_z[1]) for slot, d in ((1, 3), (0, 1))
        ]

    def over_z_again(part):
        arrived = from_z[part]
        for copy in arriving[part]:
            copy.wait_recv()
        add_into(arrived.at[1], arrived.at[1], own[part].at[place.zs[2]])
        arriving[part] = send(arrived.at[1], arrived.at[2], place.to_z[2])
        add_into(arrived.at[0], arrived.at[0], own[part].at[z])

    def back_over_y(part):
        mine, arrived = alls[part].at[y, c], from_z[part]
        arriving[part].wait_recv()
        add_into(mine, arrived.at[0], arrived.at[2])
        over_y = send(mine, mine, place.to_y)
        spread[part] = (over_y, send(mine, mine, place.to_c))

    def back_over_c(part):
        over_y, over_c = spread[part]
        over_y.wait_recv()
        other = alls[part].at[oy, c]
        last[part] = (over_c, send(other, other, place.to_c))

    def lay_out(part):
        for copy in last[part]:
            copy.wait_recv()
        number, start, wide = cuts[part]
        for yy, cc in itertools.product((0, 1), (0, 1)):
            if number == 0:
                at = (yy * 2 + cc) * piece
                outs[0][at : at + piece, :] = alls[part][yy, cc]
                continue
            at = (yy * 2 + cc) * (ins[number].shape[3] // 4) + start
            for out, (owner, low, high) in zip(outs, spans):
                left, right = max(low, at), min(high, at + wide)
                if owner != number or left >= right:
                    continue

                def body(i, carry, out=out, low=low, left=left, right=right, at=at, yy=yy, cc=cc):
                    rows = pl.ds(pl.multiple_of(i * 16, 16), 16)
                    block = alls[part][yy, cc, rows, left - at : right - at]
                    out[rows, left - low : right - low] = block.astype(jnp.float32)
                    return carry

                lax.fori_loop(0, depth // 16, body, 0)

    steps = [(over_links, 0), (over_again, 1), (over_z, 2), (over_z_again, 4)]
    steps += [(back_over_y, 5), (back_over_c, 6), (lay_out, 7)]
    swapped = []
    for turn in range(many + 7):
        for step, delay in steps:
            if 0 <= turn - delay < many:
                step(turn - delay)
        if turn == many:
            swapped = [send(total.at[:, ox], got, place.to_x) for total, got in zip(total_refs, got_refs)]
    for copy in swapped:
        copy.wait_recv()
    send.finish()


def sum_grads(small, output, mixer, totals, q_width):
    depth = output.shape[2]
    arrays = (small, output, mixer)
    wide = mixer.shape[3] // 4
    split = wide * 3 // 5 // 128 * 128
    cuts = [(0, 0, small.shape[3]), (1, 0, output.shape[3] // 4), (2, 0, split), (2, split, wide - split)]
    shapes = [((depth // 4 if number == 0 else depth, width), arrays[number].dtype) for number, _, width in cuts]
    count = len(totals)
    last = (q_width + mixer.shape[3]) // 2
    spans = [(0, 0, small.shape[3]), (1, 0, output.shape[3])]
    spans += [(2, 0, q_width), (2, q_width, last), (2, last, mixer.shape[3])]

    def scratch(lead, cut=1):
        return [pltpu.VMEM(lead + (height // cut, wide), kind) for (height, wide), kind in shapes]

    return pl.pallas_call(
        functools.partial(grads_kernel, count, cuts, spans),
        out_shape=tuple(jax.ShapeDtypeStruct((depth, high - low), jnp.float32) for _, low, high in spans)
        + tuple(jax.ShapeDtypeStruct(t.shape[:1] + t.shape[2:], t.dtype) for t in totals),
        in_specs=[pl.BlockSpec(memory_space=pl.ANY)] * count + [pl.BlockSpec(memory_space=pltpu.VMEM)] * 3,
        out_specs=(pl.BlockSpec(memory_space=pltpu.VMEM),) * len(spans)
        + (pl.BlockSpec(memory_space=pl.ANY),) * count,
        scratch_shapes=scratch((2, 2, 4))
        + scratch((2, 2, 4))
        + scratch((2, 2, 4), 2)
        + scratch((2, 4), 2)
        + scratch((4,))
        + scratch((3,))
        + scratch((2, 2))
        + [pltpu.SemaphoreType.DMA((72,)), pltpu.SemaphoreType.DMA((72,))],
        compiler_params=pltpu.CompilerParams(
            collective_id=3, has_side_effects=True, vmem_limit_bytes=60 * 2**20
        ),
        cost_estimate=pl.CostEstimate(flops=0, bytes_accessed=300_000_000, transcendentals=0),
        name="sum_grads",
    )(*totals, *arrays)


def swap_kernel(count, *refs):
    total_refs, got_refs, (send_sem, recv_sem) = refs[:count], refs[count : 2 * count], refs[2 * count :]
    place = Place()
    send = Sender(send_sem, recv_sem)
    greet([place.to_x])
    for total, got in zip(total_refs, got_refs):
        send(total.at[:, place.ox], got, place.to_x)
    for copy in send.started:
        copy.wait_recv()
    send.finish()


def swap_totals(totals, collective):
    count = len(totals)
    return pl.pallas_call(
        functools.partial(swap_kernel, count),
        out_shape=tuple(jax.ShapeDtypeStruct(t.shape[:1] + t.shape[2:], t.dtype) for t in totals),
        in_specs=[pl.BlockSpec(memory_space=pl.ANY)] * count,
        out_specs=(pl.BlockSpec(memory_space=pl.ANY),) * count,
        scratch_shapes=[pltpu.SemaphoreType.DMA((count,))] * 2,
        compiler_params=pltpu.CompilerParams(collective_id=collective, has_side_effects=True),
        cost_estimate=pl.CostEstimate(flops=0, bytes_accessed=40_000_000, transcendentals=0),
        name="swap_totals",
    )(*totals)


def place_kernel(groups, side_ref, *refs):
    kept_refs, got_refs = refs[:groups], refs[groups : 2 * groups]
    up_out, down_out = refs[2 * groups :]
    half = down_out.shape[2] // 2
    first = side_ref[0] == 0
    experts = [(g, k) for g in range(groups) for k in range(kept_refs[g].shape[0])]
    for expert, (g, k) in enumerate(experts):
        kept = kept_refs[g][k, 0].astype(jnp.float32)
        got = got_refs[g][k].astype(jnp.float32)
        low, high = jnp.where(first, kept, got), jnp.where(first, got, kept)
        for index, part in enumerate((low, high)):
            for group in (0, 1):
                at = (2 * group + index) * half
                up_out[expert, :, at : at + half] = part[:, group * half : (group + 1) * half]
            down_out[expert, :, index * half : (index + 1) * half] = part[:, 2 * half :]


def place_sums(side, totals, got):
    count = sum(g.shape[0] for g in got)
    _, depth, width = got[0].shape
    step = depth // 4
    half = width // 3
    return pl.pallas_call(
        functools.partial(place_kernel, len(got)),
        out_shape=(
            jax.ShapeDtypeStruct((count, depth, 4 * half), jnp.float32),
            jax.ShapeDtypeStruct((count, depth, 2 * half), jnp.float32),
        ),
        grid_spec=pltpu.PrefetchScalarGridSpec(
            num_scalar_prefetch=1,
            grid=(4,),
            in_specs=[
                pl.BlockSpec((t.shape[0], 1, step, width), lambda i, side: (0, side[0], i, 0)) for t in totals
            ]
            + [pl.BlockSpec((g.shape[0], step, width), lambda i, side: (0, i, 0)) for g in got],
            out_specs=(
                pl.BlockSpec((count, step, 4 * half), lambda i, side: (0, i, 0)),
                pl.BlockSpec((count, step, 2 * half), lambda i, side: (0, i, 0)),
            ),
        ),
        cost_estimate=pl.CostEstimate(flops=0, bytes_accessed=9_000_000, transcendentals=0),
        name="place_sums",
    )(side, *totals, *got)


def expert_kernel(
    expert, experts_all, first_ref, table_ref, rows_ref, dout_ref, w_ref, *refs
):
    answer_ref, row_ref, w_out, dots_ref, total, picked, picked_dout = refs[-7:]
    group, slot_rows, width = answer_ref.shape
    half = w_ref.shape[3] // 3

    def weight(columns):
        return w_ref[:, 0, :, columns].reshape(width, -1)

    both_columns, down_columns = slice(0, 2 * half), slice(2 * half, 3 * half)
    seq_len = rows_ref.shape[1]
    step = pl.program_id(0)
    slot_ids = lax.broadcasted_iota(jnp.int32, (slot_rows, seq_len), 0).astype(jnp.float32)
    gate_parts = []

    def own_row(q, at):
        return table_ref[q, pl.ds(at + first_ref[0] + expert, 1), :]

    for q in range(group):
        placing = (slot_ids == own_row(q, experts_all)).astype(jnp.float32)
        gate_parts.append(jnp.sum(placing * own_row(q, 0), axis=1, keepdims=True))
        low = placing.astype(jnp.bfloat16)
        at = slice(q * slot_rows, (q + 1) * slot_rows)
        picked[at, :] = jnp.dot(low, rows_ref[q], preferred_element_type=jnp.float32).astype(jnp.bfloat16)
        picked_dout[at, :] = jnp.dot(low, dout_ref[q], preferred_element_type=jnp.float32).astype(jnp.bfloat16)
    gate = jnp.concatenate(gate_parts, axis=0)
    both = jnp.dot(picked[...], weight(both_columns), preferred_element_type=jnp.float32)
    gate_part, up_part = both[:, :half], both[:, half:]
    sigmoid = 1.0 / (1.0 + jnp.exp(-gate_part))
    silu = gate_part * sigmoid
    active = (silu * up_part).astype(jnp.bfloat16)
    across = (((1,), (1,)), ((), ()))
    down = (((0,), (0,)), ((), ()))
    answer = lax.dot_general(active, weight(down_columns), across, preferred_element_type=jnp.float32)
    answer = answer.astype(jnp.bfloat16)
    dots = jnp.sum(picked_dout[...].astype(jnp.float32) * answer.astype(jnp.float32), axis=1, keepdims=True)
    for q in range(group):
        at = slice(q * slot_rows, (q + 1) * slot_rows)
        answer_ref[q] = answer[at, :]
        placing = (slot_ids == own_row(q, experts_all)).astype(jnp.float32)
        dots_ref[q] = jnp.sum(placing * dots[at, :], axis=0, keepdims=True)
    picked_dout[...] = (picked_dout[...].astype(jnp.float32) * gate).astype(jnp.bfloat16)
    active_grad = jnp.dot(picked_dout[...], weight(down_columns), preferred_element_type=jnp.float32)
    both_grad = jnp.concatenate(
        [
            active_grad * up_part * sigmoid * (1.0 + gate_part * (1.0 - sigmoid)),
            active_grad * silu,
        ],
        axis=1,
    ).astype(jnp.bfloat16)
    row = lax.dot_general(both_grad, weight(both_columns), across, preferred_element_type=jnp.float32)
    row = row.astype(jnp.bfloat16)
    for q in range(group):
        row_ref[q] = row[q * slot_rows : (q + 1) * slot_rows, :]
    up_term = lax.dot_general(picked[...], both_grad, down, preferred_element_type=jnp.float32)
    down_term = lax.dot_general(picked_dout[...], active, down, preferred_element_type=jnp.float32)

    @pl.when(step == 0)
    def _():
        total[:, : 2 * half] = up_term
        total[:, 2 * half :] = down_term

    @pl.when(step > 0)
    def _():
        total[:, : 2 * half] += up_term
        total[:, 2 * half :] += down_term

    @pl.when(step == pl.num_programs(0) - 1)
    def _():
        w_out[...] = total[...].astype(w_out.dtype).reshape(w_out.shape)


def run_expert(first_own, table, rows, dout, weights, expert, experts_all, slot_rows, sums, number, sum_count):
    count, seq_len, width = rows.shape
    group = count // 2
    weights, at = weights
    parts, _, deep, wide = weights.shape
    one = pl.BlockSpec((group, 1, seq_len), lambda i: (i, 0, 0))
    listed = pl.BlockSpec((group,) + table.shape[1:], lambda i: (i, 0, 0))
    tall = pl.BlockSpec((group, seq_len, width), lambda i: (i, 0, 0))
    slot = pl.BlockSpec((group, slot_rows, width), lambda i: (i, 0, 0))
    taken = pl.BlockSpec((parts, 1, deep, wide), lambda i: (0, at, 0, 0))
    given = pl.BlockSpec((parts, 1, deep, wide), lambda i: (0, number, 0, 0))
    flops = 2 * count * slot_rows * width * (2 * seq_len + 3 * wide)
    held = [] if sums is None else [sums]
    return pl.pallas_call(
        functools.partial(expert_kernel, expert, experts_all),
        grid=(2,),
        out_shape=(
            jax.ShapeDtypeStruct((count, slot_rows, width), jnp.bfloat16),
            jax.ShapeDtypeStruct((count, slot_rows, width), jnp.bfloat16),
            jax.ShapeDtypeStruct((parts, sum_count, deep, wide), jnp.bfloat16),
            jax.ShapeDtypeStruct((count, 1, seq_len), jnp.float32),
        ),
        in_specs=[pl.BlockSpec(memory_space=pltpu.SMEM), listed, tall, tall, taken]
        + [pl.BlockSpec(memory_space=pl.ANY)] * len(held),
        out_specs=(slot, slot, given, one),
        scratch_shapes=[
            pltpu.VMEM((parts * deep, wide), jnp.float32),
            pltpu.VMEM((group * slot_rows, width), jnp.bfloat16),
            pltpu.VMEM((group * slot_rows, width), jnp.bfloat16),
        ],
        input_output_aliases={5: 2} if held else {},
        compiler_params=pltpu.CompilerParams(vmem_limit_bytes=60 * 2**20),
        cost_estimate=pl.CostEstimate(flops=flops, bytes_accessed=25_000_000, transcendentals=0),
        name="run_expert",
    )(first_own, table, rows, dout, weights, *held)


def layer_on_device(
    tokens,
    lengths,
    routes,
    cotangent,
    first_gain,
    query_weight,
    key_matrix,
    value_matrix,
    output_weight,
    second_gain,
    router_weight,
    gate_up_weight,
    down_weight,
):
    seq_len, model_width = tokens.shape
    q_heads = query_weight.shape[1] // HEAD_DIM
    kv_heads = key_matrix.shape[1] // HEAD_DIM
    group_size = q_heads // kv_heads
    experts_all = router_weight.shape[1]
    local_experts = gate_up_weight.shape[1]
    inner_width = down_weight.shape[2]
    half_inner = inner_width // 2
    q_width, kv_width = query_weight.shape[1], key_matrix.shape[1]
    slot_count = 8 * max(
        seq_len // 32, (seq_len * routes.shape[1] + 8 * experts_all - 1) // (8 * experts_all)
    )
    score_factor = HEAD_DIM ** (-0.5)
    along_z = [[z * 2 + x for z in range(4)] for x in range(2)]
    expert_at, shard_at = lax.axis_index(EXPERT), lax.axis_index(SHARD)
    x_at = lax.rem(shard_at, 2)
    depth = first_gain.shape[0]

    early = 4
    up_first = gate_up_weight.transpose(1, 0, 2)
    down_first = down_weight.transpose(1, 0, 2)

    def along(halves):
        block = halves.reshape(1, halves.shape[0], 2 * depth, 3 * half_inner)
        return lax.all_gather(block, SHARD, axis=0, tiled=True, axis_index_groups=along_z)

    halves = exchange_halves(up_first, down_first, 0, 1)
    expert_weights = [(along(halves), 0)]
    up_first, down_first, _ = lax.optimization_barrier((up_first, down_first, halves))
    halves = exchange_halves(up_first, down_first, 1, early - 1)
    gathered = along(halves)
    expert_weights += [(gathered, number) for number in range(early - 1)]

    position = jnp.arange(seq_len, dtype=jnp.int32)
    length = lengths[0]
    valid_rows = (position < length).astype(jnp.float32)
    dout_full = cotangent.astype(jnp.float32) * valid_rows[:, None]
    dout_low = dout_full.astype(jnp.bfloat16)
    mixer_block = jnp.concatenate([query_weight, key_matrix, value_matrix], axis=1)
    small_block = jnp.concatenate(
        [
            router_weight.astype(jnp.float32),
            first_gain.astype(jnp.float32)[:, None],
            second_gain.astype(jnp.float32)[:, None],
            jnp.zeros((depth, 128 - experts_all - 2), jnp.float32),
        ],
        axis=1,
    )
    mixer_block, output_block, small_block, dout_low = lax.optimization_barrier(
        (mixer_block, output_weight, small_block, dout_low, halves)
    )[:4]
    mixer_full, output_full, small_full, dout_plane, *halves = gather_weights(
        mixer_block, output_block, small_block, dout_low, up_first, down_first, early, (local_experts - early,)
    )
    for some in halves:
        gathered = along(some)
        expert_weights += [(gathered, number) for number in range(some.shape[0])]
    mixer_full = mixer_full.reshape(model_width, mixer_block.shape[1])
    output_full = output_full.reshape(model_width, output_weight.shape[1])
    small_full = small_full.reshape(model_width, 128)
    dout_plane = dout_plane.reshape(8, seq_len, model_width)
    router_full = small_full[:, :experts_all].astype(jnp.bfloat16)
    gain_one, gain_two = small_full[:, experts_all], small_full[:, experts_all + 1]

    cosine, sine_table = rope_tables(seq_len, HEAD_DIM)
    source = tokens.astype(jnp.float32)
    first_scale = lax.rsqrt(jnp.mean(source * source, axis=-1, keepdims=True) + norm_eps)
    first_norm_output = (source * first_scale * gain_one).astype(jnp.bfloat16)
    mixed_in = product("za,ao->zo", first_norm_output, mixer_full)
    queries = rotate(mixed_in[:, :q_width].reshape(seq_len, q_heads, HEAD_DIM), cosine, sine_table)
    queries = queries.astype(jnp.bfloat16).reshape(seq_len, kv_heads, group_size, HEAD_DIM)
    key_row_block = rotate(
        mixed_in[:, q_width : q_width + kv_width].reshape(seq_len, kv_heads, HEAD_DIM), cosine, sine_table
    ).astype(jnp.bfloat16)
    value_row_block = (
        mixed_in[:, q_width + kv_width :].astype(jnp.bfloat16).reshape(seq_len, kv_heads, HEAD_DIM)
    )
    allowed = (position[None, :] <= position[:, None]) & (position[None, :] < length)
    scores = jnp.where(
        allowed, product("qhgd,khd->hgqk", queries, key_row_block) * score_factor, -1e30
    )
    row_max = jnp.max(scores, axis=-1, keepdims=True)
    shifted = jnp.exp(scores - row_max)
    row_total = jnp.sum(shifted, axis=-1, keepdims=True)
    log_total = row_max + jnp.log(row_total)
    probs_low = (shifted / row_total).astype(jnp.bfloat16)
    mixed_heads = (
        product("hgqk,khd->qhgd", probs_low, value_row_block)
        .reshape(seq_len, q_heads * HEAD_DIM)
        .astype(jnp.bfloat16)
    )
    hidden = source + product("sf,df->sd", mixed_heads, output_full)
    second_scale = lax.rsqrt(jnp.mean(hidden * hidden, axis=-1, keepdims=True) + norm_eps)
    second_normed = (hidden * second_scale * gain_two).astype(jnp.bfloat16)
    logits = product("sd,de->se", second_normed, router_full)
    chosen = (routes[:, :, None] == jnp.arange(experts_all, dtype=jnp.int32)).astype(jnp.float32)
    picked = jnp.sum(chosen * logits[:, None, :], axis=-1)
    gate_soft = jax.nn.softmax(picked, axis=-1)
    routed = jnp.sum(chosen, axis=1) * valid_rows[:, None]
    earlier = (position[None, :] < position[:, None]).astype(jnp.bfloat16)
    rank_rows = product("st,te->se", earlier, routed.astype(jnp.bfloat16))
    slot_of = jnp.where(routed > 0, rank_rows, -1.0)
    gate_low = gate_soft.astype(jnp.bfloat16).astype(jnp.float32)
    gate_full = jnp.sum(chosen * gate_low[:, :, None], axis=1)
    listed = -(-2 * experts_all // 16) * 16
    table = jnp.concatenate(
        [gate_full, slot_of, jnp.zeros((seq_len, listed - 2 * experts_all), jnp.float32)], axis=1
    ).T
    rows_plane, table_plane = gather_rows(second_normed, table)
    rows_plane = rows_plane.reshape(8, seq_len, model_width)
    table_plane = table_plane.reshape(8, listed, seq_len)
    first_own = (expert_at * local_experts).astype(jnp.int32).reshape(1)
    slot_rows = -(-slot_count // 16) * 16
    turn, results, sums = first_own, [], []
    for first, count in ((0, 3), (3, local_experts - 3)):
        held = None
        for number in range(count):
            e = first + number
            answer, row_grad, held, dot = run_expert(
                turn, table_plane, rows_plane, dout_plane, expert_weights[e], e, experts_all, slot_rows,
                held, number, count,
            )
            results.append((answer, row_grad, dot))
            turn = lax.optimization_barrier((first_own, dot))[0]
        sums.append(held)
    answers, row_grads, dots = zip(*results)
    dot_rows, grad_rows, value_rows = combine_rows(
        first_own, answers, row_grads, dots, table_plane, experts_all
    )
    dot_rows = dot_rows.T
    output = (hidden + value_rows).astype(jnp.bfloat16)
    gate_grad = jnp.sum(chosen * dot_rows[:, None, :experts_all], axis=-1)
    inner_sum = jnp.sum(gate_soft * gate_grad, axis=-1, keepdims=True)
    picked_grad = gate_soft * (gate_grad - inner_sum)
    logits_grad = jnp.sum(chosen * picked_grad[:, :, None], axis=1).astype(jnp.bfloat16)
    router_term = product("sd,se->de", second_normed, logits_grad)

    totals = [
        lax.psum_scatter(
            held, SHARD, scatter_dimension=0, tiled=True, axis_index_groups=along_z
        ).reshape(held.shape[1], 2, depth, 3 * half_inner)
        for held in sums
    ]

    normed_grad = grad_rows + product("se,de->sd", logits_grad, router_full)
    hidden_grad, second_gain_term = norm_back(normed_grad, hidden, second_scale, gain_two)
    hidden_grad = hidden_grad + dout_full
    attn_grad = hidden_grad.astype(jnp.bfloat16)
    output_term = product("sd,sf->df", attn_grad, mixed_heads)
    mixed_grad = (
        product("za,ao->zo", attn_grad, output_full)
        .astype(jnp.bfloat16)
        .reshape(seq_len, kv_heads, group_size, HEAD_DIM)
    )
    scores_again = jnp.where(
        allowed, product("qhgd,khd->hgqk", queries, key_row_block) * score_factor, -1e30
    )
    probs_again = jnp.exp(scores_again - log_total)
    probs_grad = product("qhgd,khd->hgqk", mixed_grad, value_row_block)
    row_inner = jnp.sum(probs_again * probs_grad, axis=-1, keepdims=True)
    scores_grad = (probs_again * (probs_grad - row_inner)).astype(jnp.bfloat16)
    query_back = product("hgqk,khd->qhgd", scores_grad, key_row_block) * score_factor
    key_back = product("hgqk,qhgd->khd", scores_grad, queries) * score_factor
    value_back = product("hgqk,qhgd->khd", probs_again.astype(jnp.bfloat16), mixed_grad)
    query_pre = (
        unrotate(query_back.reshape(seq_len, q_heads, HEAD_DIM), cosine, sine_table)
        .astype(jnp.bfloat16)
        .reshape(seq_len, q_heads * HEAD_DIM)
    )
    key_pre = (
        unrotate(key_back, cosine, sine_table)
        .astype(jnp.bfloat16)
        .reshape(seq_len, kv_heads * HEAD_DIM)
    )
    value_pre = value_back.astype(jnp.bfloat16).reshape(seq_len, kv_heads * HEAD_DIM)
    mixed_pre = jnp.concatenate([query_pre, key_pre, value_pre], axis=1)
    mixer_term = product("sd,sf->df", first_norm_output, mixed_pre).astype(jnp.bfloat16)
    normed1_grad = product("sf,df->sd", mixed_pre, mixer_full)
    tokens_grad, first_gain_term = norm_back(normed1_grad, source, first_scale, gain_one)
    tokens_grad = tokens_grad + hidden_grad
    small_terms = jnp.concatenate(
        [
            router_term,
            first_gain_term[:, None],
            second_gain_term[:, None],
            jnp.zeros((model_width, 128 - experts_all - 2), jnp.float32),
        ],
        axis=1,
    ).reshape(4, 2, depth, 128)
    small_sum, output_sum, query_sum, key_sum, value_sum, *got = sum_grads(
        small_terms,
        output_term.astype(jnp.bfloat16).reshape(4, 2, depth, output_weight.shape[1]),
        mixer_term.reshape(4, 2, depth, mixer_block.shape[1]),
        totals[:1],
        q_width,
    )
    late = lax.optimization_barrier((small_sum, totals[-1]))[1:]
    got += swap_totals(late, 5)
    both_sums, down_sums = place_sums(x_at.reshape(1), totals, got)
    return (
        output,
        tokens_grad,
        small_sum[:, experts_all],
        query_sum,
        key_sum,
        value_sum,
        output_sum,
        small_sum[:, experts_all + 1],
        small_sum[:, :experts_all],
        both_sums.transpose(1, 0, 2),
        down_sums.transpose(1, 0, 2),
    )


def solution(mesh):
    small_slice = mesh.shape[EXPERT] == 4 and mesh.shape[SHARD] == 8
    placed = (
        P((EXPERT, SHARD), None),
        P((EXPERT, SHARD)),
        P((EXPERT, SHARD), None),
        P((EXPERT, SHARD), None),
        P(SHARD),
        P(SHARD, None),
        P(SHARD, None),
        P(SHARD, None),
        P(SHARD, None),
        P(SHARD),
        P(SHARD, None),
        P(SHARD, EXPERT, None),
        P(SHARD, EXPERT, None),
    )
    return jax.shard_map(
        layer_on_device if small_slice else on_device,
        mesh=mesh,
        in_specs=placed,
        out_specs=(
            P((EXPERT, SHARD), None),
            P((EXPERT, SHARD), None),
            P(SHARD),
            P(SHARD, None),
            P(SHARD, None),
            P(SHARD, None),
            P(SHARD, None),
            P(SHARD),
            P(SHARD, None),
            P(SHARD, EXPERT, None),
            P(SHARD, EXPERT, None),
        ),
        check_vma=False,
    )
```
